128 devices in a mesh: sect: 2 (over core), exp: 16 (over y, x), tp: 4 (over z).
Axes of the slice: x: 4, y: 4, z: 4, core: 2. Of those that a mesh axis runs over, the one named last changes fastest.
Arguments:
- tokens: bfloat16 [1024, 6144], P(('sect', 'exp', 'tp')), may hold values from -6 to 6
- router_logits: float32 [1024, 2], P(('sect', 'exp', 'tp')), may hold values from -6 to 6
- expert_ids: int32 [1024, 2], P(('sect', 'exp', 'tp')), may hold values from 0 to 7, all different within a row; in each aligned block of 8 rows (0 to 7, 8 to 15, ...) at most 4 rows name the same one
- w_gate: bfloat16 [32, 6144, 2048], P(('sect', 'exp'), None, 'tp'), may hold values from -0.078125 to 0.078125
- w_up: bfloat16 [32, 6144, 2048], P(('sect', 'exp'), None, 'tp'), may hold values from -0.078125 to 0.078125
- w_down: bfloat16 [32, 2048, 6144], P(('sect', 'exp'), 'tp'), may hold values from -0.0625 to 0.0625
Outputs:
- mixture: bfloat16 [1024, 6144], P(('sect', 'exp', 'tp'))
The draws below stay inside these ranges and needn't reach their ends.
Inputs may be any that keep to these rules, and one draw needn't show every extreme that they name: `expert_ids`: each token names two different experts. Among the 8 tokens of one device no expert is named more than 4 times, and in every draw some expert is named exactly 4 times by the tokens of some device.
All inputs are finite; a program needn't handle non-finite values.
Results may differ from the reference program's by a relative error of at most 0.0049.
Values may be sent and summed in bfloat16 or wider, within the bound.
A program may use at most 128 MiB of HBM per device.

```python
import math
import jax
import jax.numpy as jnp
import numpy as np
from jax import lax

D = 6144
FF = 8192
TOK_DEV = 8
EXPERTS = 8
FFP = 2048
CAP = 4
TOKENS = 1024
DEVICES = 128


def block_scale(key, extent, pieces, smallest, largest):
    level = 1.0
    for axis_at, parts in pieces:
        heights = jax.random.uniform(jax.random.fold_in(jax.random.fold_in(key, 6), axis_at), (parts,), jnp.float32, smallest / len(pieces), largest / len(pieces))
        level = level * jnp.repeat(jnp.exp(heights), extent[axis_at] // parts).reshape((-1,) + (1,) * (len(extent) - 1 - axis_at))
    return level


def deal_out(stream_key, own, number, rows, count, top, most, skew):
    ranking = jax.random.permutation(stream_key, count)
    crowded, usual = load_shares(count, rows * top, most, skew, True), load_shares(count, rows * top, most, skew, False)
    places = jnp.arange(count)

    def named(tallies, turn):
        used = int((tallies > 0).sum())
        fixed = max(1, used // 4)
        shifted = fixed + (places - fixed + turn * (used - fixed)) % max(1, count - fixed)
        return jnp.zeros((count,), jnp.int32).at[ranking[jnp.where(places < fixed, places, shifted)]].set(jnp.asarray(tallies, jnp.int32))

    tallies = jnp.where(number % 4 == 0, named(crowded, number // 4), named(usual, number - number // 4 - 1))
    mixed = jax.random.permutation(jax.random.fold_in(own, 3), count)
    source_of, taker = mixed[0:count // 2 * 2:2], mixed[1:count // 2 * 2:2]
    slack = jnp.minimum(tallies[source_of] - 1, most - tallies[taker]) // 2
    slack = jnp.where((source_of == ranking[0]) | (taker == ranking[0]) | (tallies[taker] == 0), 0, jnp.maximum(slack, 0))
    shifted = jax.random.randint(jax.random.fold_in(own, 4), (count // 2,), 0, 1 << 20) % (slack + 1)
    tallies = tallies.at[source_of].add(-shifted).at[taker].add(shifted)
    items = jnp.searchsorted(jnp.cumsum(tallies), jnp.arange(rows * top), side="right").astype(jnp.int32)
    grid = items.reshape(top, rows).T
    grid = grid[jax.random.permutation(jax.random.fold_in(own, 1), rows)]
    turn = jax.random.randint(jax.random.fold_in(own, 2), (rows, 1), 0, top)
    return jnp.take_along_axis(grid, (jnp.arange(top)[None, :] + turn) % top, axis=1)


def load_shares(amount, total, bound, skew, full):
    portions = [(1 << 20) // math.isqrt(grade ** skew) + 1 for grade in range(1, amount + 1)]
    largest = bound if full else min(bound, max(-(-total // amount), total * portions[0] // sum(portions)))
    least = 1 if total - largest >= amount - 1 else 0
    holding, spare = [largest] + [least] * (amount - 1), total - largest - least * (amount - 1)
    while spare > 0:
        candidates = [i for i in range(1, amount) if holding[i] < largest] or [i for i in range(1, amount) if holding[i] < bound]
        mass, remaining = sum([portions[i] for i in candidates]), spare
        for i in candidates:
            extra = min(bound - holding[i], max(1, remaining * portions[i] // mass), spare)
            holding[i] = holding[i] + extra
            spare = spare - extra
    return np.array(holding)


def gaussian(stream_key, dims, width, most, split=(), held_as=jnp.bfloat16):
    gain = block_scale(stream_key, dims, split, -0.22, 0.18) if split else 1.0
    values = jax.random.normal(stream_key, dims, jnp.float32) * width * gain
    return jnp.minimum(jnp.maximum(values, -most), most).astype(held_as)


def setup_inputs(seed: int = 0) -> dict:
    key_list = jax.random.split(jax.random.key(seed), 7)
    tokens = gaussian(key_list[0], (TOKENS, D), 1.0, 6.0, ((0, 128),))
    router_logits = gaussian(key_list[1], (TOKENS, 2), 1.5, 6.0, ((0, 128),), jnp.float32)
    expert_ids_keys = jax.random.split(jax.random.fold_in(key_list[2], 1), TOKENS // TOK_DEV)
    expert_ids_turns = jax.random.permutation(jax.random.fold_in(key_list[2], 3), TOKENS // TOK_DEV)
    expert_ids = jax.vmap(lambda own, number: deal_out(jax.random.fold_in(key_list[2], 2), own, number, TOK_DEV, EXPERTS, 2, CAP, 2))(expert_ids_keys, expert_ids_turns).reshape((TOKENS, 2))
    w_gate = gaussian(key_list[3], (EXPERTS * 4, D, FFP), D ** -0.5, 0.078125, ((0, 32), (2, 4)))
    w_up = gaussian(key_list[4], (EXPERTS * 4, D, FFP), D ** -0.5, 0.078125, ((0, 32), (2, 4)))
    w_down = gaussian(key_list[5], (EXPERTS * 4, FFP, D), FF ** -0.5, 0.0625, ((0, 32), (1, 4)))
    return dict(tokens=tokens, router_logits=router_logits, expert_ids=expert_ids, w_gate=w_gate, w_up=w_up, w_down=w_down)


def place_slots(ids_block, experts):
    flat_ids = ids_block.reshape(-1)
    hits_mask = (flat_ids[:, None] == jnp.arange(experts, dtype=jnp.int32)[None, :]).astype(jnp.int32)
    earlier = jnp.cumsum(hits_mask, axis=0) - hits_mask
    slot_rank = jnp.sum(earlier * hits_mask, axis=1).astype(jnp.int32)
    return flat_ids.astype(jnp.int32), slot_rank


def expert_ffn(row_block, gate_part, up_part, down_part):
    summed = jnp.zeros((row_block.shape[0], down_part.shape[2]), jnp.float32)
    for quarter in range(4):
        gate_proj = jnp.dot(row_block, gate_part[quarter], preferred_element_type=jnp.float32)
        up_proj = jnp.dot(row_block, up_part[quarter], preferred_element_type=jnp.float32)
        hidden = (jax.nn.silu(gate_proj) * up_proj).astype(jnp.bfloat16)
        summed = summed + jnp.dot(hidden, down_part[quarter], preferred_element_type=jnp.float32)
    return summed


def reference(tokens, router_logits, expert_ids, w_gate, w_up, w_down):
    blocks = expert_ids.reshape(DEVICES, TOK_DEV * 2)
    flat_ids, slot_rank = jax.vmap(lambda b: place_slots(b, EXPERTS))(blocks)
    device_pos = jnp.arange(DEVICES, dtype=jnp.int32)[:, None]
    target = (flat_ids * (DEVICES * CAP) + device_pos * CAP + slot_rank).reshape(-1).astype(jnp.int32)
    repeated = jnp.repeat(tokens, 2, axis=0)
    slab_rows = jnp.zeros((EXPERTS * DEVICES * CAP, D), jnp.bfloat16).at[target].set(repeated)
    slab_rows = slab_rows.reshape(EXPERTS, DEVICES * CAP, D)

    def one_expert(expert):
        gate_part = lax.dynamic_slice_in_dim(w_gate, expert * 4, 4, 0)
        up_part = lax.dynamic_slice_in_dim(w_up, expert * 4, 4, 0)
        down_part = lax.dynamic_slice_in_dim(w_down, expert * 4, 4, 0)
        row_block = lax.dynamic_index_in_dim(slab_rows, expert, 0, keepdims=False)
        return expert_ffn(row_block, gate_part, up_part, down_part)

    outputs = lax.map(one_expert, jnp.arange(EXPERTS, dtype=jnp.int32)).reshape(EXPERTS * DEVICES * CAP, D)
    weights = jax.nn.sigmoid(router_logits - router_logits[:, ::-1]).reshape(-1)
    picked = outputs[target] * weights[:, None]
    mixture = jnp.sum(picked.reshape(TOKENS, 2, D), axis=1)
    return mixture.astype(jnp.bfloat16)
```

```python
import jax
import jax.numpy as jnp
import numpy as np
from jax import lax
from jax.sharding import Mesh
from jax.sharding import PartitionSpec as P

ALL = ("sect", "ey", "ex", "tp")
EXPERT_AXES = ("sect", "ey")
PLANE_AXES = ("ex", "tp")


def place_slots(ids_block, experts):
    flat_ids = ids_block.reshape(-1)
    hits_mask = (flat_ids[:, None] == jnp.arange(experts, dtype=jnp.int32)[None, :]).astype(
        jnp.int32
    )
    earlier = jnp.cumsum(hits_mask, axis=0) - hits_mask
    slot_rank = jnp.sum(earlier * hits_mask, axis=1)
    return (flat_ids, slot_rank)


def per_device(tokens, router_logits, expert_ids, w_gate, w_up, w_down):
    experts_all = lax.axis_size(EXPERT_AXES)
    plane_count = lax.axis_size(PLANE_AXES)
    token_count = tokens.shape[0]
    capacity = min(token_count, 4 * token_count // experts_all)
    model_width = tokens.shape[1]
    flat_ids, slot_rank = place_slots(expert_ids, experts_all)
    columns = flat_ids * capacity + slot_rank
    positions = jnp.arange(experts_all * capacity, dtype=jnp.int32)
    picker = (positions[:, None] == columns[None, :]).astype(jnp.bfloat16)
    repeated = jnp.repeat(tokens, 2, axis=0)
    slab = jnp.dot(picker, repeated, preferred_element_type=jnp.float32).astype(jnp.bfloat16)
    slab = slab.reshape(experts_all, capacity, model_width)
    column_rows = lax.all_to_all(slab, EXPERT_AXES, split_axis=0, concat_axis=0, tiled=True)
    plane_rows = lax.all_gather(column_rows, PLANE_AXES, axis=0, tiled=False)
    row_count = plane_count * experts_all * capacity
    expert_rows = plane_rows.reshape(row_count, model_width)
    gate_proj = jnp.dot(expert_rows, w_gate[0], preferred_element_type=jnp.float32)
    up_proj = jnp.dot(expert_rows, w_up[0], preferred_element_type=jnp.float32)
    hidden = (jax.nn.silu(gate_proj) * up_proj).astype(jnp.bfloat16)
    partial_value = jnp.dot(hidden, w_down[0], preferred_element_type=jnp.float32)
    partial_value = partial_value.reshape(plane_count, experts_all * capacity, model_width)
    owned = lax.psum_scatter(partial_value, PLANE_AXES, scatter_dimension=0, tiled=True)
    owned = owned.reshape(experts_all, capacity, model_width)
    returned = lax.all_to_all(owned, EXPERT_AXES, split_axis=0, concat_axis=0, tiled=True)
    expert_out = returned.reshape(experts_all * capacity, model_width)
    weights = jax.nn.sigmoid(router_logits - router_logits[:, ::-1]).reshape(-1)
    picked = jnp.take(expert_out, columns, axis=0) * weights[:, None]
    mixture = jnp.sum(picked.reshape(token_count, 2, model_width), axis=1)
    return mixture.astype(jnp.bfloat16)


def x_extent(devices):
    coords = [getattr(d, "coords", None) for d in devices.flat]
    if all(c is not None for c in coords):
        return len({c[0] for c in coords})
    return int(round(np.sqrt(devices.shape[1])))


def solution(mesh):
    devices = mesh.devices
    sect, exp, tp = devices.shape
    ex = x_extent(devices)
    fine = Mesh(devices.reshape(sect, exp // ex, ex, tp), ALL)
    in_specs = (
        P(ALL, None),
        P(ALL, None),
        P(ALL, None),
        P(EXPERT_AXES + PLANE_AXES[:1], None, "tp"),
        P(EXPERT_AXES + PLANE_AXES[:1], None, "tp"),
        P(EXPERT_AXES + PLANE_AXES[:1], "tp", None),
    )
    out_specs = P(ALL, None)
    return jax.shard_map(
        per_device, mesh=fine, in_specs=in_specs, out_specs=out_specs, check_vma=False
    )
```

```python
import jax
import jax.numpy as jnp
import numpy as np
from jax import lax
from jax.experimental import pallas as pl
from jax.experimental.pallas import tpu as pltpu
from jax.sharding import Mesh
from jax.sharding import PartitionSpec as P

MESH_ID = pl.DeviceIdType.MESH


def rs_kernel(p_ref, out_ref, s1, s2, send1, recv1, send2, recv2):
    nx, nz, rows, width = p_ref.shape
    quarter = width // 4
    c = lax.axis_index("sect")
    y = lax.axis_index("ey")
    mx = lax.axis_index("ex")
    mz = lax.axis_index("tp")

    def dev(axis, d):
        if axis == "z":
            return (c, y, mx, lax.rem(mz + d + nz, nz))
        return (c, y, lax.rem(mx + d + nx, nx), mz)

    barrier = pltpu.get_barrier_semaphore()
    for axis in ("x", "z"):
        for d in (1, -1):
            pl.semaphore_signal(barrier, inc=1, device_id=dev(axis, d), device_id_type=MESH_ID)
    pl.semaphore_wait(barrier, 4)

    rings = [("z", 1), ("z", -1), ("x", 1), ("x", -1)]

    def me_on(axis):
        return mz if axis == "z" else mx

    def size_on(axis):
        return nz if axis == "z" else nx

    def cols(r):
        return pl.ds(r * quarter, quarter)

    def own1(r, j):
        if rings[r][0] == "z":
            return p_ref.at[:, j, :, cols(r)]
        return p_ref.at[j, :, :, cols(r)]

    def own2(r, i):
        return s1.at[r, size_on(rings[r][0]) - 2, i]

    def other(axis):
        return "x" if axis == "z" else "z"

    def run_phase(axis_of, own, slots, send, recv, lead):
        copies = {}
        n = size_on(axis_of(0))
        for s in range(n - 1):
            for r in range(4):
                axis, d = axis_of(r), rings[r][1]
                me = me_on(axis)
                j = lax.rem(me + n * (s + 2) - d * (s + 1), n)
                if s == 0:
                    src = own(r, j)
                else:
                    copies[(r, s - 1)].wait_recv()
                    for t in range(lead):
                        slots[r, s - 1, t] += own(r, j)[t]
                    src = slots.at[r, s - 1]
                cp = pltpu.make_async_remote_copy(
                    src_ref=src,
                    dst_ref=slots.at[r, s],
                    send_sem=send.at[r, s],
                    recv_sem=recv.at[r, s],
                    device_id=dev(axis, d),
                    device_id_type=MESH_ID,
                )
                cp.start()
                copies[(r, s)] = cp
        return copies, n

    def add_own(slot_ref, own_ref, lead):
        for t in range(lead):
            slot_ref[t] += own_ref[t]

    copies1, n1 = run_phase(lambda r: rings[r][0], own1, s1, send1, recv1, 4)
    for r in range(4):
        copies1[(r, n1 - 2)].wait_recv()
        axis = rings[r][0]
        add_own(s1.at[r, n1 - 2], own1(r, me_on(axis)), 4)

    def own2b(r, i):
        return s1.at[r, n1 - 2, i]

    def run_phase2():
        copies = {}
        n = 4
        for s in range(n - 1):
            for r in range(4):
                axis, d = other(rings[r][0]), rings[r][1]
                me = me_on(axis)
                j = lax.rem(me + n * (s + 2) - d * (s + 1), n)
                if s == 0:
                    src = own2b(r, j)
                else:
                    copies[(r, s - 1)].wait_recv()
                    s2[r, s - 1] += own2b(r, j)[...]
                    src = s2.at[r, s - 1]
                cp = pltpu.make_async_remote_copy(
                    src_ref=src,
                    dst_ref=s2.at[r, s],
                    send_sem=send2.at[r, s],
                    recv_sem=recv2.at[r, s],
                    device_id=dev(axis, d),
                    device_id_type=MESH_ID,
                )
                cp.start()
                copies[(r, s)] = cp
        return copies, n

    copies2, n2 = run_phase2()
    for r in range(4):
        copies2[(r, n2 - 2)].wait_recv()
        axis = other(rings[r][0])
        out_ref[:, cols(r)] = s2[r, n2 - 2] + own2b(r, me_on(axis))[...]
    for cp in list(copies1.values()) + list(copies2.values()):
        cp.wait_send()


def plane_reduce_scatter(partial):
    nx, nz, rows, width = partial.shape
    quarter = width // 4
    return pl.pallas_call(
        rs_kernel,
        out_shape=jax.ShapeDtypeStruct((rows, width), jnp.float32),
        in_specs=[pl.BlockSpec(memory_space=pltpu.VMEM)],
        out_specs=pl.BlockSpec(memory_space=pltpu.VMEM),
        scratch_shapes=[
            pltpu.VMEM((4, nz - 1, nx, rows, quarter), jnp.float32),
            pltpu.VMEM((4, nx - 1, rows, quarter), jnp.float32),
            pltpu.SemaphoreType.DMA((4, nz - 1)),
            pltpu.SemaphoreType.DMA((4, nz - 1)),
            pltpu.SemaphoreType.DMA((4, nx - 1)),
            pltpu.SemaphoreType.DMA((4, nx - 1)),
        ],
        compiler_params=pltpu.CompilerParams(
            collective_id=0, has_side_effects=True, vmem_limit_bytes=60 * 1024 * 1024
        ),
    )(partial)

ALL = ("sect", "ey", "ex", "tp")
EXPERT_AXES = ("sect", "ey")
PLANE_AXES = ("ex", "tp")


def place_slots(ids_block, experts):
    flat_ids = ids_block.reshape(-1)
    hits_mask = (flat_ids[:, None] == jnp.arange(experts, dtype=jnp.int32)[None, :]).astype(
        jnp.int32
    )
    earlier = jnp.cumsum(hits_mask, axis=0) - hits_mask
    slot_rank = jnp.sum(earlier * hits_mask, axis=1)
    return (flat_ids, slot_rank)


def per_device(tokens, router_logits, expert_ids, w_gate, w_up, w_down):
    experts_all = lax.axis_size(EXPERT_AXES)
    plane_count = lax.axis_size(PLANE_AXES)
    token_count = tokens.shape[0]
    capacity = min(token_count, 4 * token_count // experts_all)
    model_width = tokens.shape[1]
    flat_ids, slot_rank = place_slots(expert_ids, experts_all)
    columns = flat_ids * capacity + slot_rank
    positions = jnp.arange(experts_all * capacity, dtype=jnp.int32)
    picker = (positions[:, None] == columns[None, :]).astype(jnp.bfloat16)
    repeated = jnp.repeat(tokens, 2, axis=0)
    slab = jnp.dot(picker, repeated, preferred_element_type=jnp.float32).astype(jnp.bfloat16)
    slab = slab.reshape(experts_all, capacity, model_width)
    column_rows = lax.all_to_all(slab, EXPERT_AXES, split_axis=0, concat_axis=0, tiled=True)
    plane_rows = lax.all_gather(column_rows, PLANE_AXES, axis=0, tiled=False)
    row_count = plane_count * experts_all * capacity
    expert_rows = plane_rows.reshape(row_count, model_width)
    gate_proj = jnp.dot(expert_rows, w_gate[0], preferred_element_type=jnp.float32)
    up_proj = jnp.dot(expert_rows, w_up[0], preferred_element_type=jnp.float32)
    hidden = (jax.nn.silu(gate_proj) * up_proj).astype(jnp.bfloat16)
    partial_value = jnp.dot(hidden, w_down[0], preferred_element_type=jnp.float32)
    nx = lax.axis_size("ex")
    partial_value = partial_value.reshape(
        nx, plane_count // nx, experts_all * capacity, model_width
    )
    owned = plane_reduce_scatter(partial_value)
    owned = owned.reshape(experts_all, capacity, model_width)
    returned = lax.all_to_all(owned, EXPERT_AXES, split_axis=0, concat_axis=0, tiled=True)
    expert_out = returned.reshape(experts_all * capacity, model_width)
    weights = jax.nn.sigmoid(router_logits - router_logits[:, ::-1]).reshape(-1)
    picked = jnp.take(expert_out, columns, axis=0) * weights[:, None]
    mixture = jnp.sum(picked.reshape(token_count, 2, model_width), axis=1)
    return mixture.astype(jnp.bfloat16)


def x_extent(devices):
    coords = [getattr(d, "coords", None) for d in devices.flat]
    if all(c is not None for c in coords):
        return len({c[0] for c in coords})
    return int(round(np.sqrt(devices.shape[1])))


def solution(mesh):
    devices = mesh.devices
    sect, exp, tp = devices.shape
    ex = x_extent(devices)
    fine = Mesh(devices.reshape(sect, exp // ex, ex, tp), ALL)
    in_specs = (
        P(ALL, None),
        P(ALL, None),
        P(ALL, None),
        P(EXPERT_AXES + PLANE_AXES[:1], None, "tp"),
        P(EXPERT_AXES + PLANE_AXES[:1], None, "tp"),
        P(EXPERT_AXES + PLANE_AXES[:1], "tp", None),
    )
    out_specs = P(ALL, None)
    return jax.shard_map(
        per_device, mesh=fine, in_specs=in_specs, out_specs=out_specs, check_vma=False
    )
```

```python
import jax
import jax.numpy as jnp
import numpy as np
from jax import lax
from jax.experimental import pallas as pl
from jax.experimental.pallas import tpu as pltpu
from jax.sharding import Mesh
from jax.sharding import PartitionSpec as P

MESH_ID = pl.DeviceIdType.MESH


def rs_kernel(p_ref, out_ref, s1, s2, send1, recv1, send2, recv2):
    nx, nz, rows, width = p_ref.shape
    quarter = width // 4
    c = lax.axis_index("sect")
    y = lax.axis_index("ey")
    mx = lax.axis_index("ex")
    mz = lax.axis_index("tp")

    def dev(axis, d):
        if axis == "z":
            return (c, y, mx, lax.rem(mz + d + nz, nz))
        return (c, y, lax.rem(mx + d + nx, nx), mz)

    barrier = pltpu.get_barrier_semaphore()
    for axis in ("x", "z"):
        for d in (1, -1):
            pl.semaphore_signal(barrier, inc=1, device_id=dev(axis, d), device_id_type=MESH_ID)
    pl.semaphore_wait(barrier, 4)

    rings = [("z", 1), ("z", -1), ("x", 1), ("x", -1)]

    def me_on(axis):
        return mz if axis == "z" else mx

    def size_on(axis):
        return nz if axis == "z" else nx

    def cols(r):
        return pl.ds(r * quarter, quarter)

    def own1(r, j):
        if rings[r][0] == "z":
            return p_ref.at[:, j, :, cols(r)]
        return p_ref.at[j, :, :, cols(r)]

    def own2(r, i):
        return s1.at[r, size_on(rings[r][0]) - 2, i]

    def other(axis):
        return "x" if axis == "z" else "z"

    def run_phase(axis_of, own, slots, send, recv, lead):
        copies = {}
        n = size_on(axis_of(0))
        for s in range(n - 1):
            for r in range(4):
                axis, d = axis_of(r), rings[r][1]
                me = me_on(axis)
                j = lax.rem(me + n * (s + 2) - d * (s + 1), n)
                if s == 0:
                    src = own(r, j)
                else:
                    copies[(r, s - 1)].wait_recv()
                    for t in range(lead):
                        slots[r, s - 1, t] += own(r, j)[t]
                    src = slots.at[r, s - 1]
                cp = pltpu.make_async_remote_copy(
                    src_ref=src,
                    dst_ref=slots.at[r, s],
                    send_sem=send.at[r, s],
                    recv_sem=recv.at[r, s],
                    device_id=dev(axis, d),
                    device_id_type=MESH_ID,
                )
                cp.start()
                copies[(r, s)] = cp
        return copies, n

    def add_own(slot_ref, own_ref, lead):
        for t in range(lead):
            slot_ref[t] += own_ref[t]

    copies1, n1 = run_phase(lambda r: rings[r][0], own1, s1, send1, recv1, 4)
    for r in range(4):
        copies1[(r, n1 - 2)].wait_recv()
        axis = rings[r][0]
        add_own(s1.at[r, n1 - 2], own1(r, me_on(axis)), 4)

    def own2b(r, i):
        return s1.at[r, n1 - 2, i]

    def run_phase2():
        copies = {}
        n = 4
        for s in range(n - 1):
            for r in range(4):
                axis, d = other(rings[r][0]), rings[r][1]
                me = me_on(axis)
                j = lax.rem(me + n * (s + 2) - d * (s + 1), n)
                if s == 0:
                    src = own2b(r, j)
                else:
                    copies[(r, s - 1)].wait_recv()
                    s2[r, s - 1] += own2b(r, j)[...]
                    src = s2.at[r, s - 1]
                cp = pltpu.make_async_remote_copy(
                    src_ref=src,
                    dst_ref=s2.at[r, s],
                    send_sem=send2.at[r, s],
                    recv_sem=recv2.at[r, s],
                    device_id=dev(axis, d),
                    device_id_type=MESH_ID,
                )
                cp.start()
                copies[(r, s)] = cp
        return copies, n

    copies2, n2 = run_phase2()
    for r in range(4):
        copies2[(r, n2 - 2)].wait_recv()
        axis = other(rings[r][0])
        out_ref[:, cols(r)] = s2[r, n2 - 2] + own2b(r, me_on(axis))[...]
    for cp in list(copies1.values()) + list(copies2.values()):
        cp.wait_send()


def plane_reduce_scatter(partial):
    nx, nz, rows, width = partial.shape
    quarter = width // 4
    return pl.pallas_call(
        rs_kernel,
        out_shape=jax.ShapeDtypeStruct((rows, width), jnp.float32),
        in_specs=[pl.BlockSpec(memory_space=pltpu.VMEM)],
        out_specs=pl.BlockSpec(memory_space=pltpu.VMEM),
        scratch_shapes=[
            pltpu.VMEM((4, nz - 1, nx, rows, quarter), jnp.float32),
            pltpu.VMEM((4, nx - 1, rows, quarter), jnp.float32),
            pltpu.SemaphoreType.DMA((4, nz - 1)),
            pltpu.SemaphoreType.DMA((4, nz - 1)),
            pltpu.SemaphoreType.DMA((4, nx - 1)),
            pltpu.SemaphoreType.DMA((4, nx - 1)),
        ],
        compiler_params=pltpu.CompilerParams(
            collective_id=0, has_side_effects=True, vmem_limit_bytes=60 * 1024 * 1024
        ),
    )(partial)

def ag_kernel(in_ref, out_ref, local_sem, send1, recv1, send2, recv2):
    nx, nz, rows, width = out_ref.shape
    quarter = width // 4
    c = lax.axis_index("sect")
    y = lax.axis_index("ey")
    mx = lax.axis_index("ex")
    mz = lax.axis_index("tp")

    def dev(axis, d):
        if axis == "z":
            return (c, y, mx, lax.rem(mz + d + nz, nz))
        return (c, y, lax.rem(mx + d + nx, nx), mz)

    barrier = pltpu.get_barrier_semaphore()
    for axis in ("x", "z"):
        for d in (1, -1):
            pl.semaphore_signal(barrier, inc=1, device_id=dev(axis, d), device_id_type=MESH_ID)
    pl.semaphore_wait(barrier, 4)

    local = pltpu.make_async_copy(in_ref, out_ref.at[mx, mz], local_sem)
    local.start()

    rings = [("z", 1), ("z", -1), ("x", 1), ("x", -1)]

    def cols(r):
        return pl.ds(r * quarter, quarter)

    def block(axis, r, k):
        if axis == "z":
            return out_ref.at[mx, k, :, cols(r)]
        return out_ref.at[k, mz, :, cols(r)]

    def plane_block(axis, r, k):
        if axis == "x":
            return out_ref.at[k, :, :, cols(r)]
        return out_ref.at[:, k, :, cols(r)]

    def me_on(axis):
        return mz if axis == "z" else mx

    def ring_phase(axis_of, view, first_src, send, recv, sizes):
        copies = {}
        n = sizes
        for s in range(n - 1):
            for r in range(4):
                axis, d = axis_of(r), rings[r][1]
                me = me_on(axis)
                k = lax.rem(me + n * (s + 1) - d * s, n)
                if s == 0:
                    src = first_src(r)
                else:
                    copies[(r, s - 1)].wait_recv()
                    src = view(axis, r, k)
                cp = pltpu.make_async_remote_copy(
                    src_ref=src,
                    dst_ref=view(axis, r, k),
                    send_sem=send.at[r, s],
                    recv_sem=recv.at[r, s],
                    device_id=dev(axis, d),
                    device_id_type=MESH_ID,
                )
                cp.start()
                copies[(r, s)] = cp
        for r in range(4):
            copies[(r, n - 2)].wait_recv()
        return copies

    copies1 = ring_phase(
        lambda r: rings[r][0], block, lambda r: in_ref.at[:, cols(r)], send1, recv1, nz
    )
    local.wait()

    def second(r):
        return "x" if rings[r][0] == "z" else "z"

    copies2 = ring_phase(
        second,
        plane_block,
        lambda r: plane_block(second(r), r, me_on(second(r))),
        send2,
        recv2,
        nx,
    )
    for cp in list(copies1.values()) + list(copies2.values()):
        cp.wait_send()


def plane_all_gather(rows_block, nx, nz):
    rows, width = rows_block.shape
    return pl.pallas_call(
        ag_kernel,
        out_shape=jax.ShapeDtypeStruct((nx, nz, rows, width), rows_block.dtype),
        in_specs=[pl.BlockSpec(memory_space=pltpu.VMEM)],
        out_specs=pl.BlockSpec(memory_space=pltpu.VMEM),
        scratch_shapes=[
            pltpu.SemaphoreType.DMA(()),
            pltpu.SemaphoreType.DMA((4, nz - 1)),
            pltpu.SemaphoreType.DMA((4, nz - 1)),
            pltpu.SemaphoreType.DMA((4, nx - 1)),
            pltpu.SemaphoreType.DMA((4, nx - 1)),
        ],
        compiler_params=pltpu.CompilerParams(
            collective_id=1, has_side_effects=True, vmem_limit_bytes=60 * 1024 * 1024
        ),
    )(rows_block)


ALL = ("sect", "ey", "ex", "tp")
EXPERT_AXES = ("sect", "ey")
PLANE_AXES = ("ex", "tp")


def place_slots(ids_block, experts):
    flat_ids = ids_block.reshape(-1)
    hits_mask = (flat_ids[:, None] == jnp.arange(experts, dtype=jnp.int32)[None, :]).astype(
        jnp.int32
    )
    earlier = jnp.cumsum(hits_mask, axis=0) - hits_mask
    slot_rank = jnp.sum(earlier * hits_mask, axis=1)
    return (flat_ids, slot_rank)


def per_device(tokens, router_logits, expert_ids, w_gate, w_up, w_down):
    experts_all = lax.axis_size(EXPERT_AXES)
    plane_count = lax.axis_size(PLANE_AXES)
    token_count = tokens.shape[0]
    capacity = min(token_count, 4 * token_count // experts_all)
    model_width = tokens.shape[1]
    flat_ids, slot_rank = place_slots(expert_ids, experts_all)
    columns = flat_ids * capacity + slot_rank
    positions = jnp.arange(experts_all * capacity, dtype=jnp.int32)
    picker = (positions[:, None] == columns[None, :]).astype(jnp.bfloat16)
    repeated = jnp.repeat(tokens, 2, axis=0)
    slab = jnp.dot(picker, repeated, preferred_element_type=jnp.float32).astype(jnp.bfloat16)
    slab = slab.reshape(experts_all, capacity, model_width)
    column_rows = lax.all_to_all(slab, EXPERT_AXES, split_axis=0, concat_axis=0, tiled=True)
    nx = lax.axis_size("ex")
    plane_rows = plane_all_gather(
        column_rows.reshape(experts_all * capacity, model_width), nx, plane_count // nx
    )
    row_count = plane_count * experts_all * capacity
    expert_rows = plane_rows.reshape(row_count, model_width)
    gate_proj = jnp.dot(expert_rows, w_gate[0], preferred_element_type=jnp.float32)
    up_proj = jnp.dot(expert_rows, w_up[0], preferred_element_type=jnp.float32)
    hidden = (jax.nn.silu(gate_proj) * up_proj).astype(jnp.bfloat16)
    partial_value = jnp.dot(hidden, w_down[0], preferred_element_type=jnp.float32)
    partial_value = partial_value.reshape(
        nx, plane_count // nx, experts_all * capacity, model_width
    )
    owned = plane_reduce_scatter(partial_value)
    owned = owned.reshape(experts_all, capacity, model_width)
    returned = lax.all_to_all(owned, EXPERT_AXES, split_axis=0, concat_axis=0, tiled=True)
    expert_out = returned.reshape(experts_all * capacity, model_width)
    weights = jax.nn.sigmoid(router_logits - router_logits[:, ::-1]).reshape(-1)
    picked = jnp.take(expert_out, columns, axis=0) * weights[:, None]
    mixture = jnp.sum(picked.reshape(token_count, 2, model_width), axis=1)
    return mixture.astype(jnp.bfloat16)


def x_extent(devices):
    coords = [getattr(d, "coords", None) for d in devices.flat]
    if all(c is not None for c in coords):
        return len({c[0] for c in coords})
    return int(round(np.sqrt(devices.shape[1])))


def solution(mesh):
    devices = mesh.devices
    sect, exp, tp = devices.shape
    ex = x_extent(devices)
    fine = Mesh(devices.reshape(sect, exp // ex, ex, tp), ALL)
    in_specs = (
        P(ALL, None),
        P(ALL, None),
        P(ALL, None),
        P(EXPERT_AXES + PLANE_AXES[:1], None, "tp"),
        P(EXPERT_AXES + PLANE_AXES[:1], None, "tp"),
        P(EXPERT_AXES + PLANE_AXES[:1], "tp", None),
    )
    out_specs = P(ALL, None)
    return jax.shard_map(
        per_device, mesh=fine, in_specs=in_specs, out_specs=out_specs, check_vma=False
    )
```

```python
import functools

import jax
import jax.numpy as jnp
import numpy as np
from jax import lax
from jax.experimental import pallas as pl
from jax.experimental.pallas import tpu as pltpu
from jax.sharding import Mesh
from jax.sharding import PartitionSpec as P

MESH_ID = pl.DeviceIdType.MESH


def rs_kernel(nsect, ny, p_ref, out_ref, fin, s1, s2, send1, recv1, send2, recv2, local_sem, ret_send, ret_recv):
    nx, nz, rows, width = p_ref.shape
    groups = nsect * ny
    slots = rows // groups
    quarter = width // 4
    c = lax.axis_index("sect")
    y = lax.axis_index("ey")
    mx = lax.axis_index("ex")
    mz = lax.axis_index("tp")

    def dev(axis, d):
        if axis == "z":
            return (c, y, mx, lax.rem(mz + d + nz, nz))
        return (c, y, lax.rem(mx + d + nx, nx), mz)

    me_group = c * ny + y

    def peer(o):
        g = lax.rem(me_group + o, groups)
        return (g // ny, lax.rem(g, ny), mx, mz)

    barrier = pltpu.get_barrier_semaphore()
    for axis in ("x", "z"):
        for d in (1, -1):
            pl.semaphore_signal(barrier, inc=1, device_id=dev(axis, d), device_id_type=MESH_ID)
    for o in range(1, groups):
        pl.semaphore_signal(barrier, inc=1, device_id=peer(o), device_id_type=MESH_ID)
    pl.semaphore_wait(barrier, 4 + groups - 1)

    rings = [("z", 1), ("z", -1), ("x", 1), ("x", -1)]

    def me_on(axis):
        return mz if axis == "z" else mx

    def size_on(axis):
        return nz if axis == "z" else nx

    def cols(r):
        return pl.ds(r * quarter, quarter)

    def own1(r, j):
        if rings[r][0] == "z":
            return p_ref.at[:, j, :, cols(r)]
        return p_ref.at[j, :, :, cols(r)]

    def own2(r, i):
        return s1.at[r, size_on(rings[r][0]) - 2, i]

    def other(axis):
        return "x" if axis == "z" else "z"

    def run_phase(axis_of, own, slots, send, recv, lead):
        copies = {}
        n = size_on(axis_of(0))
        for s in range(n - 1):
            for r in range(4):
                axis, d = axis_of(r), rings[r][1]
                me = me_on(axis)
                j = lax.rem(me + n * (s + 2) - d * (s + 1), n)
                if s == 0:
                    src = own(r, j)
                else:
                    copies[(r, s - 1)].wait_recv()
                    for t in range(lead):
                        slots[r, s - 1, t] += own(r, j)[t]
                    src = slots.at[r, s - 1]
                cp = pltpu.make_async_remote_copy(
                    src_ref=src,
                    dst_ref=slots.at[r, s],
                    send_sem=send.at[r, s],
                    recv_sem=recv.at[r, s],
                    device_id=dev(axis, d),
                    device_id_type=MESH_ID,
                )
                cp.start()
                copies[(r, s)] = cp
        return copies, n

    def add_own(slot_ref, own_ref, lead):
        for t in range(lead):
            slot_ref[t] += own_ref[t]

    copies1, n1 = run_phase(lambda r: rings[r][0], own1, s1, send1, recv1, nx)
    for r in range(4):
        copies1[(r, n1 - 2)].wait_recv()
        axis = rings[r][0]
        add_own(s1.at[r, n1 - 2], own1(r, me_on(axis)), nx)

    def own2b(r, i):
        return s1.at[r, n1 - 2, i]

    def run_phase2():
        copies = {}
        n = nx
        for s in range(n - 1):
            for r in range(4):
                axis, d = other(rings[r][0]), rings[r][1]
                me = me_on(axis)
                j = lax.rem(me + n * (s + 2) - d * (s + 1), n)
                if s == 0:
                    src = own2b(r, j)
                else:
                    copies[(r, s - 1)].wait_recv()
                    s2[r, s - 1] += own2b(r, j)[...]
                    src = s2.at[r, s - 1]
                cp = pltpu.make_async_remote_copy(
                    src_ref=src,
                    dst_ref=s2.at[r, s],
                    send_sem=send2.at[r, s],
                    recv_sem=recv2.at[r, s],
                    device_id=dev(axis, d),
                    device_id_type=MESH_ID,
                )
                cp.start()
                copies[(r, s)] = cp
        return copies, n

    copies2, n2 = run_phase2()
    for r in range(4):
        copies2[(r, n2 - 2)].wait_recv()
        axis = other(rings[r][0])
        fin[:, cols(r)] = s2[r, n2 - 2] + own2b(r, me_on(axis))[...]
    mine = pl.ds(pl.multiple_of(me_group * slots, slots), slots)
    local = pltpu.make_async_copy(fin.at[mine], out_ref.at[mine], local_sem)
    local.start()
    returns = []
    for o in range(1, groups):
        g = lax.rem(me_group + o, groups)
        cp = pltpu.make_async_remote_copy(
            src_ref=fin.at[pl.ds(pl.multiple_of(g * slots, slots), slots)],
            dst_ref=out_ref.at[mine],
            send_sem=ret_send.at[o],
            recv_sem=ret_recv.at[o],
            device_id=peer(o),
            device_id_type=MESH_ID,
        )
        cp.start()
        returns.append(cp)
    local.wait()
    for cp in returns:
        cp.wait_recv()
    for cp in list(copies1.values()) + list(copies2.values()) + returns:
        cp.wait_send()


def plane_reduce_scatter(partial, nsect, ny):
    nx, nz, rows, width = partial.shape
    quarter = width // 4
    groups = nsect * ny
    return pl.pallas_call(
        functools.partial(rs_kernel, nsect, ny),
        out_shape=jax.ShapeDtypeStruct((rows, width), jnp.float32),
        in_specs=[pl.BlockSpec(memory_space=pltpu.VMEM)],
        out_specs=pl.BlockSpec(memory_space=pltpu.VMEM),
        scratch_shapes=[
            pltpu.VMEM((rows, width), jnp.float32),
            pltpu.VMEM((4, nz - 1, nx, rows, quarter), jnp.float32),
            pltpu.VMEM((4, nx - 1, rows, quarter), jnp.float32),
            pltpu.SemaphoreType.DMA((4, nz - 1)),
            pltpu.SemaphoreType.DMA((4, nz - 1)),
            pltpu.SemaphoreType.DMA((4, nx - 1)),
            pltpu.SemaphoreType.DMA((4, nx - 1)),
            pltpu.SemaphoreType.DMA(()),
            pltpu.SemaphoreType.DMA((groups,)),
            pltpu.SemaphoreType.DMA((groups,)),
        ],
        compiler_params=pltpu.CompilerParams(
            collective_id=0, has_side_effects=True, vmem_limit_bytes=60 * 1024 * 1024
        ),
    )(partial)

def ag_kernel(in_ref, out_ref, local_sem, send1, recv1, send2, recv2):
    nx, nz, rows, width = out_ref.shape
    quarter = width // 4
    c = lax.axis_index("sect")
    y = lax.axis_index("ey")
    mx = lax.axis_index("ex")
    mz = lax.axis_index("tp")

    def dev(axis, d):
        if axis == "z":
            return (c, y, mx, lax.rem(mz + d + nz, nz))
        return (c, y, lax.rem(mx + d + nx, nx), mz)

    barrier = pltpu.get_barrier_semaphore()
    for axis in ("x", "z"):
        for d in (1, -1):
            pl.semaphore_signal(barrier, inc=1, device_id=dev(axis, d), device_id_type=MESH_ID)
    pl.semaphore_wait(barrier, 4)

    local = pltpu.make_async_copy(in_ref, out_ref.at[mx, mz], local_sem)
    local.start()

    rings = [("z", 1), ("z", -1), ("x", 1), ("x", -1)]

    def cols(r):
        return pl.ds(r * quarter, quarter)

    def block(axis, r, k):
        if axis == "z":
            return out_ref.at[mx, k, :, cols(r)]
        return out_ref.at[k, mz, :, cols(r)]

    def plane_block(axis, r, k):
        if axis == "x":
            return out_ref.at[k, :, :, cols(r)]
        return out_ref.at[:, k, :, cols(r)]

    def me_on(axis):
        return mz if axis == "z" else mx

    def ring_phase(axis_of, view, first_src, send, recv, sizes):
        copies = {}
        n = sizes
        for s in range(n - 1):
            for r in range(4):
                axis, d = axis_of(r), rings[r][1]
                me = me_on(axis)
                k = lax.rem(me + n * (s + 1) - d * s, n)
                if s == 0:
                    src = first_src(r)
                else:
                    copies[(r, s - 1)].wait_recv()
                    src = view(axis, r, k)
                cp = pltpu.make_async_remote_copy(
                    src_ref=src,
                    dst_ref=view(axis, r, k),
                    send_sem=send.at[r, s],
                    recv_sem=recv.at[r, s],
                    device_id=dev(axis, d),
                    device_id_type=MESH_ID,
                )
                cp.start()
                copies[(r, s)] = cp
        for r in range(4):
            copies[(r, n - 2)].wait_recv()
        return copies

    copies1 = ring_phase(
        lambda r: rings[r][0], block, lambda r: in_ref.at[:, cols(r)], send1, recv1, nz
    )
    local.wait()

    def second(r):
        return "x" if rings[r][0] == "z" else "z"

    copies2 = ring_phase(
        second,
        plane_block,
        lambda r: plane_block(second(r), r, me_on(second(r))),
        send2,
        recv2,
        nx,
    )
    for cp in list(copies1.values()) + list(copies2.values()):
        cp.wait_send()


def plane_all_gather(rows_block, nx, nz):
    rows, width = rows_block.shape
    return pl.pallas_call(
        ag_kernel,
        out_shape=jax.ShapeDtypeStruct((nx, nz, rows, width), rows_block.dtype),
        in_specs=[pl.BlockSpec(memory_space=pltpu.VMEM)],
        out_specs=pl.BlockSpec(memory_space=pltpu.VMEM),
        scratch_shapes=[
            pltpu.SemaphoreType.DMA(()),
            pltpu.SemaphoreType.DMA((4, nz - 1)),
            pltpu.SemaphoreType.DMA((4, nz - 1)),
            pltpu.SemaphoreType.DMA((4, nx - 1)),
            pltpu.SemaphoreType.DMA((4, nx - 1)),
        ],
        compiler_params=pltpu.CompilerParams(
            collective_id=1, has_side_effects=True, vmem_limit_bytes=60 * 1024 * 1024
        ),
    )(rows_block)


ALL = ("sect", "ey", "ex", "tp")
EXPERT_AXES = ("sect", "ey")
PLANE_AXES = ("ex", "tp")


def place_slots(ids_block, experts):
    flat_ids = ids_block.reshape(-1)
    hits_mask = (flat_ids[:, None] == jnp.arange(experts, dtype=jnp.int32)[None, :]).astype(
        jnp.int32
    )
    earlier = jnp.cumsum(hits_mask, axis=0) - hits_mask
    slot_rank = jnp.sum(earlier * hits_mask, axis=1)
    return (flat_ids, slot_rank)


def per_device(tokens, router_logits, expert_ids, w_gate, w_up, w_down):
    experts_all = lax.axis_size(EXPERT_AXES)
    plane_count = lax.axis_size(PLANE_AXES)
    token_count = tokens.shape[0]
    capacity = min(token_count, 4 * token_count // experts_all)
    model_width = tokens.shape[1]
    flat_ids, slot_rank = place_slots(expert_ids, experts_all)
    columns = flat_ids * capacity + slot_rank
    positions = jnp.arange(experts_all * capacity, dtype=jnp.int32)
    picker = (positions[:, None] == columns[None, :]).astype(jnp.bfloat16)
    repeated = jnp.repeat(tokens, 2, axis=0)
    slab = jnp.dot(picker, repeated, preferred_element_type=jnp.float32).astype(jnp.bfloat16)
    slab = slab.reshape(experts_all, capacity, model_width)
    column_rows = lax.all_to_all(slab, EXPERT_AXES, split_axis=0, concat_axis=0, tiled=True)
    nx = lax.axis_size("ex")
    plane_rows = plane_all_gather(
        column_rows.reshape(experts_all * capacity, model_width), nx, plane_count // nx
    )
    row_count = plane_count * experts_all * capacity
    expert_rows = plane_rows.reshape(row_count, model_width)
    gate_proj = jnp.dot(expert_rows, w_gate[0], preferred_element_type=jnp.float32)
    up_proj = jnp.dot(expert_rows, w_up[0], preferred_element_type=jnp.float32)
    hidden = (jax.nn.silu(gate_proj) * up_proj).astype(jnp.bfloat16)
    partial_value = jnp.dot(hidden, w_down[0], preferred_element_type=jnp.float32)
    partial_value = partial_value.reshape(
        nx, plane_count // nx, experts_all * capacity, model_width
    )
    expert_out = plane_reduce_scatter(partial_value, lax.axis_size("sect"), lax.axis_size("ey"))
    weights = jax.nn.sigmoid(router_logits - router_logits[:, ::-1]).reshape(-1)
    picked = jnp.take(expert_out, columns, axis=0) * weights[:, None]
    mixture = jnp.sum(picked.reshape(token_count, 2, model_width), axis=1)
    return mixture.astype(jnp.bfloat16)


def x_extent(devices):
    coords = [getattr(d, "coords", None) for d in devices.flat]
    if all(c is not None for c in coords):
        return len({c[0] for c in coords})
    return int(round(np.sqrt(devices.shape[1])))


def solution(mesh):
    devices = mesh.devices
    sect, exp, tp = devices.shape
    ex = x_extent(devices)
    fine = Mesh(devices.reshape(sect, exp // ex, ex, tp), ALL)
    in_specs = (
        P(ALL, None),
        P(ALL, None),
        P(ALL, None),
        P(EXPERT_AXES + PLANE_AXES[:1], None, "tp"),
        P(EXPERT_AXES + PLANE_AXES[:1], None, "tp"),
        P(EXPERT_AXES + PLANE_AXES[:1], "tp", None),
    )
    out_specs = P(ALL, None)
    return jax.shard_map(
        per_device, mesh=fine, in_specs=in_specs, out_specs=out_specs, check_vma=False
    )
```

```python
import functools

import jax
import jax.numpy as jnp
import numpy as np
from jax import lax
from jax.experimental import pallas as pl
from jax.experimental.pallas import tpu as pltpu
from jax.sharding import Mesh
from jax.sharding import PartitionSpec as P

MESH_ID = pl.DeviceIdType.MESH


def rs_kernel(
    nsect, ny, rows_ref, wg_hbm, wu_hbm, wd_hbm, out_ref,
    wg, wu, wd, hid, stage, fin, s1, s2, wsem, send1, recv1, send2, recv2, local_sem, ret_send, ret_recv,
):
    nx, nz, rows, width = rows_ref.shape
    hidden_width = wd.shape[0]
    quarter = width // 4
    groups = nsect * ny
    slots = rows // groups
    c = lax.axis_index("sect")
    y = lax.axis_index("ey")
    mx = lax.axis_index("ex")
    mz = lax.axis_index("tp")

    weight_copies = [
        pltpu.make_async_copy(src, dst, wsem.at[i])
        for i, (src, dst) in enumerate(((wg_hbm, wg), (wu_hbm, wu), (wd_hbm, wd)))
    ]
    for cp in weight_copies:
        cp.start()

    def dev(axis, d):
        if axis == "z":
            return (c, y, mx, lax.rem(mz + d + nz, nz))
        return (c, y, lax.rem(mx + d + nx, nx), mz)

    me_group = c * ny + y

    def peer(o):
        g = lax.rem(me_group + o, groups)
        return (g // ny, lax.rem(g, ny), mx, mz)

    barrier = pltpu.get_barrier_semaphore()
    for axis in ("x", "z"):
        for d in (1, -1):
            pl.semaphore_signal(barrier, inc=1, device_id=dev(axis, d), device_id_type=MESH_ID)
    for o in range(1, groups):
        pl.semaphore_signal(barrier, inc=1, device_id=peer(o), device_id_type=MESH_ID)
    pl.semaphore_wait(barrier, 4 + groups - 1)

    weight_copies[0].wait()
    weight_copies[1].wait()

    def hidden_group(i, carry):
        block = rows_ref[i].reshape(nz * rows, width)
        gate = jnp.dot(block, wg[...], preferred_element_type=jnp.float32)
        up = jnp.dot(block, wu[...], preferred_element_type=jnp.float32)
        act = (jax.nn.silu(gate) * up).astype(hid.dtype)
        hid[i] = act.reshape(nz, rows, hidden_width)
        return carry

    lax.fori_loop(0, nx, hidden_group, 0)
    weight_copies[2].wait()

    rings = [("z", 1), ("z", -1), ("x", 1), ("x", -1)]

    def me_on(axis):
        return mz if axis == "z" else mx

    def cols(r):
        return pl.ds(r * quarter, quarter)

    def chunk(r, j):
        if rings[r][0] == "z":
            h = hid[:, j]
        else:
            h = hid[j]
        lead = h.shape[0]
        part = jnp.dot(
            h.reshape(lead * rows, hidden_width), wd[:, cols(r)], preferred_element_type=jnp.float32
        )
        return part.reshape(lead, rows, quarter)

    def other(axis):
        return "x" if axis == "z" else "z"

    n1 = nz
    copies1 = {}
    for s in range(n1 - 1):
        for r in range(4):
            axis, d = rings[r][0], rings[r][1]
            j = lax.rem(me_on(axis) + n1 * (s + 2) - d * (s + 1), n1)
            if s == 0:
                stage[r] = chunk(r, j)
                src = stage.at[r]
            else:
                part = chunk(r, j)
                copies1[(r, s - 1)].wait_recv()
                s1[r, s - 1] = s1[r, s - 1] + part
                src = s1.at[r, s - 1]
            cp = pltpu.make_async_remote_copy(
                src_ref=src,
                dst_ref=s1.at[r, s],
                send_sem=send1.at[r, s],
                recv_sem=recv1.at[r, s],
                device_id=dev(axis, d),
                device_id_type=MESH_ID,
            )
            cp.start()
            copies1[(r, s)] = cp
    for r in range(4):
        part = chunk(r, me_on(rings[r][0]))
        copies1[(r, n1 - 2)].wait_recv()
        s1[r, n1 - 2] = s1[r, n1 - 2] + part

    n2 = nx
    copies2 = {}
    for s in range(n2 - 1):
        for r in range(4):
            axis, d = other(rings[r][0]), rings[r][1]
            j = lax.rem(me_on(axis) + n2 * (s + 2) - d * (s + 1), n2)
            if s == 0:
                src = s1.at[r, n1 - 2, j]
            else:
                copies2[(r, s - 1)].wait_recv()
                s2[r, s - 1] += s1[r, n1 - 2, j]
                src = s2.at[r, s - 1]
            cp = pltpu.make_async_remote_copy(
                src_ref=src,
                dst_ref=s2.at[r, s],
                send_sem=send2.at[r, s],
                recv_sem=recv2.at[r, s],
                device_id=dev(axis, d),
                device_id_type=MESH_ID,
            )
            cp.start()
            copies2[(r, s)] = cp
    for r in range(4):
        copies2[(r, n2 - 2)].wait_recv()
        axis = other(rings[r][0])
        fin[:, cols(r)] = s2[r, n2 - 2] + s1[r, n1 - 2, me_on(axis)]

    mine = pl.ds(pl.multiple_of(me_group * slots, slots), slots)
    local = pltpu.make_async_copy(fin.at[mine], out_ref.at[mine], local_sem)
    local.start()
    returns = []
    for o in range(1, groups):
        g = lax.rem(me_group + o, groups)
        cp = pltpu.make_async_remote_copy(
            src_ref=fin.at[pl.ds(pl.multiple_of(g * slots, slots), slots)],
            dst_ref=out_ref.at[mine],
            send_sem=ret_send.at[o],
            recv_sem=ret_recv.at[o],
            device_id=peer(o),
            device_id_type=MESH_ID,
        )
        cp.start()
        returns.append(cp)
    local.wait()
    for cp in returns:
        cp.wait_recv()
    for cp in list(copies1.values()) + list(copies2.values()) + returns:
        cp.wait_send()


def expert_reduce_scatter(expert_rows, w_gate, w_up, w_down, nsect, ny):
    nx, nz, rows, width = expert_rows.shape
    hidden_width = w_down.shape[0]
    quarter = width // 4
    groups = nsect * ny
    return pl.pallas_call(
        functools.partial(rs_kernel, nsect, ny),
        out_shape=jax.ShapeDtypeStruct((rows, width), jnp.float32),
        in_specs=[
            pl.BlockSpec(memory_space=pltpu.VMEM),
            pl.BlockSpec(memory_space=pl.ANY),
            pl.BlockSpec(memory_space=pl.ANY),
            pl.BlockSpec(memory_space=pl.ANY),
        ],
        out_specs=pl.BlockSpec(memory_space=pltpu.VMEM),
        scratch_shapes=[
            pltpu.VMEM(w_gate.shape, w_gate.dtype),
            pltpu.VMEM(w_up.shape, w_up.dtype),
            pltpu.VMEM(w_down.shape, w_down.dtype),
            pltpu.VMEM((nx, nz, rows, hidden_width), jnp.bfloat16),
            pltpu.VMEM((4, nx, rows, quarter), jnp.float32),
            pltpu.VMEM((rows, width), jnp.float32),
            pltpu.VMEM((4, nz - 1, nx, rows, quarter), jnp.float32),
            pltpu.VMEM((4, nx - 1, rows, quarter), jnp.float32),
            pltpu.SemaphoreType.DMA((3,)),
            pltpu.SemaphoreType.DMA((4, nz - 1)),
            pltpu.SemaphoreType.DMA((4, nz - 1)),
            pltpu.SemaphoreType.DMA((4, nx - 1)),
            pltpu.SemaphoreType.DMA((4, nx - 1)),
            pltpu.SemaphoreType.DMA(()),
            pltpu.SemaphoreType.DMA((groups,)),
            pltpu.SemaphoreType.DMA((groups,)),
        ],
        compiler_params=pltpu.CompilerParams(
            collective_id=0, has_side_effects=True, vmem_limit_bytes=64 * 1024 * 1024
        ),
    )(expert_rows, w_gate, w_up, w_down)


def ag_kernel(in_ref, out_ref, local_sem, send1, recv1, send2, recv2):
    nx, nz, rows, width = out_ref.shape
    quarter = width // 4
    c = lax.axis_index("sect")
    y = lax.axis_index("ey")
    mx = lax.axis_index("ex")
    mz = lax.axis_index("tp")

    def dev(axis, d):
        if axis == "z":
            return (c, y, mx, lax.rem(mz + d + nz, nz))
        return (c, y, lax.rem(mx + d + nx, nx), mz)

    barrier = pltpu.get_barrier_semaphore()
    for axis in ("x", "z"):
        for d in (1, -1):
            pl.semaphore_signal(barrier, inc=1, device_id=dev(axis, d), device_id_type=MESH_ID)
    pl.semaphore_wait(barrier, 4)

    local = pltpu.make_async_copy(in_ref, out_ref.at[mx, mz], local_sem)
    local.start()

    rings = [("z", 1), ("z", -1), ("x", 1), ("x", -1)]

    def cols(r):
        return pl.ds(r * quarter, quarter)

    def block(axis, r, k):
        if axis == "z":
            return out_ref.at[mx, k, :, cols(r)]
        return out_ref.at[k, mz, :, cols(r)]

    def plane_block(axis, r, k):
        if axis == "x":
            return out_ref.at[k, :, :, cols(r)]
        return out_ref.at[:, k, :, cols(r)]

    def me_on(axis):
        return mz if axis == "z" else mx

    def ring_phase(axis_of, view, first_src, send, recv, sizes):
        copies = {}
        n = sizes
        for s in range(n - 1):
            for r in range(4):
                axis, d = axis_of(r), rings[r][1]
                me = me_on(axis)
                k = lax.rem(me + n * (s + 1) - d * s, n)
                if s == 0:
                    src = first_src(r)
                else:
                    copies[(r, s - 1)].wait_recv()
                    src = view(axis, r, k)
                cp = pltpu.make_async_remote_copy(
                    src_ref=src,
                    dst_ref=view(axis, r, k),
                    send_sem=send.at[r, s],
                    recv_sem=recv.at[r, s],
                    device_id=dev(axis, d),
                    device_id_type=MESH_ID,
                )
                cp.start()
                copies[(r, s)] = cp
        for r in range(4):
            copies[(r, n - 2)].wait_recv()
        return copies

    copies1 = ring_phase(
        lambda r: rings[r][0], block, lambda r: in_ref.at[:, cols(r)], send1, recv1, nz
    )
    local.wait()

    def second(r):
        return "x" if rings[r][0] == "z" else "z"

    copies2 = ring_phase(
        second,
        plane_block,
        lambda r: plane_block(second(r), r, me_on(second(r))),
        send2,
        recv2,
        nx,
    )
    for cp in list(copies1.values()) + list(copies2.values()):
        cp.wait_send()


def plane_all_gather(rows_block, nx, nz):
    rows, width = rows_block.shape
    return pl.pallas_call(
        ag_kernel,
        out_shape=jax.ShapeDtypeStruct((nx, nz, rows, width), rows_block.dtype),
        in_specs=[pl.BlockSpec(memory_space=pltpu.VMEM)],
        out_specs=pl.BlockSpec(memory_space=pltpu.VMEM),
        scratch_shapes=[
            pltpu.SemaphoreType.DMA(()),
            pltpu.SemaphoreType.DMA((4, nz - 1)),
            pltpu.SemaphoreType.DMA((4, nz - 1)),
            pltpu.SemaphoreType.DMA((4, nx - 1)),
            pltpu.SemaphoreType.DMA((4, nx - 1)),
        ],
        compiler_params=pltpu.CompilerParams(
            collective_id=1, has_side_effects=True, vmem_limit_bytes=60 * 1024 * 1024
        ),
    )(rows_block)


ALL = ("sect", "ey", "ex", "tp")
EXPERT_AXES = ("sect", "ey")
PLANE_AXES = ("ex", "tp")


def place_slots(ids_block, experts):
    flat_ids = ids_block.reshape(-1)
    hits_mask = (flat_ids[:, None] == jnp.arange(experts, dtype=jnp.int32)[None, :]).astype(
        jnp.int32
    )
    earlier = jnp.cumsum(hits_mask, axis=0) - hits_mask
    slot_rank = jnp.sum(earlier * hits_mask, axis=1)
    return (flat_ids, slot_rank)


def per_device(tokens, router_logits, expert_ids, w_gate, w_up, w_down):
    experts_all = lax.axis_size(EXPERT_AXES)
    plane_count = lax.axis_size(PLANE_AXES)
    token_count = tokens.shape[0]
    capacity = min(token_count, 4 * token_count // experts_all)
    model_width = tokens.shape[1]
    flat_ids, slot_rank = place_slots(expert_ids, experts_all)
    columns = flat_ids * capacity + slot_rank
    positions = jnp.arange(experts_all * capacity, dtype=jnp.int32)
    picker = (positions[:, None] == columns[None, :]).astype(jnp.bfloat16)
    repeated = jnp.repeat(tokens, 2, axis=0)
    slab = jnp.dot(picker, repeated, preferred_element_type=jnp.float32).astype(jnp.bfloat16)
    slab = slab.reshape(experts_all, capacity, model_width)
    column_rows = lax.all_to_all(slab, EXPERT_AXES, split_axis=0, concat_axis=0, tiled=True)
    nx = lax.axis_size("ex")
    plane_rows = plane_all_gather(
        column_rows.reshape(experts_all * capacity, model_width), nx, plane_count // nx
    )
    expert_out = expert_reduce_scatter(
        plane_rows, w_gate[0], w_up[0], w_down[0], lax.axis_size("sect"), lax.axis_size("ey")
    )
    weights = jax.nn.sigmoid(router_logits - router_logits[:, ::-1]).reshape(-1)
    picked = jnp.take(expert_out, columns, axis=0) * weights[:, None]
    mixture = jnp.sum(picked.reshape(token_count, 2, model_width), axis=1)
    return mixture.astype(jnp.bfloat16)


def x_extent(devices):
    coords = [getattr(d, "coords", None) for d in devices.flat]
    if all(c is not None for c in coords):
        return len({c[0] for c in coords})
    return int(round(np.sqrt(devices.shape[1])))


def solution(mesh):
    devices = mesh.devices
    sect, exp, tp = devices.shape
    ex = x_extent(devices)
    fine = Mesh(devices.reshape(sect, exp // ex, ex, tp), ALL)
    in_specs = (
        P(ALL, None),
        P(ALL, None),
        P(ALL, None),
        P(EXPERT_AXES + PLANE_AXES[:1], None, "tp"),
        P(EXPERT_AXES + PLANE_AXES[:1], None, "tp"),
        P(EXPERT_AXES + PLANE_AXES[:1], "tp", None),
    )
    out_specs = P(ALL, None)
    return jax.shard_map(
        per_device, mesh=fine, in_specs=in_specs, out_specs=out_specs, check_vma=False
    )
```

```python
import functools

import jax
import jax.numpy as jnp
import numpy as np
from jax import lax
from jax.experimental import pallas as pl
from jax.experimental.pallas import tpu as pltpu
from jax.sharding import Mesh
from jax.sharding import PartitionSpec as P

MESH_ID = pl.DeviceIdType.MESH


def rs_kernel(
    nsect, ny, rows_ref, wg_hbm, wu_hbm, wd_hbm, out_ref,
    wg, wu, wd, hid, stage, fin, s1, total1, s2, wsem, send1, recv1, send2, recv2, local_sem, ret_send, ret_recv,
):
    nx, nz, rows, width = rows_ref.shape
    hidden_width = wd.shape[0]
    quarter = width // 4
    groups = nsect * ny
    slots = rows // groups
    c = lax.axis_index("sect")
    y = lax.axis_index("ey")
    mx = lax.axis_index("ex")
    mz = lax.axis_index("tp")

    weight_copies = [
        pltpu.make_async_copy(src, dst, wsem.at[i])
        for i, (src, dst) in enumerate(((wg_hbm, wg), (wu_hbm, wu), (wd_hbm, wd)))
    ]
    for cp in weight_copies:
        cp.start()

    def dev(axis, d):
        if axis == "z":
            return (c, y, mx, lax.rem(mz + d + nz, nz))
        return (c, y, lax.rem(mx + d + nx, nx), mz)

    me_group = c * ny + y

    def peer(o):
        g = lax.rem(me_group + o, groups)
        return (g // ny, lax.rem(g, ny), mx, mz)

    barrier = pltpu.get_barrier_semaphore()
    for axis in ("x", "z"):
        for d in (1, -1):
            pl.semaphore_signal(barrier, inc=1, device_id=dev(axis, d), device_id_type=MESH_ID)
    for o in range(1, groups):
        pl.semaphore_signal(barrier, inc=1, device_id=peer(o), device_id_type=MESH_ID)
    pl.semaphore_wait(barrier, 4 + groups - 1)

    weight_copies[0].wait()
    weight_copies[1].wait()

    def hidden_group(i, carry):
        block = rows_ref[i].reshape(nz * rows, width)
        gate = jnp.dot(block, wg[...], preferred_element_type=jnp.float32)
        up = jnp.dot(block, wu[...], preferred_element_type=jnp.float32)
        act = (jax.nn.silu(gate) * up).astype(hid.dtype)
        hid[i] = act.reshape(nz, rows, hidden_width)
        return carry

    lax.fori_loop(0, nx, hidden_group, 0)
    weight_copies[2].wait()

    rings = [("z", 1), ("z", -1), ("x", 1), ("x", -1)]

    def me_on(axis):
        return mz if axis == "z" else mx

    def cols(r):
        return pl.ds(r * quarter, quarter)

    def chunk(r, j):
        if rings[r][0] == "z":
            h = hid[:, j]
        else:
            h = hid[j]
        lead = h.shape[0]
        part = jnp.dot(
            h.reshape(lead * rows, hidden_width), wd[:, cols(r)], preferred_element_type=jnp.float32
        )
        return part.reshape(lead, rows, quarter)

    def other(axis):
        return "x" if axis == "z" else "z"

    n1 = nz
    copies1 = {}
    for s in range(n1 - 1):
        for r in range(4):
            axis, d = rings[r][0], rings[r][1]
            j = lax.rem(me_on(axis) + n1 * (s + 2) - d * (s + 1), n1)
            if s == 0:
                stage[r] = chunk(r, j).astype(stage.dtype)
                src = stage.at[r]
            else:
                part = chunk(r, j)
                copies1[(r, s - 1)].wait_recv()
                s1[r, s - 1] = (s1[r, s - 1].astype(jnp.float32) + part).astype(s1.dtype)
                src = s1.at[r, s - 1]
            cp = pltpu.make_async_remote_copy(
                src_ref=src,
                dst_ref=s1.at[r, s],
                send_sem=send1.at[r, s],
                recv_sem=recv1.at[r, s],
                device_id=dev(axis, d),
                device_id_type=MESH_ID,
            )
            cp.start()
            copies1[(r, s)] = cp
    for r in range(4):
        part = chunk(r, me_on(rings[r][0]))
        copies1[(r, n1 - 2)].wait_recv()
        total1[r] = s1[r, n1 - 2].astype(jnp.float32) + part

    n2 = nx
    copies2 = {}
    for s in range(n2 - 1):
        for r in range(4):
            axis, d = other(rings[r][0]), rings[r][1]
            j = lax.rem(me_on(axis) + n2 * (s + 2) - d * (s + 1), n2)
            if s == 0:
                src = total1.at[r, j]
            else:
                copies2[(r, s - 1)].wait_recv()
                s2[r, s - 1] += total1[r, j]
                src = s2.at[r, s - 1]
            cp = pltpu.make_async_remote_copy(
                src_ref=src,
                dst_ref=s2.at[r, s],
                send_sem=send2.at[r, s],
                recv_sem=recv2.at[r, s],
                device_id=dev(axis, d),
                device_id_type=MESH_ID,
            )
            cp.start()
            copies2[(r, s)] = cp
    for r in range(4):
        copies2[(r, n2 - 2)].wait_recv()
        axis = other(rings[r][0])
        fin[:, cols(r)] = s2[r, n2 - 2] + total1[r, me_on(axis)]

    mine = pl.ds(pl.multiple_of(me_group * slots, slots), slots)
    local = pltpu.make_async_copy(fin.at[mine], out_ref.at[mine], local_sem)
    local.start()
    returns = []
    for o in range(1, groups):
        g = lax.rem(me_group + o, groups)
        cp = pltpu.make_async_remote_copy(
            src_ref=fin.at[pl.ds(pl.multiple_of(g * slots, slots), slots)],
            dst_ref=out_ref.at[mine],
            send_sem=ret_send.at[o],
            recv_sem=ret_recv.at[o],
            device_id=peer(o),
            device_id_type=MESH_ID,
        )
        cp.start()
        returns.append(cp)
    local.wait()
    for cp in returns:
        cp.wait_recv()
    for cp in list(copies1.values()) + list(copies2.values()) + returns:
        cp.wait_send()


def expert_reduce_scatter(expert_rows, w_gate, w_up, w_down, nsect, ny):
    nx, nz, rows, width = expert_rows.shape
    hidden_width = w_down.shape[0]
    quarter = width // 4
    groups = nsect * ny
    return pl.pallas_call(
        functools.partial(rs_kernel, nsect, ny),
        out_shape=jax.ShapeDtypeStruct((rows, width), jnp.float32),
        in_specs=[
            pl.BlockSpec(memory_space=pltpu.VMEM),
            pl.BlockSpec(memory_space=pl.ANY),
            pl.BlockSpec(memory_space=pl.ANY),
            pl.BlockSpec(memory_space=pl.ANY),
        ],
        out_specs=pl.BlockSpec(memory_space=pltpu.VMEM),
        scratch_shapes=[
            pltpu.VMEM(w_gate.shape, w_gate.dtype),
            pltpu.VMEM(w_up.shape, w_up.dtype),
            pltpu.VMEM(w_down.shape, w_down.dtype),
            pltpu.VMEM((nx, nz, rows, hidden_width), jnp.bfloat16),
            pltpu.VMEM((4, nx, rows, quarter), jnp.bfloat16),
            pltpu.VMEM((rows, width), jnp.float32),
            pltpu.VMEM((4, nz - 1, nx, rows, quarter), jnp.bfloat16),
            pltpu.VMEM((4, nx, rows, quarter), jnp.float32),
            pltpu.VMEM((4, nx - 1, rows, quarter), jnp.float32),
            pltpu.SemaphoreType.DMA((3,)),
            pltpu.SemaphoreType.DMA((4, nz - 1)),
            pltpu.SemaphoreType.DMA((4, nz - 1)),
            pltpu.SemaphoreType.DMA((4, nx - 1)),
            pltpu.SemaphoreType.DMA((4, nx - 1)),
            pltpu.SemaphoreType.DMA(()),
            pltpu.SemaphoreType.DMA((groups,)),
            pltpu.SemaphoreType.DMA((groups,)),
        ],
        compiler_params=pltpu.CompilerParams(
            collective_id=0, has_side_effects=True, vmem_limit_bytes=64 * 1024 * 1024
        ),
    )(expert_rows, w_gate, w_up, w_down)


def ag_kernel(in_ref, out_ref, local_sem, send1, recv1, send2, recv2):
    nx, nz, rows, width = out_ref.shape
    quarter = width // 4
    c = lax.axis_index("sect")
    y = lax.axis_index("ey")
    mx = lax.axis_index("ex")
    mz = lax.axis_index("tp")

    def dev(axis, d):
        if axis == "z":
            return (c, y, mx, lax.rem(mz + d + nz, nz))
        return (c, y, lax.rem(mx + d + nx, nx), mz)

    barrier = pltpu.get_barrier_semaphore()
    for axis in ("x", "z"):
        for d in (1, -1):
            pl.semaphore_signal(barrier, inc=1, device_id=dev(axis, d), device_id_type=MESH_ID)
    pl.semaphore_wait(barrier, 4)

    local = pltpu.make_async_copy(in_ref, out_ref.at[mx, mz], local_sem)
    local.start()

    rings = [("z", 1), ("z", -1), ("x", 1), ("x", -1)]

    def cols(r):
        return pl.ds(r * quarter, quarter)

    def block(axis, r, k):
        if axis == "z":
            return out_ref.at[mx, k, :, cols(r)]
        return out_ref.at[k, mz, :, cols(r)]

    def plane_block(axis, r, k):
        if axis == "x":
            return out_ref.at[k, :, :, cols(r)]
        return out_ref.at[:, k, :, cols(r)]

    def me_on(axis):
        return mz if axis == "z" else mx

    def ring_phase(axis_of, view, first_src, send, recv, sizes):
        copies = {}
        n = sizes
        for s in range(n - 1):
            for r in range(4):
                axis, d = axis_of(r), rings[r][1]
                me = me_on(axis)
                k = lax.rem(me + n * (s + 1) - d * s, n)
                if s == 0:
                    src = first_src(r)
                else:
                    copies[(r, s - 1)].wait_recv()
                    src = view(axis, r, k)
                cp = pltpu.make_async_remote_copy(
                    src_ref=src,
                    dst_ref=view(axis, r, k),
                    send_sem=send.at[r, s],
                    recv_sem=recv.at[r, s],
                    device_id=dev(axis, d),
                    device_id_type=MESH_ID,
                )
                cp.start()
                copies[(r, s)] = cp
        for r in range(4):
            copies[(r, n - 2)].wait_recv()
        return copies

    copies1 = ring_phase(
        lambda r: rings[r][0], block, lambda r: in_ref.at[:, cols(r)], send1, recv1, nz
    )
    local.wait()

    def second(r):
        return "x" if rings[r][0] == "z" else "z"

    copies2 = ring_phase(
        second,
        plane_block,
        lambda r: plane_block(second(r), r, me_on(second(r))),
        send2,
        recv2,
        nx,
    )
    for cp in list(copies1.values()) + list(copies2.values()):
        cp.wait_send()


def plane_all_gather(rows_block, nx, nz):
    rows, width = rows_block.shape
    return pl.pallas_call(
        ag_kernel,
        out_shape=jax.ShapeDtypeStruct((nx, nz, rows, width), rows_block.dtype),
        in_specs=[pl.BlockSpec(memory_space=pltpu.VMEM)],
        out_specs=pl.BlockSpec(memory_space=pltpu.VMEM),
        scratch_shapes=[
            pltpu.SemaphoreType.DMA(()),
            pltpu.SemaphoreType.DMA((4, nz - 1)),
            pltpu.SemaphoreType.DMA((4, nz - 1)),
            pltpu.SemaphoreType.DMA((4, nx - 1)),
            pltpu.SemaphoreType.DMA((4, nx - 1)),
        ],
        compiler_params=pltpu.CompilerParams(
            collective_id=1, has_side_effects=True, vmem_limit_bytes=60 * 1024 * 1024
        ),
    )(rows_block)


ALL = ("sect", "ey", "ex", "tp")
EXPERT_AXES = ("sect", "ey")
PLANE_AXES = ("ex", "tp")


def place_slots(ids_block, experts):
    flat_ids = ids_block.reshape(-1)
    hits_mask = (flat_ids[:, None] == jnp.arange(experts, dtype=jnp.int32)[None, :]).astype(
        jnp.int32
    )
    earlier = jnp.cumsum(hits_mask, axis=0) - hits_mask
    slot_rank = jnp.sum(earlier * hits_mask, axis=1)
    return (flat_ids, slot_rank)


def per_device(tokens, router_logits, expert_ids, w_gate, w_up, w_down):
    experts_all = lax.axis_size(EXPERT_AXES)
    plane_count = lax.axis_size(PLANE_AXES)
    token_count = tokens.shape[0]
    capacity = min(token_count, 4 * token_count // experts_all)
    model_width = tokens.shape[1]
    flat_ids, slot_rank = place_slots(expert_ids, experts_all)
    columns = flat_ids * capacity + slot_rank
    positions = jnp.arange(experts_all * capacity, dtype=jnp.int32)
    picker = (positions[:, None] == columns[None, :]).astype(jnp.bfloat16)
    repeated = jnp.repeat(tokens, 2, axis=0)
    slab = jnp.dot(picker, repeated, preferred_element_type=jnp.float32).astype(jnp.bfloat16)
    slab = slab.reshape(experts_all, capacity, model_width)
    column_rows = lax.all_to_all(slab, EXPERT_AXES, split_axis=0, concat_axis=0, tiled=True)
    nx = lax.axis_size("ex")
    plane_rows = plane_all_gather(
        column_rows.reshape(experts_all * capacity, model_width), nx, plane_count // nx
    )
    expert_out = expert_reduce_scatter(
        plane_rows, w_gate[0], w_up[0], w_down[0], lax.axis_size("sect"), lax.axis_size("ey")
    )
    weights = jax.nn.sigmoid(router_logits - router_logits[:, ::-1]).reshape(-1)
    picked = jnp.take(expert_out, columns, axis=0) * weights[:, None]
    mixture = jnp.sum(picked.reshape(token_count, 2, model_width), axis=1)
    return mixture.astype(jnp.bfloat16)


def x_extent(devices):
    coords = [getattr(d, "coords", None) for d in devices.flat]
    if all(c is not None for c in coords):
        return len({c[0] for c in coords})
    return int(round(np.sqrt(devices.shape[1])))


def solution(mesh):
    devices = mesh.devices
    sect, exp, tp = devices.shape
    ex = x_extent(devices)
    fine = Mesh(devices.reshape(sect, exp // ex, ex, tp), ALL)
    in_specs = (
        P(ALL, None),
        P(ALL, None),
        P(ALL, None),
        P(EXPERT_AXES + PLANE_AXES[:1], None, "tp"),
        P(EXPERT_AXES + PLANE_AXES[:1], None, "tp"),
        P(EXPERT_AXES + PLANE_AXES[:1], "tp", None),
    )
    out_specs = P(ALL, None)
    return jax.shard_map(
        per_device, mesh=fine, in_specs=in_specs, out_specs=out_specs, check_vma=False
    )
```

```python
import functools

import jax
import jax.numpy as jnp
import numpy as np
from jax import lax
from jax.experimental import pallas as pl
from jax.experimental.pallas import tpu as pltpu
from jax.sharding import Mesh
from jax.sharding import PartitionSpec as P

MESH_ID = pl.DeviceIdType.MESH


def rs_kernel(
    nsect, ny, rows_ref, wg_hbm, wu_hbm, wd_hbm, out_ref,
    wg, wu, wd, hid, stage, fin, s1, total1, s2, wsem, send1, recv1, send2, recv2, local_sem, ret_send, ret_recv,
):
    nx, nz, rows, width = rows_ref.shape
    hidden_width = wd.shape[0]
    quarter = width // 4
    groups = nsect * ny
    slots = rows // groups
    c = lax.axis_index("sect")
    y = lax.axis_index("ey")
    mx = lax.axis_index("ex")
    mz = lax.axis_index("tp")

    weight_copies = [
        pltpu.make_async_copy(src, dst, wsem.at[i])
        for i, (src, dst) in enumerate(((wg_hbm, wg), (wu_hbm, wu), (wd_hbm, wd)))
    ]
    for cp in weight_copies:
        cp.start()

    def dev(axis, d):
        if axis == "z":
            return (c, y, mx, lax.rem(mz + d + nz, nz))
        return (c, y, lax.rem(mx + d + nx, nx), mz)

    me_group = c * ny + y

    def peer(o):
        g = lax.rem(me_group + o, groups)
        return (g // ny, lax.rem(g, ny), mx, mz)

    barrier = pltpu.get_barrier_semaphore()
    for axis in ("x", "z"):
        for d in (1, -1):
            pl.semaphore_signal(barrier, inc=1, device_id=dev(axis, d), device_id_type=MESH_ID)
    for o in range(1, groups):
        pl.semaphore_signal(barrier, inc=1, device_id=peer(o), device_id_type=MESH_ID)
    pl.semaphore_wait(barrier, 4 + groups - 1)

    weight_copies[0].wait()
    weight_copies[1].wait()

    def hidden_group(i, carry):
        block = rows_ref[i].reshape(nz * rows, width)
        gate = jnp.dot(block, wg[...], preferred_element_type=jnp.float32)
        up = jnp.dot(block, wu[...], preferred_element_type=jnp.float32)
        act = (jax.nn.silu(gate) * up).astype(hid.dtype)
        hid[i] = act.reshape(nz, rows, hidden_width)
        return carry

    lax.fori_loop(0, nx, hidden_group, 0)
    weight_copies[2].wait()

    rings = [("z", 1), ("z", -1), ("x", 1), ("x", -1)]

    def me_on(axis):
        return mz if axis == "z" else mx

    def cols(r):
        return pl.ds(r * quarter, quarter)

    def chunk(r, j):
        if rings[r][0] == "z":
            h = hid[:, j]
        else:
            h = hid[j]
        lead = h.shape[0]
        part = jnp.dot(
            h.reshape(lead * rows, hidden_width), wd[:, cols(r)], preferred_element_type=jnp.float32
        )
        return part.reshape(lead, rows, quarter)

    def other(axis):
        return "x" if axis == "z" else "z"

    n1 = nz
    copies1 = {}
    for s in range(n1 - 1):
        for r in range(4):
            axis, d = rings[r][0], rings[r][1]
            j = lax.rem(me_on(axis) + n1 * (s + 2) - d * (s + 1), n1)
            if s == 0:
                stage[r] = chunk(r, j).astype(stage.dtype)
                src = stage.at[r]
            else:
                part = chunk(r, j)
                copies1[(r, s - 1)].wait_recv()
                s1[r, s - 1] = (s1[r, s - 1].astype(jnp.float32) + part).astype(s1.dtype)
                src = s1.at[r, s - 1]
            cp = pltpu.make_async_remote_copy(
                src_ref=src,
                dst_ref=s1.at[r, s],
                send_sem=send1.at[r, s],
                recv_sem=recv1.at[r, s],
                device_id=dev(axis, d),
                device_id_type=MESH_ID,
            )
            cp.start()
            copies1[(r, s)] = cp
    for r in range(4):
        part = chunk(r, me_on(rings[r][0]))
        copies1[(r, n1 - 2)].wait_recv()
        total1[r] = s1[r, n1 - 2].astype(jnp.float32) + part

    n2 = nx
    copies2 = {}
    for s in range(n2 - 1):
        for r in range(4):
            axis, d = other(rings[r][0]), rings[r][1]
            j = lax.rem(me_on(axis) + n2 * (s + 2) - d * (s + 1), n2)
            if s == 0:
                src = total1.at[r, j]
            else:
                copies2[(r, s - 1)].wait_recv()
                s2[r, s - 1] += total1[r, j]
                src = s2.at[r, s - 1]
            cp = pltpu.make_async_remote_copy(
                src_ref=src,
                dst_ref=s2.at[r, s],
                send_sem=send2.at[r, s],
                recv_sem=recv2.at[r, s],
                device_id=dev(axis, d),
                device_id_type=MESH_ID,
            )
            cp.start()
            copies2[(r, s)] = cp
    for r in range(4):
        copies2[(r, n2 - 2)].wait_recv()
        axis = other(rings[r][0])
        fin[:, cols(r)] = s2[r, n2 - 2] + total1[r, me_on(axis)]

    mine = pl.ds(pl.multiple_of(me_group * slots, slots), slots)
    local = pltpu.make_async_copy(fin.at[mine], out_ref.at[mine], local_sem)
    local.start()
    returns = []
    for o in range(1, groups):
        g = lax.rem(me_group + o, groups)
        cp = pltpu.make_async_remote_copy(
            src_ref=fin.at[pl.ds(pl.multiple_of(g * slots, slots), slots)],
            dst_ref=out_ref.at[mine],
            send_sem=ret_send.at[o],
            recv_sem=ret_recv.at[o],
            device_id=peer(o),
            device_id_type=MESH_ID,
        )
        cp.start()
        returns.append(cp)
    local.wait()
    for cp in returns:
        cp.wait_recv()
    for cp in list(copies1.values()) + list(copies2.values()) + returns:
        cp.wait_send()


def expert_reduce_scatter(expert_rows, w_gate, w_up, w_down, nsect, ny):
    nx, nz, rows, width = expert_rows.shape
    hidden_width = w_down.shape[0]
    quarter = width // 4
    groups = nsect * ny
    return pl.pallas_call(
        functools.partial(rs_kernel, nsect, ny),
        out_shape=jax.ShapeDtypeStruct((rows, width), jnp.float32),
        in_specs=[
            pl.BlockSpec(memory_space=pltpu.VMEM),
            pl.BlockSpec(memory_space=pl.ANY),
            pl.BlockSpec(memory_space=pl.ANY),
            pl.BlockSpec(memory_space=pl.ANY),
        ],
        out_specs=pl.BlockSpec(memory_space=pltpu.VMEM),
        scratch_shapes=[
            pltpu.VMEM(w_gate.shape, w_gate.dtype),
            pltpu.VMEM(w_up.shape, w_up.dtype),
            pltpu.VMEM(w_down.shape, w_down.dtype),
            pltpu.VMEM((nx, nz, rows, hidden_width), jnp.bfloat16),
            pltpu.VMEM((4, nx, rows, quarter), jnp.bfloat16),
            pltpu.VMEM((rows, width), jnp.float32),
            pltpu.VMEM((4, nz - 1, nx, rows, quarter), jnp.bfloat16),
            pltpu.VMEM((4, nx, rows, quarter), jnp.float32),
            pltpu.VMEM((4, nx - 1, rows, quarter), jnp.float32),
            pltpu.SemaphoreType.DMA((3,)),
            pltpu.SemaphoreType.DMA((4, nz - 1)),
            pltpu.SemaphoreType.DMA((4, nz - 1)),
            pltpu.SemaphoreType.DMA((4, nx - 1)),
            pltpu.SemaphoreType.DMA((4, nx - 1)),
            pltpu.SemaphoreType.DMA(()),
            pltpu.SemaphoreType.DMA((groups,)),
            pltpu.SemaphoreType.DMA((groups,)),
        ],
        compiler_params=pltpu.CompilerParams(
            collective_id=0, has_side_effects=True, vmem_limit_bytes=64 * 1024 * 1024
        ),
    )(expert_rows, w_gate, w_up, w_down)


def ag_kernel(nsect, ny, in_ref, out_ref, local_sem, in_send, in_recv, send1, recv1, send2, recv2):
    nx, nz, rows, width = out_ref.shape
    groups = nsect * ny
    slots = rows // groups
    quarter = width // 4
    c = lax.axis_index("sect")
    y = lax.axis_index("ey")
    mx = lax.axis_index("ex")
    mz = lax.axis_index("tp")

    def dev(axis, d):
        if axis == "z":
            return (c, y, mx, lax.rem(mz + d + nz, nz))
        return (c, y, lax.rem(mx + d + nx, nx), mz)

    me_group = c * ny + y

    def peer(o):
        g = lax.rem(me_group + o, groups)
        return (g // ny, lax.rem(g, ny), mx, mz)

    barrier = pltpu.get_barrier_semaphore()
    for axis in ("x", "z"):
        for d in (1, -1):
            pl.semaphore_signal(barrier, inc=1, device_id=dev(axis, d), device_id_type=MESH_ID)
    for o in range(1, groups):
        pl.semaphore_signal(barrier, inc=1, device_id=peer(o), device_id_type=MESH_ID)
    pl.semaphore_wait(barrier, 4 + groups - 1)

    mine = pl.ds(pl.multiple_of(me_group * slots, slots), slots)
    local = pltpu.make_async_copy(in_ref.at[me_group], out_ref.at[mx, mz, mine], local_sem)
    local.start()
    dispatch = []
    for o in range(1, groups):
        cp = pltpu.make_async_remote_copy(
            src_ref=in_ref.at[lax.rem(me_group + o, groups)],
            dst_ref=out_ref.at[mx, mz, mine],
            send_sem=in_send.at[o],
            recv_sem=in_recv.at[o],
            device_id=peer(o),
            device_id_type=MESH_ID,
        )
        cp.start()
        dispatch.append(cp)
    local.wait()
    for cp in dispatch:
        cp.wait_recv()

    rings = [("z", 1), ("z", -1), ("x", 1), ("x", -1)]

    def cols(r):
        return pl.ds(r * quarter, quarter)

    def block(axis, r, k):
        if axis == "z":
            return out_ref.at[mx, k, :, cols(r)]
        return out_ref.at[k, mz, :, cols(r)]

    def plane_block(axis, r, k):
        if axis == "x":
            return out_ref.at[k, :, :, cols(r)]
        return out_ref.at[:, k, :, cols(r)]

    def me_on(axis):
        return mz if axis == "z" else mx

    def ring_phase(axis_of, view, first_src, send, recv, sizes):
        copies = {}
        n = sizes
        for s in range(n - 1):
            for r in range(4):
                axis, d = axis_of(r), rings[r][1]
                me = me_on(axis)
                k = lax.rem(me + n * (s + 1) - d * s, n)
                if s == 0:
                    src = first_src(r)
                else:
                    copies[(r, s - 1)].wait_recv()
                    src = view(axis, r, k)
                cp = pltpu.make_async_remote_copy(
                    src_ref=src,
                    dst_ref=view(axis, r, k),
                    send_sem=send.at[r, s],
                    recv_sem=recv.at[r, s],
                    device_id=dev(axis, d),
                    device_id_type=MESH_ID,
                )
                cp.start()
                copies[(r, s)] = cp
        for r in range(4):
            copies[(r, n - 2)].wait_recv()
        return copies

    copies1 = ring_phase(
        lambda r: rings[r][0], block, lambda r: out_ref.at[mx, mz, :, cols(r)], send1, recv1, nz
    )

    def second(r):
        return "x" if rings[r][0] == "z" else "z"

    copies2 = ring_phase(
        second,
        plane_block,
        lambda r: plane_block(second(r), r, me_on(second(r))),
        send2,
        recv2,
        nx,
    )
    for cp in list(copies1.values()) + list(copies2.values()) + dispatch:
        cp.wait_send()


def plane_all_gather(slab, nx, nz, nsect, ny):
    groups, slots, width = slab.shape
    rows = groups * slots
    return pl.pallas_call(
        functools.partial(ag_kernel, nsect, ny),
        out_shape=jax.ShapeDtypeStruct((nx, nz, rows, width), slab.dtype),
        in_specs=[pl.BlockSpec(memory_space=pltpu.VMEM)],
        out_specs=pl.BlockSpec(memory_space=pltpu.VMEM),
        scratch_shapes=[
            pltpu.SemaphoreType.DMA(()),
            pltpu.SemaphoreType.DMA((groups,)),
            pltpu.SemaphoreType.DMA((groups,)),
            pltpu.SemaphoreType.DMA((4, nz - 1)),
            pltpu.SemaphoreType.DMA((4, nz - 1)),
            pltpu.SemaphoreType.DMA((4, nx - 1)),
            pltpu.SemaphoreType.DMA((4, nx - 1)),
        ],
        compiler_params=pltpu.CompilerParams(
            collective_id=1, has_side_effects=True, vmem_limit_bytes=60 * 1024 * 1024
        ),
    )(slab)


ALL = ("sect", "ey", "ex", "tp")
EXPERT_AXES = ("sect", "ey")
PLANE_AXES = ("ex", "tp")


def place_slots(ids_block, experts):
    flat_ids = ids_block.reshape(-1)
    hits_mask = (flat_ids[:, None] == jnp.arange(experts, dtype=jnp.int32)[None, :]).astype(
        jnp.int32
    )
    earlier = jnp.cumsum(hits_mask, axis=0) - hits_mask
    slot_rank = jnp.sum(earlier * hits_mask, axis=1)
    return (flat_ids, slot_rank)


def per_device(tokens, router_logits, expert_ids, w_gate, w_up, w_down):
    experts_all = lax.axis_size(EXPERT_AXES)
    plane_count = lax.axis_size(PLANE_AXES)
    token_count = tokens.shape[0]
    capacity = min(token_count, 4 * token_count // experts_all)
    model_width = tokens.shape[1]
    flat_ids, slot_rank = place_slots(expert_ids, experts_all)
    columns = flat_ids * capacity + slot_rank
    positions = jnp.arange(experts_all * capacity, dtype=jnp.int32)
    picker = (positions[:, None] == columns[None, :]).astype(jnp.bfloat16)
    repeated = jnp.repeat(tokens, 2, axis=0)
    slab = jnp.dot(picker, repeated, preferred_element_type=jnp.float32).astype(jnp.bfloat16)
    slab = slab.reshape(experts_all, capacity, model_width)
    nx = lax.axis_size("ex")
    plane_rows = plane_all_gather(
        slab, nx, plane_count // nx, lax.axis_size("sect"), lax.axis_size("ey")
    )
    expert_out = expert_reduce_scatter(
        plane_rows, w_gate[0], w_up[0], w_down[0], lax.axis_size("sect"), lax.axis_size("ey")
    )
    weights = jax.nn.sigmoid(router_logits - router_logits[:, ::-1]).reshape(-1)
    picked = jnp.take(expert_out, columns, axis=0) * weights[:, None]
    mixture = jnp.sum(picked.reshape(token_count, 2, model_width), axis=1)
    return mixture.astype(jnp.bfloat16)


def x_extent(devices):
    coords = [getattr(d, "coords", None) for d in devices.flat]
    if all(c is not None for c in coords):
        return len({c[0] for c in coords})
    return int(round(np.sqrt(devices.shape[1])))


def solution(mesh):
    devices = mesh.devices
    sect, exp, tp = devices.shape
    ex = x_extent(devices)
    fine = Mesh(devices.reshape(sect, exp // ex, ex, tp), ALL)
    in_specs = (
        P(ALL, None),
        P(ALL, None),
        P(ALL, None),
        P(EXPERT_AXES + PLANE_AXES[:1], None, "tp"),
        P(EXPERT_AXES + PLANE_AXES[:1], None, "tp"),
        P(EXPERT_AXES + PLANE_AXES[:1], "tp", None),
    )
    out_specs = P(ALL, None)
    return jax.shard_map(
        per_device, mesh=fine, in_specs=in_specs, out_specs=out_specs, check_vma=False
    )
```

```python
import functools

import jax
import jax.numpy as jnp
import numpy as np
from jax import lax
from jax.experimental import pallas as pl
from jax.experimental.pallas import tpu as pltpu
from jax.sharding import Mesh
from jax.sharding import PartitionSpec as P

MESH_ID = pl.DeviceIdType.MESH


def rs_kernel(
    nsect, ny, col_ref, mix_w_ref, rows_ref, wg_hbm, wu_hbm, wd_hbm, mix_ref,
    out_ref, wg, wu, wd, hid, stage, fin, s1, total1, s2, wsem, send1, recv1, send2, recv2, local_sem, ret_send, ret_recv,
):
    nx, nz, rows, width = rows_ref.shape
    hidden_width = wd.shape[0]
    quarter = width // 4
    groups = nsect * ny
    slots = rows // groups
    c = lax.axis_index("sect")
    y = lax.axis_index("ey")
    mx = lax.axis_index("ex")
    mz = lax.axis_index("tp")

    weight_copies = [
        pltpu.make_async_copy(src, dst, wsem.at[i])
        for i, (src, dst) in enumerate(((wg_hbm, wg), (wu_hbm, wu), (wd_hbm, wd)))
    ]
    for cp in weight_copies:
        cp.start()

    def dev(axis, d):
        if axis == "z":
            return (c, y, mx, lax.rem(mz + d + nz, nz))
        return (c, y, lax.rem(mx + d + nx, nx), mz)

    me_group = c * ny + y

    def peer(o):
        g = lax.rem(me_group + o, groups)
        return (g // ny, lax.rem(g, ny), mx, mz)

    barrier = pltpu.get_barrier_semaphore()
    for axis in ("x", "z"):
        for d in (1, -1):
            pl.semaphore_signal(barrier, inc=1, device_id=dev(axis, d), device_id_type=MESH_ID)
    for o in range(1, groups):
        pl.semaphore_signal(barrier, inc=1, device_id=peer(o), device_id_type=MESH_ID)
    pl.semaphore_wait(barrier, 4 + groups - 1)

    weight_copies[0].wait()
    weight_copies[1].wait()

    def hidden_group(i, carry):
        block = rows_ref[i].reshape(nz * rows, width)
        gate = jnp.dot(block, wg[...], preferred_element_type=jnp.float32)
        up = jnp.dot(block, wu[...], preferred_element_type=jnp.float32)
        act = (jax.nn.silu(gate) * up).astype(hid.dtype)
        hid[i] = act.reshape(nz, rows, hidden_width)
        return carry

    lax.fori_loop(0, nx, hidden_group, 0)
    weight_copies[2].wait()

    rings = [("z", 1), ("z", -1), ("x", 1), ("x", -1)]

    def me_on(axis):
        return mz if axis == "z" else mx

    def cols(r):
        return pl.ds(r * quarter, quarter)

    def chunk(r, j):
        if rings[r][0] == "z":
            h = hid[:, j]
        else:
            h = hid[j]
        lead = h.shape[0]
        part = jnp.dot(
            h.reshape(lead * rows, hidden_width), wd[:, cols(r)], preferred_element_type=jnp.float32
        )
        return part.reshape(lead, rows, quarter)

    def other(axis):
        return "x" if axis == "z" else "z"

    n1 = nz
    copies1 = {}
    for s in range(n1 - 1):
        for r in range(4):
            axis, d = rings[r][0], rings[r][1]
            j = lax.rem(me_on(axis) + n1 * (s + 2) - d * (s + 1), n1)
            if s == 0:
                stage[r] = chunk(r, j).astype(stage.dtype)
                src = stage.at[r]
            else:
                part = chunk(r, j)
                copies1[(r, s - 1)].wait_recv()
                s1[r, s - 1] = (s1[r, s - 1].astype(jnp.float32) + part).astype(s1.dtype)
                src = s1.at[r, s - 1]
            cp = pltpu.make_async_remote_copy(
                src_ref=src,
                dst_ref=s1.at[r, s],
                send_sem=send1.at[r, s],
                recv_sem=recv1.at[r, s],
                device_id=dev(axis, d),
                device_id_type=MESH_ID,
            )
            cp.start()
            copies1[(r, s)] = cp
    for r in range(4):
        part = chunk(r, me_on(rings[r][0]))
        copies1[(r, n1 - 2)].wait_recv()
        total1[r] = s1[r, n1 - 2].astype(jnp.float32) + part

    n2 = nx
    copies2 = {}
    for s in range(n2 - 1):
        for r in range(4):
            axis, d = other(rings[r][0]), rings[r][1]
            j = lax.rem(me_on(axis) + n2 * (s + 2) - d * (s + 1), n2)
            if s == 0:
                src = total1.at[r, j]
            else:
                copies2[(r, s - 1)].wait_recv()
                s2[r, s - 1] += total1[r, j]
                src = s2.at[r, s - 1]
            cp = pltpu.make_async_remote_copy(
                src_ref=src,
                dst_ref=s2.at[r, s],
                send_sem=send2.at[r, s],
                recv_sem=recv2.at[r, s],
                device_id=dev(axis, d),
                device_id_type=MESH_ID,
            )
            cp.start()
            copies2[(r, s)] = cp
    for r in range(4):
        copies2[(r, n2 - 2)].wait_recv()
        axis = other(rings[r][0])
        fin[:, cols(r)] = s2[r, n2 - 2] + total1[r, me_on(axis)]

    mine = pl.ds(pl.multiple_of(me_group * slots, slots), slots)
    local = pltpu.make_async_copy(fin.at[mine], out_ref.at[mine], local_sem)
    local.start()
    returns = []
    for o in range(1, groups):
        g = lax.rem(me_group + o, groups)
        cp = pltpu.make_async_remote_copy(
            src_ref=fin.at[pl.ds(pl.multiple_of(g * slots, slots), slots)],
            dst_ref=out_ref.at[mine],
            send_sem=ret_send.at[o],
            recv_sem=ret_recv.at[o],
            device_id=peer(o),
            device_id_type=MESH_ID,
        )
        cp.start()
        returns.append(cp)
    local.wait()
    for cp in returns:
        cp.wait_recv()
    for t in range(mix_ref.shape[0]):
        first = out_ref[pl.ds(col_ref[2 * t], 1), :]
        second = out_ref[pl.ds(col_ref[2 * t + 1], 1), :]
        mix = mix_w_ref[2 * t] * first + mix_w_ref[2 * t + 1] * second
        mix_ref[pl.ds(t, 1), :] = mix.astype(mix_ref.dtype)
    for cp in list(copies1.values()) + list(copies2.values()) + returns:
        cp.wait_send()


def expert_reduce_scatter(columns, mix_w, expert_rows, w_gate, w_up, w_down, nsect, ny):
    nx, nz, rows, width = expert_rows.shape
    hidden_width = w_down.shape[0]
    quarter = width // 4
    groups = nsect * ny
    return pl.pallas_call(
        functools.partial(rs_kernel, nsect, ny),
        out_shape=jax.ShapeDtypeStruct((columns.shape[0] // 2, width), jnp.bfloat16),
        in_specs=[
            pl.BlockSpec(memory_space=pltpu.SMEM),
            pl.BlockSpec(memory_space=pltpu.SMEM),
            pl.BlockSpec(memory_space=pltpu.VMEM),
            pl.BlockSpec(memory_space=pl.ANY),
            pl.BlockSpec(memory_space=pl.ANY),
            pl.BlockSpec(memory_space=pl.ANY),
        ],
        out_specs=pl.BlockSpec(memory_space=pltpu.VMEM),
        scratch_shapes=[
            pltpu.VMEM((rows, width), jnp.float32),
            pltpu.VMEM(w_gate.shape, w_gate.dtype),
            pltpu.VMEM(w_up.shape, w_up.dtype),
            pltpu.VMEM(w_down.shape, w_down.dtype),
            pltpu.VMEM((nx, nz, rows, hidden_width), jnp.bfloat16),
            pltpu.VMEM((4, nx, rows, quarter), jnp.bfloat16),
            pltpu.VMEM((rows, width), jnp.float32),
            pltpu.VMEM((4, nz - 1, nx, rows, quarter), jnp.bfloat16),
            pltpu.VMEM((4, nx, rows, quarter), jnp.float32),
            pltpu.VMEM((4, nx - 1, rows, quarter), jnp.float32),
            pltpu.SemaphoreType.DMA((3,)),
            pltpu.SemaphoreType.DMA((4, nz - 1)),
            pltpu.SemaphoreType.DMA((4, nz - 1)),
            pltpu.SemaphoreType.DMA((4, nx - 1)),
            pltpu.SemaphoreType.DMA((4, nx - 1)),
            pltpu.SemaphoreType.DMA(()),
            pltpu.SemaphoreType.DMA((groups,)),
            pltpu.SemaphoreType.DMA((groups,)),
        ],
        compiler_params=pltpu.CompilerParams(
            collective_id=0, has_side_effects=True, vmem_limit_bytes=64 * 1024 * 1024
        ),
    )(columns, mix_w, expert_rows, w_gate, w_up, w_down)


def ag_kernel(nsect, ny, in_ref, out_ref, local_sem, in_send, in_recv, send1, recv1, send2, recv2):
    nx, nz, rows, width = out_ref.shape
    groups = nsect * ny
    slots = rows // groups
    quarter = width // 4
    c = lax.axis_index("sect")
    y = lax.axis_index("ey")
    mx = lax.axis_index("ex")
    mz = lax.axis_index("tp")

    def dev(axis, d):
        if axis == "z":
            return (c, y, mx, lax.rem(mz + d + nz, nz))
        return (c, y, lax.rem(mx + d + nx, nx), mz)

    me_group = c * ny + y

    def peer(o):
        g = lax.rem(me_group + o, groups)
        return (g // ny, lax.rem(g, ny), mx, mz)

    barrier = pltpu.get_barrier_semaphore()
    for axis in ("x", "z"):
        for d in (1, -1):
            pl.semaphore_signal(barrier, inc=1, device_id=dev(axis, d), device_id_type=MESH_ID)
    for o in range(1, groups):
        pl.semaphore_signal(barrier, inc=1, device_id=peer(o), device_id_type=MESH_ID)
    pl.semaphore_wait(barrier, 4 + groups - 1)

    mine = pl.ds(pl.multiple_of(me_group * slots, slots), slots)
    local = pltpu.make_async_copy(in_ref.at[me_group], out_ref.at[mx, mz, mine], local_sem)
    local.start()
    dispatch = []
    for o in range(1, groups):
        cp = pltpu.make_async_remote_copy(
            src_ref=in_ref.at[lax.rem(me_group + o, groups)],
            dst_ref=out_ref.at[mx, mz, mine],
            send_sem=in_send.at[o],
            recv_sem=in_recv.at[o],
            device_id=peer(o),
            device_id_type=MESH_ID,
        )
        cp.start()
        dispatch.append(cp)
    local.wait()
    for cp in dispatch:
        cp.wait_recv()

    rings = [("z", 1), ("z", -1), ("x", 1), ("x", -1)]

    def cols(r):
        return pl.ds(r * quarter, quarter)

    def block(axis, r, k):
        if axis == "z":
            return out_ref.at[mx, k, :, cols(r)]
        return out_ref.at[k, mz, :, cols(r)]

    def plane_block(axis, r, k):
        if axis == "x":
            return out_ref.at[k, :, :, cols(r)]
        return out_ref.at[:, k, :, cols(r)]

    def me_on(axis):
        return mz if axis == "z" else mx

    def ring_phase(axis_of, view, first_src, send, recv, sizes):
        copies = {}
        n = sizes
        for s in range(n - 1):
            for r in range(4):
                axis, d = axis_of(r), rings[r][1]
                me = me_on(axis)
                k = lax.rem(me + n * (s + 1) - d * s, n)
                if s == 0:
                    src = first_src(r)
                else:
                    copies[(r, s - 1)].wait_recv()
                    src = view(axis, r, k)
                cp = pltpu.make_async_remote_copy(
                    src_ref=src,
                    dst_ref=view(axis, r, k),
                    send_sem=send.at[r, s],
                    recv_sem=recv.at[r, s],
                    device_id=dev(axis, d),
                    device_id_type=MESH_ID,
                )
                cp.start()
                copies[(r, s)] = cp
        for r in range(4):
            copies[(r, n - 2)].wait_recv()
        return copies

    copies1 = ring_phase(
        lambda r: rings[r][0], block, lambda r: out_ref.at[mx, mz, :, cols(r)], send1, recv1, nz
    )

    def second(r):
        return "x" if rings[r][0] == "z" else "z"

    copies2 = ring_phase(
        second,
        plane_block,
        lambda r: plane_block(second(r), r, me_on(second(r))),
        send2,
        recv2,
        nx,
    )
    for cp in list(copies1.values()) + list(copies2.values()) + dispatch:
        cp.wait_send()


def plane_all_gather(slab, nx, nz, nsect, ny):
    groups, slots, width = slab.shape
    rows = groups * slots
    return pl.pallas_call(
        functools.partial(ag_kernel, nsect, ny),
        out_shape=jax.ShapeDtypeStruct((nx, nz, rows, width), slab.dtype),
        in_specs=[pl.BlockSpec(memory_space=pltpu.VMEM)],
        out_specs=pl.BlockSpec(memory_space=pltpu.VMEM),
        scratch_shapes=[
            pltpu.SemaphoreType.DMA(()),
            pltpu.SemaphoreType.DMA((groups,)),
            pltpu.SemaphoreType.DMA((groups,)),
            pltpu.SemaphoreType.DMA((4, nz - 1)),
            pltpu.SemaphoreType.DMA((4, nz - 1)),
            pltpu.SemaphoreType.DMA((4, nx - 1)),
            pltpu.SemaphoreType.DMA((4, nx - 1)),
        ],
        compiler_params=pltpu.CompilerParams(
            collective_id=1, has_side_effects=True, vmem_limit_bytes=60 * 1024 * 1024
        ),
    )(slab)


ALL = ("sect", "ey", "ex", "tp")
EXPERT_AXES = ("sect", "ey")
PLANE_AXES = ("ex", "tp")


def place_slots(ids_block, experts):
    flat_ids = ids_block.reshape(-1)
    hits_mask = (flat_ids[:, None] == jnp.arange(experts, dtype=jnp.int32)[None, :]).astype(
        jnp.int32
    )
    earlier = jnp.cumsum(hits_mask, axis=0) - hits_mask
    slot_rank = jnp.sum(earlier * hits_mask, axis=1)
    return (flat_ids, slot_rank)


def per_device(tokens, router_logits, expert_ids, w_gate, w_up, w_down):
    experts_all = lax.axis_size(EXPERT_AXES)
    plane_count = lax.axis_size(PLANE_AXES)
    token_count = tokens.shape[0]
    capacity = min(token_count, 4 * token_count // experts_all)
    model_width = tokens.shape[1]
    flat_ids, slot_rank = place_slots(expert_ids, experts_all)
    columns = flat_ids * capacity + slot_rank
    positions = jnp.arange(experts_all * capacity, dtype=jnp.int32)
    picker = (positions[:, None] == columns[None, :]).astype(jnp.bfloat16)
    repeated = jnp.repeat(tokens, 2, axis=0)
    slab = jnp.dot(picker, repeated, preferred_element_type=jnp.float32).astype(jnp.bfloat16)
    slab = slab.reshape(experts_all, capacity, model_width)
    nx = lax.axis_size("ex")
    plane_rows = plane_all_gather(
        slab, nx, plane_count // nx, lax.axis_size("sect"), lax.axis_size("ey")
    )
    weights = jax.nn.sigmoid(router_logits - router_logits[:, ::-1]).reshape(-1)
    return expert_reduce_scatter(
        columns.astype(jnp.int32),
        weights,
        plane_rows,
        w_gate[0],
        w_up[0],
        w_down[0],
        lax.axis_size("sect"),
        lax.axis_size("ey"),
    )


def x_extent(devices):
    coords = [getattr(d, "coords", None) for d in devices.flat]
    if all(c is not None for c in coords):
        return len({c[0] for c in coords})
    return int(round(np.sqrt(devices.shape[1])))


def solution(mesh):
    devices = mesh.devices
    sect, exp, tp = devices.shape
    ex = x_extent(devices)
    fine = Mesh(devices.reshape(sect, exp // ex, ex, tp), ALL)
    in_specs = (
        P(ALL, None),
        P(ALL, None),
        P(ALL, None),
        P(EXPERT_AXES + PLANE_AXES[:1], None, "tp"),
        P(EXPERT_AXES + PLANE_AXES[:1], None, "tp"),
        P(EXPERT_AXES + PLANE_AXES[:1], "tp", None),
    )
    out_specs = P(ALL, None)
    return jax.shard_map(
        per_device, mesh=fine, in_specs=in_specs, out_specs=out_specs, check_vma=False
    )
```

```python
import functools

import jax
import jax.numpy as jnp
import numpy as np
from jax import lax
from jax.experimental import pallas as pl
from jax.experimental.pallas import tpu as pltpu
from jax.sharding import Mesh
from jax.sharding import PartitionSpec as P

MESH_ID = pl.DeviceIdType.MESH


def rs_kernel(
    nsect, ny, col_ref, mix_w_ref, rows_ref, wg_hbm, wu_hbm, wd_hbm, mix_ref,
    out_ref, wg, wu, wd, hid, stage, stage_f1, stage2_d, stage2_f, fin, s1, total1, s2, wsem, send1, recv1, send2, recv2, local_sem, ret_send, ret_recv,
):
    nx, nz, rows, width = rows_ref.shape
    hidden_width = wd.shape[0]
    quarter = width // 4
    groups = nsect * ny
    slots = rows // groups
    c = lax.axis_index("sect")
    y = lax.axis_index("ey")
    mx = lax.axis_index("ex")
    mz = lax.axis_index("tp")

    weight_copies = [
        pltpu.make_async_copy(src, dst, wsem.at[i])
        for i, (src, dst) in enumerate(((wg_hbm, wg), (wu_hbm, wu), (wd_hbm, wd)))
    ]
    for cp in weight_copies:
        cp.start()

    def dev(axis, d):
        if axis == "z":
            return (c, y, mx, lax.rem(mz + d + nz, nz))
        return (c, y, lax.rem(mx + d + nx, nx), mz)

    me_group = c * ny + y

    def peer(o):
        g = lax.rem(me_group + o, groups)
        return (g // ny, lax.rem(g, ny), mx, mz)

    barrier = pltpu.get_barrier_semaphore()
    for axis in ("x", "z"):
        for d in (1, -1):
            pl.semaphore_signal(barrier, inc=1, device_id=dev(axis, d), device_id_type=MESH_ID)
    for o in range(1, groups):
        pl.semaphore_signal(barrier, inc=1, device_id=peer(o), device_id_type=MESH_ID)
    pl.semaphore_wait(barrier, 4 + groups - 1)

    weight_copies[0].wait()
    weight_copies[1].wait()

    def hidden_group(i, carry):
        block = rows_ref[i].reshape(nz * rows, width)
        gate = jnp.dot(block, wg[...], preferred_element_type=jnp.float32)
        up = jnp.dot(block, wu[...], preferred_element_type=jnp.float32)
        act = (jax.nn.silu(gate) * up).astype(hid.dtype)
        hid[i] = act.reshape(nz, rows, hidden_width)
        return carry

    lax.fori_loop(0, nx, hidden_group, 0)
    weight_copies[2].wait()

    rings = [("z", 1), ("z", -1), ("x", 1), ("x", -1)]

    def me_on(axis):
        return mz if axis == "z" else mx

    def size_on(axis):
        return nz if axis == "z" else nx

    def cols(r):
        return pl.ds(r * quarter, quarter)

    def chunk(r, j):
        if rings[r][0] == "z":
            h = hid[:, j]
        else:
            h = hid[j]
        lead = h.shape[0]
        part = jnp.dot(
            h.reshape(lead * rows, hidden_width), wd[:, cols(r)], preferred_element_type=jnp.float32
        )
        return part.reshape(lead, rows, quarter)

    def other(axis):
        return "x" if axis == "z" else "z"

    def both_sides(axis_of, own, stage_d, stage_f, recv_d, recv_f, recv_s, send, recv, finish):
        copies = []
        pending = {}
        for r in range(4):
            axis, d = axis_of(r), rings[r][1]
            n = size_on(axis)
            me = me_on(axis)
            stage_d[r] = own(r, lax.rem(me + n + d, n)).astype(stage_d.dtype)
            direct = pltpu.make_async_remote_copy(
                src_ref=stage_d.at[r], dst_ref=recv_d.at[r], send_sem=send.at[r, 0],
                recv_sem=recv.at[r, 0], device_id=dev(axis, d), device_id_type=MESH_ID,
            )
            direct.start()
            stage_f[r] = own(r, lax.rem(me + 2 * n - 2 * d, n)).astype(stage_f.dtype)
            forward = pltpu.make_async_remote_copy(
                src_ref=stage_f.at[r], dst_ref=recv_f.at[r], send_sem=send.at[r, 1],
                recv_sem=recv.at[r, 1], device_id=dev(axis, -d), device_id_type=MESH_ID,
            )
            forward.start()
            pending[r] = (direct, forward)
            copies += [direct, forward]
        for r in range(4):
            axis, d = axis_of(r), rings[r][1]
            n = size_on(axis)
            me = me_on(axis)
            term = own(r, lax.rem(me + n - d, n))
            pending[r][1].wait_recv()
            recv_f[r] = (recv_f[r].astype(jnp.float32) + term).astype(recv_f.dtype)
            second = pltpu.make_async_remote_copy(
                src_ref=recv_f.at[r], dst_ref=recv_s.at[r], send_sem=send.at[r, 2],
                recv_sem=recv.at[r, 2], device_id=dev(axis, -d), device_id_type=MESH_ID,
            )
            second.start()
            pending[r] = (pending[r][0], second)
            copies.append(second)
        for r in range(4):
            axis = axis_of(r)
            term = own(r, me_on(axis))
            pending[r][0].wait_recv()
            pending[r][1].wait_recv()
            finish(r, term + recv_d[r].astype(jnp.float32) + recv_s[r].astype(jnp.float32))
        return copies

    def keep_total1(r, value):
        total1[r] = value

    copies1 = both_sides(
        lambda r: rings[r][0], chunk, stage, stage_f1, s1.at[:, 0], s1.at[:, 1], s1.at[:, 2],
        send1, recv1, keep_total1,
    )

    def other_axis(r):
        return other(rings[r][0])

    def keep_fin(r, value):
        fin[:, cols(r)] = value

    copies2 = both_sides(
        other_axis, lambda r, j: total1[r, j], stage2_d, stage2_f, s2.at[:, 0], s2.at[:, 1], s2.at[:, 2],
        send2, recv2, keep_fin,
    )

    mine = pl.ds(pl.multiple_of(me_group * slots, slots), slots)
    local = pltpu.make_async_copy(fin.at[mine], out_ref.at[mine], local_sem)
    local.start()
    returns = []
    for o in range(1, groups):
        g = lax.rem(me_group + o, groups)
        cp = pltpu.make_async_remote_copy(
            src_ref=fin.at[pl.ds(pl.multiple_of(g * slots, slots), slots)],
            dst_ref=out_ref.at[mine],
            send_sem=ret_send.at[o],
            recv_sem=ret_recv.at[o],
            device_id=peer(o),
            device_id_type=MESH_ID,
        )
        cp.start()
        returns.append(cp)
    local.wait()
    for cp in returns:
        cp.wait_recv()
    for t in range(mix_ref.shape[0]):
        first = out_ref[pl.ds(col_ref[2 * t], 1), :]
        second = out_ref[pl.ds(col_ref[2 * t + 1], 1), :]
        mix = mix_w_ref[2 * t] * first + mix_w_ref[2 * t + 1] * second
        mix_ref[pl.ds(t, 1), :] = mix.astype(mix_ref.dtype)
    for cp in copies1 + copies2 + returns:
        cp.wait_send()


def expert_reduce_scatter(columns, mix_w, expert_rows, w_gate, w_up, w_down, nsect, ny):
    nx, nz, rows, width = expert_rows.shape
    hidden_width = w_down.shape[0]
    quarter = width // 4
    groups = nsect * ny
    return pl.pallas_call(
        functools.partial(rs_kernel, nsect, ny),
        out_shape=jax.ShapeDtypeStruct((columns.shape[0] // 2, width), jnp.bfloat16),
        in_specs=[
            pl.BlockSpec(memory_space=pltpu.SMEM),
            pl.BlockSpec(memory_space=pltpu.SMEM),
            pl.BlockSpec(memory_space=pltpu.VMEM),
            pl.BlockSpec(memory_space=pl.ANY),
            pl.BlockSpec(memory_space=pl.ANY),
            pl.BlockSpec(memory_space=pl.ANY),
        ],
        out_specs=pl.BlockSpec(memory_space=pltpu.VMEM),
        scratch_shapes=[
            pltpu.VMEM((rows, width), jnp.float32),
            pltpu.VMEM(w_gate.shape, w_gate.dtype),
            pltpu.VMEM(w_up.shape, w_up.dtype),
            pltpu.VMEM(w_down.shape, w_down.dtype),
            pltpu.VMEM((nx, nz, rows, hidden_width), jnp.bfloat16),
            pltpu.VMEM((4, nx, rows, quarter), jnp.bfloat16),
            pltpu.VMEM((4, nx, rows, quarter), jnp.bfloat16),
            pltpu.VMEM((4, rows, quarter), jnp.float32),
            pltpu.VMEM((4, rows, quarter), jnp.float32),
            pltpu.VMEM((rows, width), jnp.float32),
            pltpu.VMEM((4, 3, nx, rows, quarter), jnp.bfloat16),
            pltpu.VMEM((4, nx, rows, quarter), jnp.float32),
            pltpu.VMEM((4, 3, rows, quarter), jnp.float32),
            pltpu.SemaphoreType.DMA((3,)),
            pltpu.SemaphoreType.DMA((4, 3)),
            pltpu.SemaphoreType.DMA((4, 3)),
            pltpu.SemaphoreType.DMA((4, 3)),
            pltpu.SemaphoreType.DMA((4, 3)),
            pltpu.SemaphoreType.DMA(()),
            pltpu.SemaphoreType.DMA((groups,)),
            pltpu.SemaphoreType.DMA((groups,)),
        ],
        compiler_params=pltpu.CompilerParams(
            collective_id=0, has_side_effects=True, vmem_limit_bytes=64 * 1024 * 1024
        ),
    )(columns, mix_w, expert_rows, w_gate, w_up, w_down)


def ag_kernel(nsect, ny, in_ref, out_ref, local_sem, in_send, in_recv, send1, recv1, send2, recv2):
    nx, nz, rows, width = out_ref.shape
    groups = nsect * ny
    slots = rows // groups
    quarter = width // 4
    c = lax.axis_index("sect")
    y = lax.axis_index("ey")
    mx = lax.axis_index("ex")
    mz = lax.axis_index("tp")

    def dev(axis, d):
        if axis == "z":
            return (c, y, mx, lax.rem(mz + d + nz, nz))
        return (c, y, lax.rem(mx + d + nx, nx), mz)

    me_group = c * ny + y

    def peer(o):
        g = lax.rem(me_group + o, groups)
        return (g // ny, lax.rem(g, ny), mx, mz)

    barrier = pltpu.get_barrier_semaphore()
    for axis in ("x", "z"):
        for d in (1, -1):
            pl.semaphore_signal(barrier, inc=1, device_id=dev(axis, d), device_id_type=MESH_ID)
    for o in range(1, groups):
        pl.semaphore_signal(barrier, inc=1, device_id=peer(o), device_id_type=MESH_ID)
    pl.semaphore_wait(barrier, 4 + groups - 1)

    mine = pl.ds(pl.multiple_of(me_group * slots, slots), slots)
    local = pltpu.make_async_copy(in_ref.at[me_group], out_ref.at[mx, mz, mine], local_sem)
    local.start()
    dispatch = []
    for o in range(1, groups):
        cp = pltpu.make_async_remote_copy(
            src_ref=in_ref.at[lax.rem(me_group + o, groups)],
            dst_ref=out_ref.at[mx, mz, mine],
            send_sem=in_send.at[o],
            recv_sem=in_recv.at[o],
            device_id=peer(o),
            device_id_type=MESH_ID,
        )
        cp.start()
        dispatch.append(cp)
    local.wait()
    for cp in dispatch:
        cp.wait_recv()

    rings = [("z", 1), ("z", -1), ("x", 1), ("x", -1)]

    def cols(r):
        return pl.ds(r * quarter, quarter)

    def block(axis, r, k):
        if axis == "z":
            return out_ref.at[mx, k, :, cols(r)]
        return out_ref.at[k, mz, :, cols(r)]

    def plane_block(axis, r, k):
        if axis == "x":
            return out_ref.at[k, :, :, cols(r)]
        return out_ref.at[:, k, :, cols(r)]

    def me_on(axis):
        return mz if axis == "z" else mx

    def ring_phase(axis_of, view, first_src, send, recv, sizes):
        copies = {}
        n = sizes
        for s in range(n - 1):
            for r in range(4):
                axis, d = axis_of(r), rings[r][1]
                me = me_on(axis)
                k = lax.rem(me + n * (s + 1) - d * s, n)
                if s == 0:
                    src = first_src(r)
                else:
                    copies[(r, s - 1)].wait_recv()
                    src = view(axis, r, k)
                cp = pltpu.make_async_remote_copy(
                    src_ref=src,
                    dst_ref=view(axis, r, k),
                    send_sem=send.at[r, s],
                    recv_sem=recv.at[r, s],
                    device_id=dev(axis, d),
                    device_id_type=MESH_ID,
                )
                cp.start()
                copies[(r, s)] = cp
        for r in range(4):
            copies[(r, n - 2)].wait_recv()
        return copies

    copies1 = ring_phase(
        lambda r: rings[r][0], block, lambda r: out_ref.at[mx, mz, :, cols(r)], send1, recv1, nz
    )

    def second(r):
        return "x" if rings[r][0] == "z" else "z"

    copies2 = ring_phase(
        second,
        plane_block,
        lambda r: plane_block(second(r), r, me_on(second(r))),
        send2,
        recv2,
        nx,
    )
    for cp in list(copies1.values()) + list(copies2.values()) + dispatch:
        cp.wait_send()


def plane_all_gather(slab, nx, nz, nsect, ny):
    groups, slots, width = slab.shape
    rows = groups * slots
    return pl.pallas_call(
        functools.partial(ag_kernel, nsect, ny),
        out_shape=jax.ShapeDtypeStruct((nx, nz, rows, width), slab.dtype),
        in_specs=[pl.BlockSpec(memory_space=pltpu.VMEM)],
        out_specs=pl.BlockSpec(memory_space=pltpu.VMEM),
        scratch_shapes=[
            pltpu.SemaphoreType.DMA(()),
            pltpu.SemaphoreType.DMA((groups,)),
            pltpu.SemaphoreType.DMA((groups,)),
            pltpu.SemaphoreType.DMA((4, nz - 1)),
            pltpu.SemaphoreType.DMA((4, nz - 1)),
            pltpu.SemaphoreType.DMA((4, nx - 1)),
            pltpu.SemaphoreType.DMA((4, nx - 1)),
        ],
        compiler_params=pltpu.CompilerParams(
            collective_id=1, has_side_effects=True, vmem_limit_bytes=60 * 1024 * 1024
        ),
    )(slab)


ALL = ("sect", "ey", "ex", "tp")
EXPERT_AXES = ("sect", "ey")
PLANE_AXES = ("ex", "tp")


def place_slots(ids_block, experts):
    flat_ids = ids_block.reshape(-1)
    hits_mask = (flat_ids[:, None] == jnp.arange(experts, dtype=jnp.int32)[None, :]).astype(
        jnp.int32
    )
    earlier = jnp.cumsum(hits_mask, axis=0) - hits_mask
    slot_rank = jnp.sum(earlier * hits_mask, axis=1)
    return (flat_ids, slot_rank)


def per_device(tokens, router_logits, expert_ids, w_gate, w_up, w_down):
    experts_all = lax.axis_size(EXPERT_AXES)
    plane_count = lax.axis_size(PLANE_AXES)
    token_count = tokens.shape[0]
    capacity = min(token_count, 4 * token_count // experts_all)
    model_width = tokens.shape[1]
    flat_ids, slot_rank = place_slots(expert_ids, experts_all)
    columns = flat_ids * capacity + slot_rank
    positions = jnp.arange(experts_all * capacity, dtype=jnp.int32)
    picker = (positions[:, None] == columns[None, :]).astype(jnp.bfloat16)
    repeated = jnp.repeat(tokens, 2, axis=0)
    slab = jnp.dot(picker, repeated, preferred_element_type=jnp.float32).astype(jnp.bfloat16)
    slab = slab.reshape(experts_all, capacity, model_width)
    nx = lax.axis_size("ex")
    plane_rows = plane_all_gather(
        slab, nx, plane_count // nx, lax.axis_size("sect"), lax.axis_size("ey")
    )
    weights = jax.nn.sigmoid(router_logits - router_logits[:, ::-1]).reshape(-1)
    return expert_reduce_scatter(
        columns.astype(jnp.int32),
        weights,
        plane_rows,
        w_gate[0],
        w_up[0],
        w_down[0],
        lax.axis_size("sect"),
        lax.axis_size("ey"),
    )


def x_extent(devices):
    coords = [getattr(d, "coords", None) for d in devices.flat]
    if all(c is not None for c in coords):
        return len({c[0] for c in coords})
    return int(round(np.sqrt(devices.shape[1])))


def solution(mesh):
    devices = mesh.devices
    sect, exp, tp = devices.shape
    ex = x_extent(devices)
    fine = Mesh(devices.reshape(sect, exp // ex, ex, tp), ALL)
    in_specs = (
        P(ALL, None),
        P(ALL, None),
        P(ALL, None),
        P(EXPERT_AXES + PLANE_AXES[:1], None, "tp"),
        P(EXPERT_AXES + PLANE_AXES[:1], None, "tp"),
        P(EXPERT_AXES + PLANE_AXES[:1], "tp", None),
    )
    out_specs = P(ALL, None)
    return jax.shard_map(
        per_device, mesh=fine, in_specs=in_specs, out_specs=out_specs, check_vma=False
    )
```

```python
import functools

import jax
import jax.numpy as jnp
import numpy as np
from jax import lax
from jax.experimental import pallas as pl
from jax.experimental.pallas import tpu as pltpu
from jax.sharding import Mesh
from jax.sharding import PartitionSpec as P

MESH_ID = pl.DeviceIdType.MESH


def rs_kernel(
    nsect, ny, col_ref, mix_w_ref, rows_ref, wg_hbm, wu_hbm, wd_hbm, mix_ref,
    out_ref, wg, wu, wd, hid, stage, stage_f1, stage2_d, stage2_f, fin, s1, total1, s2, wsem, send1, recv1, send2, recv2, local_sem, ret_send, ret_recv,
):
    nx, nz, rows, width = rows_ref.shape
    hidden_width = wd.shape[0]
    quarter = width // 4
    groups = nsect * ny
    slots = rows // groups
    c = lax.axis_index("sect")
    y = lax.axis_index("ey")
    mx = lax.axis_index("ex")
    mz = lax.axis_index("tp")

    weight_copies = [
        pltpu.make_async_copy(src, dst, wsem.at[i])
        for i, (src, dst) in enumerate(((wg_hbm, wg), (wu_hbm, wu), (wd_hbm, wd)))
    ]
    for cp in weight_copies:
        cp.start()

    def dev(axis, d):
        if axis == "z":
            return (c, y, mx, lax.rem(mz + d + nz, nz))
        return (c, y, lax.rem(mx + d + nx, nx), mz)

    me_group = c * ny + y

    def peer(o):
        g = lax.rem(me_group + o, groups)
        return (g // ny, lax.rem(g, ny), mx, mz)

    barrier = pltpu.get_barrier_semaphore()
    for axis in ("x", "z"):
        for d in (1, -1):
            pl.semaphore_signal(barrier, inc=1, device_id=dev(axis, d), device_id_type=MESH_ID)
    for o in range(1, groups):
        pl.semaphore_signal(barrier, inc=1, device_id=peer(o), device_id_type=MESH_ID)
    pl.semaphore_wait(barrier, 4 + groups - 1)

    weight_copies[0].wait()
    weight_copies[1].wait()

    def hidden_group(i, carry):
        block = rows_ref[i].reshape(nz * rows, width)
        gate = jnp.dot(block, wg[...], preferred_element_type=jnp.float32)
        up = jnp.dot(block, wu[...], preferred_element_type=jnp.float32)
        act = (jax.nn.silu(gate) * up).astype(hid.dtype)
        hid[i] = act.reshape(nz, rows, hidden_width)
        return carry

    lax.fori_loop(0, nx, hidden_group, 0)
    weight_copies[2].wait()

    rings = [("z", 1), ("z", -1), ("x", 1), ("x", -1)]

    def me_on(axis):
        return mz if axis == "z" else mx

    def size_on(axis):
        return nz if axis == "z" else nx

    def cols(r):
        return pl.ds(r * quarter, quarter)

    def chunk(r, j):
        if rings[r][0] == "z":
            h = hid[:, j]
        else:
            h = hid[j]
        lead = h.shape[0]
        part = jnp.dot(
            h.reshape(lead * rows, hidden_width), wd[:, cols(r)], preferred_element_type=jnp.float32
        )
        return part.reshape(lead, rows, quarter)

    def other(axis):
        return "x" if axis == "z" else "z"

    def both_sides(axis_of, own, stage_d, stage_f, recv_d, recv_f, recv_s, send, recv, finish):
        copies = []
        pending = {}
        for r in range(4):
            axis, d = axis_of(r), rings[r][1]
            n = size_on(axis)
            me = me_on(axis)
            stage_d[r] = own(r, lax.rem(me + n + d, n)).astype(stage_d.dtype)
            direct = pltpu.make_async_remote_copy(
                src_ref=stage_d.at[r], dst_ref=recv_d.at[r], send_sem=send.at[r, 0],
                recv_sem=recv.at[r, 0], device_id=dev(axis, d), device_id_type=MESH_ID,
            )
            direct.start()
            stage_f[r] = own(r, lax.rem(me + 2 * n - 2 * d, n)).astype(stage_f.dtype)
            forward = pltpu.make_async_remote_copy(
                src_ref=stage_f.at[r], dst_ref=recv_f.at[r], send_sem=send.at[r, 1],
                recv_sem=recv.at[r, 1], device_id=dev(axis, -d), device_id_type=MESH_ID,
            )
            forward.start()
            pending[r] = (direct, forward)
            copies += [direct, forward]
        for r in range(4):
            axis, d = axis_of(r), rings[r][1]
            n = size_on(axis)
            me = me_on(axis)
            term = own(r, lax.rem(me + n - d, n))
            pending[r][1].wait_recv()
            recv_f[r] = (recv_f[r].astype(jnp.float32) + term).astype(recv_f.dtype)
            second = pltpu.make_async_remote_copy(
                src_ref=recv_f.at[r], dst_ref=recv_s.at[r], send_sem=send.at[r, 2],
                recv_sem=recv.at[r, 2], device_id=dev(axis, -d), device_id_type=MESH_ID,
            )
            second.start()
            pending[r] = (pending[r][0], second)
            copies.append(second)
        for r in range(4):
            axis = axis_of(r)
            term = own(r, me_on(axis))
            pending[r][0].wait_recv()
            pending[r][1].wait_recv()
            finish(r, term + recv_d[r].astype(jnp.float32) + recv_s[r].astype(jnp.float32))
        return copies

    def keep_total1(r, value):
        total1[r] = value

    copies1 = both_sides(
        lambda r: rings[r][0], chunk, stage, stage_f1, s1.at[:, 0], s1.at[:, 1], s1.at[:, 2],
        send1, recv1, keep_total1,
    )

    def other_axis(r):
        return other(rings[r][0])

    def keep_fin(r, value):
        fin[:, cols(r)] = value

    copies2 = both_sides(
        other_axis, lambda r, j: total1[r, j], stage2_d, stage2_f, s2.at[:, 0], s2.at[:, 1], s2.at[:, 2],
        send2, recv2, keep_fin,
    )

    mine = pl.ds(pl.multiple_of(me_group * slots, slots), slots)
    local = pltpu.make_async_copy(fin.at[mine], out_ref.at[mine], local_sem)
    local.start()
    returns = []
    for o in range(1, groups):
        g = lax.rem(me_group + o, groups)
        cp = pltpu.make_async_remote_copy(
            src_ref=fin.at[pl.ds(pl.multiple_of(g * slots, slots), slots)],
            dst_ref=out_ref.at[mine],
            send_sem=ret_send.at[o],
            recv_sem=ret_recv.at[o],
            device_id=peer(o),
            device_id_type=MESH_ID,
        )
        cp.start()
        returns.append(cp)
    local.wait()
    for cp in returns:
        cp.wait_recv()
    for t in range(mix_ref.shape[0]):
        first = out_ref[pl.ds(col_ref[2 * t], 1), :]
        second = out_ref[pl.ds(col_ref[2 * t + 1], 1), :]
        mix = mix_w_ref[2 * t] * first + mix_w_ref[2 * t + 1] * second
        mix_ref[pl.ds(t, 1), :] = mix.astype(mix_ref.dtype)
    for cp in copies1 + copies2 + returns:
        cp.wait_send()


def expert_reduce_scatter(columns, mix_w, expert_rows, w_gate, w_up, w_down, nsect, ny):
    nx, nz, rows, width = expert_rows.shape
    hidden_width = w_down.shape[0]
    quarter = width // 4
    groups = nsect * ny
    return pl.pallas_call(
        functools.partial(rs_kernel, nsect, ny),
        out_shape=jax.ShapeDtypeStruct((columns.shape[0] // 2, width), jnp.bfloat16),
        in_specs=[
            pl.BlockSpec(memory_space=pltpu.SMEM),
            pl.BlockSpec(memory_space=pltpu.SMEM),
            pl.BlockSpec(memory_space=pltpu.VMEM),
            pl.BlockSpec(memory_space=pl.ANY),
            pl.BlockSpec(memory_space=pl.ANY),
            pl.BlockSpec(memory_space=pl.ANY),
        ],
        out_specs=pl.BlockSpec(memory_space=pltpu.VMEM),
        scratch_shapes=[
            pltpu.VMEM((rows, width), jnp.float32),
            pltpu.VMEM(w_gate.shape, w_gate.dtype),
            pltpu.VMEM(w_up.shape, w_up.dtype),
            pltpu.VMEM(w_down.shape, w_down.dtype),
            pltpu.VMEM((nx, nz, rows, hidden_width), jnp.bfloat16),
            pltpu.VMEM((4, nx, rows, quarter), jnp.bfloat16),
            pltpu.VMEM((4, nx, rows, quarter), jnp.bfloat16),
            pltpu.VMEM((4, rows, quarter), jnp.float32),
            pltpu.VMEM((4, rows, quarter), jnp.float32),
            pltpu.VMEM((rows, width), jnp.float32),
            pltpu.VMEM((4, 3, nx, rows, quarter), jnp.bfloat16),
            pltpu.VMEM((4, nx, rows, quarter), jnp.float32),
            pltpu.VMEM((4, 3, rows, quarter), jnp.float32),
            pltpu.SemaphoreType.DMA((3,)),
            pltpu.SemaphoreType.DMA((4, 3)),
            pltpu.SemaphoreType.DMA((4, 3)),
            pltpu.SemaphoreType.DMA((4, 3)),
            pltpu.SemaphoreType.DMA((4, 3)),
            pltpu.SemaphoreType.DMA(()),
            pltpu.SemaphoreType.DMA((groups,)),
            pltpu.SemaphoreType.DMA((groups,)),
        ],
        compiler_params=pltpu.CompilerParams(
            collective_id=0, has_side_effects=True, vmem_limit_bytes=64 * 1024 * 1024
        ),
    )(columns, mix_w, expert_rows, w_gate, w_up, w_down)


def ag_kernel(nsect, ny, in_ref, out_ref, local_sem, in_send, in_recv, send1, recv1, send2, recv2):
    nx, nz, rows, width = out_ref.shape
    groups = nsect * ny
    slots = rows // groups
    quarter = width // 4
    c = lax.axis_index("sect")
    y = lax.axis_index("ey")
    mx = lax.axis_index("ex")
    mz = lax.axis_index("tp")

    def dev(axis, d):
        if axis == "z":
            return (c, y, mx, lax.rem(mz + d + nz, nz))
        return (c, y, lax.rem(mx + d + nx, nx), mz)

    me_group = c * ny + y

    def peer(o):
        g = lax.rem(me_group + o, groups)
        return (g // ny, lax.rem(g, ny), mx, mz)

    barrier = pltpu.get_barrier_semaphore()
    for axis in ("x", "z"):
        for d in (1, -1):
            pl.semaphore_signal(barrier, inc=1, device_id=dev(axis, d), device_id_type=MESH_ID)
    for o in range(1, groups):
        pl.semaphore_signal(barrier, inc=1, device_id=peer(o), device_id_type=MESH_ID)
    pl.semaphore_wait(barrier, 4 + groups - 1)

    mine = pl.ds(pl.multiple_of(me_group * slots, slots), slots)
    local = pltpu.make_async_copy(in_ref.at[me_group], out_ref.at[mx, mz, mine], local_sem)
    local.start()
    dispatch = []
    for o in range(1, groups):
        cp = pltpu.make_async_remote_copy(
            src_ref=in_ref.at[lax.rem(me_group + o, groups)],
            dst_ref=out_ref.at[mx, mz, mine],
            send_sem=in_send.at[o],
            recv_sem=in_recv.at[o],
            device_id=peer(o),
            device_id_type=MESH_ID,
        )
        cp.start()
        dispatch.append(cp)
    local.wait()
    for cp in dispatch:
        cp.wait_recv()

    rings = [("z", 1), ("z", -1), ("x", 1), ("x", -1)]

    def cols(r):
        return pl.ds(r * quarter, quarter)

    def block(axis, r, k):
        if axis == "z":
            return out_ref.at[mx, k, :, cols(r)]
        return out_ref.at[k, mz, :, cols(r)]

    def plane_block(axis, r, k):
        if axis == "x":
            return out_ref.at[k, :, :, cols(r)]
        return out_ref.at[:, k, :, cols(r)]

    def me_on(axis):
        return mz if axis == "z" else mx

    def both_sides(axis_of, view, send, recv):
        copies = []
        first = {}
        for r in range(4):
            axis, d = axis_of(r), rings[r][1]
            me = me_on(axis)
            src = view(axis, r, me)
            for side, sign in ((0, d), (1, -d)):
                cp = pltpu.make_async_remote_copy(
                    src_ref=src, dst_ref=src, send_sem=send.at[r, side], recv_sem=recv.at[r, side],
                    device_id=dev(axis, sign), device_id_type=MESH_ID,
                )
                cp.start()
                first[(r, side)] = cp
                copies.append(cp)
        later = {}
        for r in range(4):
            axis, d = axis_of(r), rings[r][1]
            n = nz if axis == "z" else nx
            first[(r, 1)].wait_recv()
            passing = view(axis, r, lax.rem(me_on(axis) + n + d, n))
            cp = pltpu.make_async_remote_copy(
                src_ref=passing, dst_ref=passing, send_sem=send.at[r, 2], recv_sem=recv.at[r, 2],
                device_id=dev(axis, -d), device_id_type=MESH_ID,
            )
            cp.start()
            later[r] = cp
            copies.append(cp)
        for r in range(4):
            first[(r, 0)].wait_recv()
            later[r].wait_recv()
        return copies

    copies1 = both_sides(lambda r: rings[r][0], block, send1, recv1)

    def second(r):
        return "x" if rings[r][0] == "z" else "z"

    copies2 = both_sides(second, plane_block, send2, recv2)
    for cp in copies1 + copies2 + dispatch:
        cp.wait_send()


def plane_all_gather(slab, nx, nz, nsect, ny):
    groups, slots, width = slab.shape
    rows = groups * slots
    return pl.pallas_call(
        functools.partial(ag_kernel, nsect, ny),
        out_shape=jax.ShapeDtypeStruct((nx, nz, rows, width), slab.dtype),
        in_specs=[pl.BlockSpec(memory_space=pltpu.VMEM)],
        out_specs=pl.BlockSpec(memory_space=pltpu.VMEM),
        scratch_shapes=[
            pltpu.SemaphoreType.DMA(()),
            pltpu.SemaphoreType.DMA((groups,)),
            pltpu.SemaphoreType.DMA((groups,)),
            pltpu.SemaphoreType.DMA((4, 3)),
            pltpu.SemaphoreType.DMA((4, 3)),
            pltpu.SemaphoreType.DMA((4, 3)),
            pltpu.SemaphoreType.DMA((4, 3)),
        ],
        compiler_params=pltpu.CompilerParams(
            collective_id=1, has_side_effects=True, vmem_limit_bytes=60 * 1024 * 1024
        ),
    )(slab)


ALL = ("sect", "ey", "ex", "tp")
EXPERT_AXES = ("sect", "ey")
PLANE_AXES = ("ex", "tp")


def place_slots(ids_block, experts):
    flat_ids = ids_block.reshape(-1)
    hits_mask = (flat_ids[:, None] == jnp.arange(experts, dtype=jnp.int32)[None, :]).astype(
        jnp.int32
    )
    earlier = jnp.cumsum(hits_mask, axis=0) - hits_mask
    slot_rank = jnp.sum(earlier * hits_mask, axis=1)
    return (flat_ids, slot_rank)


def per_device(tokens, router_logits, expert_ids, w_gate, w_up, w_down):
    experts_all = lax.axis_size(EXPERT_AXES)
    plane_count = lax.axis_size(PLANE_AXES)
    token_count = tokens.shape[0]
    capacity = min(token_count, 4 * token_count // experts_all)
    model_width = tokens.shape[1]
    flat_ids, slot_rank = place_slots(expert_ids, experts_all)
    columns = flat_ids * capacity + slot_rank
    positions = jnp.arange(experts_all * capacity, dtype=jnp.int32)
    picker = (positions[:, None] == columns[None, :]).astype(jnp.bfloat16)
    repeated = jnp.repeat(tokens, 2, axis=0)
    slab = jnp.dot(picker, repeated, preferred_element_type=jnp.float32).astype(jnp.bfloat16)
    slab = slab.reshape(experts_all, capacity, model_width)
    nx = lax.axis_size("ex")
    plane_rows = plane_all_gather(
        slab, nx, plane_count // nx, lax.axis_size("sect"), lax.axis_size("ey")
    )
    weights = jax.nn.sigmoid(router_logits - router_logits[:, ::-1]).reshape(-1)
    return expert_reduce_scatter(
        columns.astype(jnp.int32),
        weights,
        plane_rows,
        w_gate[0],
        w_up[0],
        w_down[0],
        lax.axis_size("sect"),
        lax.axis_size("ey"),
    )


def x_extent(devices):
    coords = [getattr(d, "coords", None) for d in devices.flat]
    if all(c is not None for c in coords):
        return len({c[0] for c in coords})
    return int(round(np.sqrt(devices.shape[1])))


def solution(mesh):
    devices = mesh.devices
    sect, exp, tp = devices.shape
    ex = x_extent(devices)
    fine = Mesh(devices.reshape(sect, exp // ex, ex, tp), ALL)
    in_specs = (
        P(ALL, None),
        P(ALL, None),
        P(ALL, None),
        P(EXPERT_AXES + PLANE_AXES[:1], None, "tp"),
        P(EXPERT_AXES + PLANE_AXES[:1], None, "tp"),
        P(EXPERT_AXES + PLANE_AXES[:1], "tp", None),
    )
    out_specs = P(ALL, None)
    return jax.shard_map(
        per_device, mesh=fine, in_specs=in_specs, out_specs=out_specs, check_vma=False
    )
```

```python
import functools

import jax
import jax.numpy as jnp
import numpy as np
from jax import lax
from jax.experimental import pallas as pl
from jax.experimental.pallas import tpu as pltpu
from jax.sharding import Mesh
from jax.sharding import PartitionSpec as P

MESH_ID = pl.DeviceIdType.MESH


def rs_kernel(
    nsect, ny, col_ref, mix_w_ref, slab_ref, wg_hbm, wu_hbm, wd_hbm, mix_ref,
    out_ref, wg, wu, wd, hid, stage, stage_f1, stage2_d, stage2_f, fin, s1, total1, s2, wsem, send1, recv1, send2, recv2, local_sem, ret_send, ret_recv,
    rows_ref, g_local, g_in_send, g_in_recv, g_send1, g_recv1, g_send2, g_recv2,
):
    nx, nz, rows, width = rows_ref.shape
    hidden_width = wd.shape[0]
    quarter = width // 4
    groups = nsect * ny
    slots = rows // groups
    c = lax.axis_index("sect")
    y = lax.axis_index("ey")
    mx = lax.axis_index("ex")
    mz = lax.axis_index("tp")

    weight_copies = [
        pltpu.make_async_copy(src, dst, wsem.at[i])
        for i, (src, dst) in enumerate(((wg_hbm, wg), (wu_hbm, wu), (wd_hbm, wd)))
    ]
    for cp in weight_copies:
        cp.start()

    def dev(axis, d):
        if axis == "z":
            return (c, y, mx, lax.rem(mz + d + nz, nz))
        return (c, y, lax.rem(mx + d + nx, nx), mz)

    me_group = c * ny + y

    def peer(o):
        g = lax.rem(me_group + o, groups)
        return (g // ny, lax.rem(g, ny), mx, mz)

    barrier = pltpu.get_barrier_semaphore()
    for axis in ("x", "z"):
        for d in (1, -1):
            pl.semaphore_signal(barrier, inc=1, device_id=dev(axis, d), device_id_type=MESH_ID)
    for o in range(1, groups):
        pl.semaphore_signal(barrier, inc=1, device_id=peer(o), device_id_type=MESH_ID)
    pl.semaphore_wait(barrier, 4 + groups - 1)

    gather_body(
        nsect, ny, slab_ref, rows_ref, g_local, g_in_send, g_in_recv, g_send1, g_recv1, g_send2, g_recv2
    )
    weight_copies[0].wait()
    weight_copies[1].wait()

    def hidden_group(i, carry):
        block = rows_ref[i].reshape(nz * rows, width)
        gate = jnp.dot(block, wg[...], preferred_element_type=jnp.float32)
        up = jnp.dot(block, wu[...], preferred_element_type=jnp.float32)
        act = (jax.nn.silu(gate) * up).astype(hid.dtype)
        hid[i] = act.reshape(nz, rows, hidden_width)
        return carry

    lax.fori_loop(0, nx, hidden_group, 0)
    weight_copies[2].wait()

    rings = [("z", 1), ("z", -1), ("x", 1), ("x", -1)]

    def me_on(axis):
        return mz if axis == "z" else mx

    def size_on(axis):
        return nz if axis == "z" else nx

    def cols(r):
        return pl.ds(r * quarter, quarter)

    def chunk(r, j):
        if rings[r][0] == "z":
            h = hid[:, j]
        else:
            h = hid[j]
        lead = h.shape[0]
        part = jnp.dot(
            h.reshape(lead * rows, hidden_width), wd[:, cols(r)], preferred_element_type=jnp.float32
        )
        return part.reshape(lead, rows, quarter)

    def other(axis):
        return "x" if axis == "z" else "z"

    def both_sides(axis_of, own, stage_d, stage_f, recv_d, recv_f, recv_s, send, recv, finish):
        copies = []
        pending = {}
        for r in range(4):
            axis, d = axis_of(r), rings[r][1]
            n = size_on(axis)
            me = me_on(axis)
            stage_d[r] = own(r, lax.rem(me + n + d, n)).astype(stage_d.dtype)
            direct = pltpu.make_async_remote_copy(
                src_ref=stage_d.at[r], dst_ref=recv_d.at[r], send_sem=send.at[r, 0],
                recv_sem=recv.at[r, 0], device_id=dev(axis, d), device_id_type=MESH_ID,
            )
            direct.start()
            stage_f[r] = own(r, lax.rem(me + 2 * n - 2 * d, n)).astype(stage_f.dtype)
            forward = pltpu.make_async_remote_copy(
                src_ref=stage_f.at[r], dst_ref=recv_f.at[r], send_sem=send.at[r, 1],
                recv_sem=recv.at[r, 1], device_id=dev(axis, -d), device_id_type=MESH_ID,
            )
            forward.start()
            pending[r] = (direct, forward)
            copies += [direct, forward]
        for r in range(4):
            axis, d = axis_of(r), rings[r][1]
            n = size_on(axis)
            me = me_on(axis)
            term = own(r, lax.rem(me + n - d, n))
            pending[r][1].wait_recv()
            recv_f[r] = (recv_f[r].astype(jnp.float32) + term).astype(recv_f.dtype)
            second = pltpu.make_async_remote_copy(
                src_ref=recv_f.at[r], dst_ref=recv_s.at[r], send_sem=send.at[r, 2],
                recv_sem=recv.at[r, 2], device_id=dev(axis, -d), device_id_type=MESH_ID,
            )
            second.start()
            pending[r] = (pending[r][0], second)
            copies.append(second)
        for r in range(4):
            axis = axis_of(r)
            term = own(r, me_on(axis))
            pending[r][0].wait_recv()
            pending[r][1].wait_recv()
            finish(r, term + recv_d[r].astype(jnp.float32) + recv_s[r].astype(jnp.float32))
        return copies

    def keep_total1(r, value):
        total1[r] = value

    copies1 = both_sides(
        lambda r: rings[r][0], chunk, stage, stage_f1, s1.at[:, 0], s1.at[:, 1], s1.at[:, 2],
        send1, recv1, keep_total1,
    )

    def other_axis(r):
        return other(rings[r][0])

    def keep_fin(r, value):
        fin[:, cols(r)] = value

    copies2 = both_sides(
        other_axis, lambda r, j: total1[r, j], stage2_d, stage2_f, s2.at[:, 0], s2.at[:, 1], s2.at[:, 2],
        send2, recv2, keep_fin,
    )

    mine = pl.ds(pl.multiple_of(me_group * slots, slots), slots)
    local = pltpu.make_async_copy(fin.at[mine], out_ref.at[mine], local_sem)
    local.start()
    returns = []
    for o in range(1, groups):
        g = lax.rem(me_group + o, groups)
        cp = pltpu.make_async_remote_copy(
            src_ref=fin.at[pl.ds(pl.multiple_of(g * slots, slots), slots)],
            dst_ref=out_ref.at[mine],
            send_sem=ret_send.at[o],
            recv_sem=ret_recv.at[o],
            device_id=peer(o),
            device_id_type=MESH_ID,
        )
        cp.start()
        returns.append(cp)
    local.wait()
    for cp in returns:
        cp.wait_recv()
    for t in range(mix_ref.shape[0]):
        first = out_ref[pl.ds(col_ref[2 * t], 1), :]
        second = out_ref[pl.ds(col_ref[2 * t + 1], 1), :]
        mix = mix_w_ref[2 * t] * first + mix_w_ref[2 * t + 1] * second
        mix_ref[pl.ds(t, 1), :] = mix.astype(mix_ref.dtype)
    for cp in copies1 + copies2 + returns:
        cp.wait_send()


def expert_reduce_scatter(columns, mix_w, slab, w_gate, w_up, w_down, nsect, ny, nx, nz):
    groups, slots, width = slab.shape
    rows = groups * slots
    hidden_width = w_down.shape[0]
    quarter = width // 4
    return pl.pallas_call(
        functools.partial(rs_kernel, nsect, ny),
        out_shape=jax.ShapeDtypeStruct((columns.shape[0] // 2, width), jnp.bfloat16),
        in_specs=[
            pl.BlockSpec(memory_space=pltpu.SMEM),
            pl.BlockSpec(memory_space=pltpu.SMEM),
            pl.BlockSpec(memory_space=pltpu.VMEM),
            pl.BlockSpec(memory_space=pl.ANY),
            pl.BlockSpec(memory_space=pl.ANY),
            pl.BlockSpec(memory_space=pl.ANY),
        ],
        out_specs=pl.BlockSpec(memory_space=pltpu.VMEM),
        scratch_shapes=[
            pltpu.VMEM((rows, width), jnp.float32),
            pltpu.VMEM(w_gate.shape, w_gate.dtype),
            pltpu.VMEM(w_up.shape, w_up.dtype),
            pltpu.VMEM(w_down.shape, w_down.dtype),
            pltpu.VMEM((nx, nz, rows, hidden_width), jnp.bfloat16),
            pltpu.VMEM((4, nx, rows, quarter), jnp.bfloat16),
            pltpu.VMEM((4, nx, rows, quarter), jnp.bfloat16),
            pltpu.VMEM((4, rows, quarter), jnp.float32),
            pltpu.VMEM((4, rows, quarter), jnp.float32),
            pltpu.VMEM((rows, width), jnp.float32),
            pltpu.VMEM((4, 3, nx, rows, quarter), jnp.bfloat16),
            pltpu.VMEM((4, nx, rows, quarter), jnp.float32),
            pltpu.VMEM((4, 3, rows, quarter), jnp.float32),
            pltpu.SemaphoreType.DMA((3,)),
            pltpu.SemaphoreType.DMA((4, 3)),
            pltpu.SemaphoreType.DMA((4, 3)),
            pltpu.SemaphoreType.DMA((4, 3)),
            pltpu.SemaphoreType.DMA((4, 3)),
            pltpu.SemaphoreType.DMA(()),
            pltpu.SemaphoreType.DMA((groups,)),
            pltpu.SemaphoreType.DMA((groups,)),
            pltpu.VMEM((nx, nz, rows, width), slab.dtype),
            pltpu.SemaphoreType.DMA(()),
            pltpu.SemaphoreType.DMA((groups,)),
            pltpu.SemaphoreType.DMA((groups,)),
            pltpu.SemaphoreType.DMA((4, 3)),
            pltpu.SemaphoreType.DMA((4, 3)),
            pltpu.SemaphoreType.DMA((4, 3)),
            pltpu.SemaphoreType.DMA((4, 3)),
        ],
        compiler_params=pltpu.CompilerParams(
            collective_id=0, has_side_effects=True, vmem_limit_bytes=64 * 1024 * 1024
        ),
    )(columns, mix_w, slab, w_gate, w_up, w_down)


def gather_body(nsect, ny, in_ref, out_ref, local_sem, in_send, in_recv, send1, recv1, send2, recv2):
    nx, nz, rows, width = out_ref.shape
    groups = nsect * ny
    slots = rows // groups
    quarter = width // 4
    c = lax.axis_index("sect")
    y = lax.axis_index("ey")
    mx = lax.axis_index("ex")
    mz = lax.axis_index("tp")

    def dev(axis, d):
        if axis == "z":
            return (c, y, mx, lax.rem(mz + d + nz, nz))
        return (c, y, lax.rem(mx + d + nx, nx), mz)

    me_group = c * ny + y

    def peer(o):
        g = lax.rem(me_group + o, groups)
        return (g // ny, lax.rem(g, ny), mx, mz)

    mine = pl.ds(pl.multiple_of(me_group * slots, slots), slots)
    local = pltpu.make_async_copy(in_ref.at[me_group], out_ref.at[mx, mz, mine], local_sem)
    local.start()
    dispatch = []
    for o in range(1, groups):
        cp = pltpu.make_async_remote_copy(
            src_ref=in_ref.at[lax.rem(me_group + o, groups)],
            dst_ref=out_ref.at[mx, mz, mine],
            send_sem=in_send.at[o],
            recv_sem=in_recv.at[o],
            device_id=peer(o),
            device_id_type=MESH_ID,
        )
        cp.start()
        dispatch.append(cp)
    local.wait()
    for cp in dispatch:
        cp.wait_recv()

    rings = [("z", 1), ("z", -1), ("x", 1), ("x", -1)]

    def cols(r):
        return pl.ds(r * quarter, quarter)

    def block(axis, r, k):
        if axis == "z":
            return out_ref.at[mx, k, :, cols(r)]
        return out_ref.at[k, mz, :, cols(r)]

    def plane_block(axis, r, k):
        if axis == "x":
            return out_ref.at[k, :, :, cols(r)]
        return out_ref.at[:, k, :, cols(r)]

    def me_on(axis):
        return mz if axis == "z" else mx

    def both_sides(axis_of, view, send, recv):
        copies = []
        first = {}
        for r in range(4):
            axis, d = axis_of(r), rings[r][1]
            me = me_on(axis)
            src = view(axis, r, me)
            for side, sign in ((0, d), (1, -d)):
                cp = pltpu.make_async_remote_copy(
                    src_ref=src, dst_ref=src, send_sem=send.at[r, side], recv_sem=recv.at[r, side],
                    device_id=dev(axis, sign), device_id_type=MESH_ID,
                )
                cp.start()
                first[(r, side)] = cp
                copies.append(cp)
        later = {}
        for r in range(4):
            axis, d = axis_of(r), rings[r][1]
            n = nz if axis == "z" else nx
            first[(r, 1)].wait_recv()
            passing = view(axis, r, lax.rem(me_on(axis) + n + d, n))
            cp = pltpu.make_async_remote_copy(
                src_ref=passing, dst_ref=passing, send_sem=send.at[r, 2], recv_sem=recv.at[r, 2],
                device_id=dev(axis, -d), device_id_type=MESH_ID,
            )
            cp.start()
            later[r] = cp
            copies.append(cp)
        for r in range(4):
            first[(r, 0)].wait_recv()
            later[r].wait_recv()
        return copies

    copies1 = both_sides(lambda r: rings[r][0], block, send1, recv1)

    def second(r):
        return "x" if rings[r][0] == "z" else "z"

    copies2 = both_sides(second, plane_block, send2, recv2)
    for cp in copies1 + copies2 + dispatch:
        cp.wait_send()


ALL = ("sect", "ey", "ex", "tp")
EXPERT_AXES = ("sect", "ey")
PLANE_AXES = ("ex", "tp")


def place_slots(ids_block, experts):
    flat_ids = ids_block.reshape(-1)
    hits_mask = (flat_ids[:, None] == jnp.arange(experts, dtype=jnp.int32)[None, :]).astype(
        jnp.int32
    )
    earlier = jnp.cumsum(hits_mask, axis=0) - hits_mask
    slot_rank = jnp.sum(earlier * hits_mask, axis=1)
    return (flat_ids, slot_rank)


def per_device(tokens, router_logits, expert_ids, w_gate, w_up, w_down):
    experts_all = lax.axis_size(EXPERT_AXES)
    plane_count = lax.axis_size(PLANE_AXES)
    token_count = tokens.shape[0]
    capacity = min(token_count, 4 * token_count // experts_all)
    model_width = tokens.shape[1]
    flat_ids, slot_rank = place_slots(expert_ids, experts_all)
    columns = flat_ids * capacity + slot_rank
    positions = jnp.arange(experts_all * capacity, dtype=jnp.int32)
    picker = (positions[:, None] == columns[None, :]).astype(jnp.bfloat16)
    repeated = jnp.repeat(tokens, 2, axis=0)
    slab = jnp.dot(picker, repeated, preferred_element_type=jnp.float32).astype(jnp.bfloat16)
    slab = slab.reshape(experts_all, capacity, model_width)
    nx = lax.axis_size("ex")
    weights = jax.nn.sigmoid(router_logits - router_logits[:, ::-1]).reshape(-1)
    return expert_reduce_scatter(
        columns.astype(jnp.int32),
        weights,
        slab,
        w_gate[0],
        w_up[0],
        w_down[0],
        lax.axis_size("sect"),
        lax.axis_size("ey"),
        nx,
        plane_count // nx,
    )


def x_extent(devices):
    coords = [getattr(d, "coords", None) for d in devices.flat]
    if all(c is not None for c in coords):
        return len({c[0] for c in coords})
    return int(round(np.sqrt(devices.shape[1])))


def solution(mesh):
    devices = mesh.devices
    sect, exp, tp = devices.shape
    ex = x_extent(devices)
    fine = Mesh(devices.reshape(sect, exp // ex, ex, tp), ALL)
    in_specs = (
        P(ALL, None),
        P(ALL, None),
        P(ALL, None),
        P(EXPERT_AXES + PLANE_AXES[:1], None, "tp"),
        P(EXPERT_AXES + PLANE_AXES[:1], None, "tp"),
        P(EXPERT_AXES + PLANE_AXES[:1], "tp", None),
    )
    out_specs = P(ALL, None)
    return jax.shard_map(
        per_device, mesh=fine, in_specs=in_specs, out_specs=out_specs, check_vma=False
    )
```

```python
import functools

import jax
import jax.numpy as jnp
import numpy as np
from jax import lax
from jax.experimental import pallas as pl
from jax.experimental.pallas import tpu as pltpu
from jax.sharding import Mesh
from jax.sharding import PartitionSpec as P

MESH_ID = pl.DeviceIdType.MESH


def rs_kernel(
    nsect, ny, col_ref, logits_ref, slab_ref, wg_hbm, wu_hbm, wd_hbm, mix_ref,
    out_ref, wg, wu, wd, hid, stage, stage_f1, stage2_d, stage2_f, fin, s1, total1, s2, wsem, send1, recv1, send2, recv2, local_sem, ret_send, ret_recv,
    rows_ref, g_local, g_in_send, g_in_recv, g_send1, g_recv1, g_send2, g_recv2,
):
    nx, nz, rows, width = rows_ref.shape
    hidden_width = wd.shape[0]
    quarter = width // 4
    groups = nsect * ny
    slots = rows // groups
    c = lax.axis_index("sect")
    y = lax.axis_index("ey")
    mx = lax.axis_index("ex")
    mz = lax.axis_index("tp")

    weight_copies = [
        pltpu.make_async_copy(src, dst, wsem.at[i])
        for i, (src, dst) in enumerate(((wg_hbm, wg), (wu_hbm, wu), (wd_hbm, wd)))
    ]
    for cp in weight_copies:
        cp.start()

    def dev(axis, d):
        if axis == "z":
            return (c, y, mx, lax.rem(mz + d + nz, nz))
        return (c, y, lax.rem(mx + d + nx, nx), mz)

    me_group = c * ny + y

    def peer(o):
        g = lax.rem(me_group + o, groups)
        return (g // ny, lax.rem(g, ny), mx, mz)

    barrier = pltpu.get_barrier_semaphore()
    for axis in ("x", "z"):
        for d in (1, -1):
            pl.semaphore_signal(barrier, inc=1, device_id=dev(axis, d), device_id_type=MESH_ID)
    for o in range(1, groups):
        pl.semaphore_signal(barrier, inc=1, device_id=peer(o), device_id_type=MESH_ID)
    pl.semaphore_wait(barrier, 4 + groups - 1)

    gather_body(
        nsect, ny, slab_ref, rows_ref, g_local, g_in_send, g_in_recv, g_send1, g_recv1, g_send2, g_recv2
    )
    weight_copies[0].wait()
    weight_copies[1].wait()

    def hidden_group(i, carry):
        block = rows_ref[i].reshape(nz * rows, width)
        gate = jnp.dot(block, wg[...], preferred_element_type=jnp.float32)
        up = jnp.dot(block, wu[...], preferred_element_type=jnp.float32)
        act = (jax.nn.silu(gate) * up).astype(hid.dtype)
        hid[i] = act.reshape(nz, rows, hidden_width)
        return carry

    lax.fori_loop(0, nx, hidden_group, 0)
    weight_copies[2].wait()

    rings = [("z", 1), ("z", -1), ("x", 1), ("x", -1)]

    def me_on(axis):
        return mz if axis == "z" else mx

    def size_on(axis):
        return nz if axis == "z" else nx

    def cols(r):
        return pl.ds(r * quarter, quarter)

    def chunk(r, j):
        if rings[r][0] == "z":
            h = hid[:, j]
        else:
            h = hid[j]
        lead = h.shape[0]
        part = jnp.dot(
            h.reshape(lead * rows, hidden_width), wd[:, cols(r)], preferred_element_type=jnp.float32
        )
        return part.reshape(lead, rows, quarter)

    def other(axis):
        return "x" if axis == "z" else "z"

    def both_sides(axis_of, own, stage_d, stage_f, recv_d, recv_f, recv_s, send, recv, finish):
        copies = []
        pending = {}
        for r in range(4):
            axis, d = axis_of(r), rings[r][1]
            n = size_on(axis)
            me = me_on(axis)
            stage_d[r] = own(r, lax.rem(me + n + d, n)).astype(stage_d.dtype)
            direct = pltpu.make_async_remote_copy(
                src_ref=stage_d.at[r], dst_ref=recv_d.at[r], send_sem=send.at[r, 0],
                recv_sem=recv.at[r, 0], device_id=dev(axis, d), device_id_type=MESH_ID,
            )
            direct.start()
            stage_f[r] = own(r, lax.rem(me + 2 * n - 2 * d, n)).astype(stage_f.dtype)
            forward = pltpu.make_async_remote_copy(
                src_ref=stage_f.at[r], dst_ref=recv_f.at[r], send_sem=send.at[r, 1],
                recv_sem=recv.at[r, 1], device_id=dev(axis, -d), device_id_type=MESH_ID,
            )
            forward.start()
            pending[r] = (direct, forward)
            copies += [direct, forward]
        for r in range(4):
            axis, d = axis_of(r), rings[r][1]
            n = size_on(axis)
            me = me_on(axis)
            term = own(r, lax.rem(me + n - d, n))
            pending[r][1].wait_recv()
            recv_f[r] = (recv_f[r].astype(jnp.float32) + term).astype(recv_f.dtype)
            second = pltpu.make_async_remote_copy(
                src_ref=recv_f.at[r], dst_ref=recv_s.at[r], send_sem=send.at[r, 2],
                recv_sem=recv.at[r, 2], device_id=dev(axis, -d), device_id_type=MESH_ID,
            )
            second.start()
            pending[r] = (pending[r][0], second)
            copies.append(second)
        for r in range(4):
            axis = axis_of(r)
            term = own(r, me_on(axis))
            pending[r][0].wait_recv()
            pending[r][1].wait_recv()
            finish(r, term + recv_d[r].astype(jnp.float32) + recv_s[r].astype(jnp.float32))
        return copies

    def keep_total1(r, value):
        total1[r] = value

    copies1 = both_sides(
        lambda r: rings[r][0], chunk, stage, stage_f1, s1.at[:, 0], s1.at[:, 1], s1.at[:, 2],
        send1, recv1, keep_total1,
    )

    def other_axis(r):
        return other(rings[r][0])

    def keep_fin(r, value):
        fin[:, cols(r)] = value

    copies2 = both_sides(
        other_axis, lambda r, j: total1[r, j], stage2_d, stage2_f, s2.at[:, 0], s2.at[:, 1], s2.at[:, 2],
        send2, recv2, keep_fin,
    )

    mine = pl.ds(pl.multiple_of(me_group * slots, slots), slots)
    local = pltpu.make_async_copy(fin.at[mine], out_ref.at[mine], local_sem)
    local.start()
    returns = []
    for o in range(1, groups):
        g = lax.rem(me_group + o, groups)
        cp = pltpu.make_async_remote_copy(
            src_ref=fin.at[pl.ds(pl.multiple_of(g * slots, slots), slots)],
            dst_ref=out_ref.at[mine],
            send_sem=ret_send.at[o],
            recv_sem=ret_recv.at[o],
            device_id=peer(o),
            device_id_type=MESH_ID,
        )
        cp.start()
        returns.append(cp)
    local.wait()
    for cp in returns:
        cp.wait_recv()
    logits = logits_ref[...]
    gap = logits[:, 1:2] - logits[:, 0:1]
    w_first = 1.0 / (1.0 + jnp.exp(gap))
    w_second = 1.0 / (1.0 + jnp.exp(-gap))
    for t in range(mix_ref.shape[0]):
        first = out_ref[pl.ds(col_ref[2 * t], 1), :]
        second = out_ref[pl.ds(col_ref[2 * t + 1], 1), :]
        mix = w_first[t : t + 1] * first + w_second[t : t + 1] * second
        mix_ref[pl.ds(t, 1), :] = mix.astype(mix_ref.dtype)
    for cp in copies1 + copies2 + returns:
        cp.wait_send()


def expert_reduce_scatter(columns, logits, slab, w_gate, w_up, w_down, nsect, ny, nx, nz):
    rows, width = slab.shape
    groups = nsect * ny
    hidden_width = w_down.shape[0]
    quarter = width // 4
    return pl.pallas_call(
        functools.partial(rs_kernel, nsect, ny),
        out_shape=jax.ShapeDtypeStruct((columns.shape[0] // 2, width), jnp.bfloat16),
        in_specs=[
            pl.BlockSpec(memory_space=pltpu.SMEM),
            pl.BlockSpec(memory_space=pltpu.VMEM),
            pl.BlockSpec(memory_space=pltpu.VMEM),
            pl.BlockSpec(memory_space=pl.ANY),
            pl.BlockSpec(memory_space=pl.ANY),
            pl.BlockSpec(memory_space=pl.ANY),
        ],
        out_specs=pl.BlockSpec(memory_space=pltpu.VMEM),
        scratch_shapes=[
            pltpu.VMEM((rows, width), jnp.float32),
            pltpu.VMEM(w_gate.shape, w_gate.dtype),
            pltpu.VMEM(w_up.shape, w_up.dtype),
            pltpu.VMEM(w_down.shape, w_down.dtype),
            pltpu.VMEM((nx, nz, rows, hidden_width), jnp.bfloat16),
            pltpu.VMEM((4, nx, rows, quarter), jnp.bfloat16),
            pltpu.VMEM((4, nx, rows, quarter), jnp.bfloat16),
            pltpu.VMEM((4, rows, quarter), jnp.float32),
            pltpu.VMEM((4, rows, quarter), jnp.float32),
            pltpu.VMEM((rows, width), jnp.float32),
            pltpu.VMEM((4, 3, nx, rows, quarter), jnp.bfloat16),
            pltpu.VMEM((4, nx, rows, quarter), jnp.float32),
            pltpu.VMEM((4, 3, rows, quarter), jnp.float32),
            pltpu.SemaphoreType.DMA((3,)),
            pltpu.SemaphoreType.DMA((4, 3)),
            pltpu.SemaphoreType.DMA((4, 3)),
            pltpu.SemaphoreType.DMA((4, 3)),
            pltpu.SemaphoreType.DMA((4, 3)),
            pltpu.SemaphoreType.DMA(()),
            pltpu.SemaphoreType.DMA((groups,)),
            pltpu.SemaphoreType.DMA((groups,)),
            pltpu.VMEM((nx, nz, rows, width), slab.dtype),
            pltpu.SemaphoreType.DMA(()),
            pltpu.SemaphoreType.DMA((groups,)),
            pltpu.SemaphoreType.DMA((groups,)),
            pltpu.SemaphoreType.DMA((4, 3)),
            pltpu.SemaphoreType.DMA((4, 3)),
            pltpu.SemaphoreType.DMA((4, 3)),
            pltpu.SemaphoreType.DMA((4, 3)),
        ],
        compiler_params=pltpu.CompilerParams(
            collective_id=0, has_side_effects=True, vmem_limit_bytes=64 * 1024 * 1024
        ),
    )(columns, logits, slab, w_gate, w_up, w_down)


def gather_body(nsect, ny, in_ref, out_ref, local_sem, in_send, in_recv, send1, recv1, send2, recv2):
    nx, nz, rows, width = out_ref.shape
    groups = nsect * ny
    slots = rows // groups
    quarter = width // 4
    c = lax.axis_index("sect")
    y = lax.axis_index("ey")
    mx = lax.axis_index("ex")
    mz = lax.axis_index("tp")

    def dev(axis, d):
        if axis == "z":
            return (c, y, mx, lax.rem(mz + d + nz, nz))
        return (c, y, lax.rem(mx + d + nx, nx), mz)

    me_group = c * ny + y

    def peer(o):
        g = lax.rem(me_group + o, groups)
        return (g // ny, lax.rem(g, ny), mx, mz)

    mine = pl.ds(pl.multiple_of(me_group * slots, slots), slots)
    local = pltpu.make_async_copy(in_ref.at[mine], out_ref.at[mx, mz, mine], local_sem)
    local.start()
    dispatch = []
    for o in range(1, groups):
        cp = pltpu.make_async_remote_copy(
            src_ref=in_ref.at[pl.ds(pl.multiple_of(lax.rem(me_group + o, groups) * slots, slots), slots)],
            dst_ref=out_ref.at[mx, mz, mine],
            send_sem=in_send.at[o],
            recv_sem=in_recv.at[o],
            device_id=peer(o),
            device_id_type=MESH_ID,
        )
        cp.start()
        dispatch.append(cp)
    local.wait()
    for cp in dispatch:
        cp.wait_recv()

    rings = [("z", 1), ("z", -1), ("x", 1), ("x", -1)]

    def cols(r):
        return pl.ds(r * quarter, quarter)

    def block(axis, r, k):
        if axis == "z":
            return out_ref.at[mx, k, :, cols(r)]
        return out_ref.at[k, mz, :, cols(r)]

    def plane_block(axis, r, k):
        if axis == "x":
            return out_ref.at[k, :, :, cols(r)]
        return out_ref.at[:, k, :, cols(r)]

    def me_on(axis):
        return mz if axis == "z" else mx

    def both_sides(axis_of, view, send, recv):
        copies = []
        first = {}
        for r in range(4):
            axis, d = axis_of(r), rings[r][1]
            me = me_on(axis)
            src = view(axis, r, me)
            for side, sign in ((0, d), (1, -d)):
                cp = pltpu.make_async_remote_copy(
                    src_ref=src, dst_ref=src, send_sem=send.at[r, side], recv_sem=recv.at[r, side],
                    device_id=dev(axis, sign), device_id_type=MESH_ID,
                )
                cp.start()
                first[(r, side)] = cp
                copies.append(cp)
        later = {}
        for r in range(4):
            axis, d = axis_of(r), rings[r][1]
            n = nz if axis == "z" else nx
            first[(r, 1)].wait_recv()
            passing = view(axis, r, lax.rem(me_on(axis) + n + d, n))
            cp = pltpu.make_async_remote_copy(
                src_ref=passing, dst_ref=passing, send_sem=send.at[r, 2], recv_sem=recv.at[r, 2],
                device_id=dev(axis, -d), device_id_type=MESH_ID,
            )
            cp.start()
            later[r] = cp
            copies.append(cp)
        for r in range(4):
            first[(r, 0)].wait_recv()
            later[r].wait_recv()
        return copies

    copies1 = both_sides(lambda r: rings[r][0], block, send1, recv1)

    def second(r):
        return "x" if rings[r][0] == "z" else "z"

    copies2 = both_sides(second, plane_block, send2, recv2)
    for cp in copies1 + copies2 + dispatch:
        cp.wait_send()


ALL = ("sect", "ey", "ex", "tp")
EXPERT_AXES = ("sect", "ey")
PLANE_AXES = ("ex", "tp")


def place_slots(ids_block, experts):
    flat_ids = ids_block.reshape(-1)
    hits_mask = (flat_ids[:, None] == jnp.arange(experts, dtype=jnp.int32)[None, :]).astype(
        jnp.int32
    )
    earlier = jnp.cumsum(hits_mask, axis=0) - hits_mask
    slot_rank = jnp.sum(earlier * hits_mask, axis=1)
    return (flat_ids, slot_rank)


def per_device(tokens, router_logits, expert_ids, w_gate, w_up, w_down):
    experts_all = lax.axis_size(EXPERT_AXES)
    plane_count = lax.axis_size(PLANE_AXES)
    token_count = tokens.shape[0]
    capacity = min(token_count, 4 * token_count // experts_all)
    model_width = tokens.shape[1]
    flat_ids, slot_rank = place_slots(expert_ids, experts_all)
    columns = flat_ids * capacity + slot_rank
    positions = jnp.arange(experts_all * capacity, dtype=jnp.int32)
    picker = (positions[:, None] == columns[None, :]).astype(jnp.bfloat16)
    repeated = jnp.repeat(tokens, 2, axis=0)
    slab = jnp.dot(picker, repeated, preferred_element_type=jnp.float32).astype(jnp.bfloat16)
    nx = lax.axis_size("ex")
    return expert_reduce_scatter(
        columns.astype(jnp.int32),
        router_logits,
        slab,
        w_gate[0],
        w_up[0],
        w_down[0],
        lax.axis_size("sect"),
        lax.axis_size("ey"),
        nx,
        plane_count // nx,
    )


def x_extent(devices):
    coords = [getattr(d, "coords", None) for d in devices.flat]
    if all(c is not None for c in coords):
        return len({c[0] for c in coords})
    return int(round(np.sqrt(devices.shape[1])))


def solution(mesh):
    devices = mesh.devices
    sect, exp, tp = devices.shape
    ex = x_extent(devices)
    fine = Mesh(devices.reshape(sect, exp // ex, ex, tp), ALL)
    in_specs = (
        P(ALL, None),
        P(ALL, None),
        P(ALL, None),
        P(EXPERT_AXES + PLANE_AXES[:1], None, "tp"),
        P(EXPERT_AXES + PLANE_AXES[:1], None, "tp"),
        P(EXPERT_AXES + PLANE_AXES[:1], "tp", None),
    )
    out_specs = P(ALL, None)
    return jax.shard_map(
        per_device, mesh=fine, in_specs=in_specs, out_specs=out_specs, check_vma=False
    )
```

```python
import functools

import jax
import jax.numpy as jnp
import numpy as np
from jax import lax
from jax.experimental import pallas as pl
from jax.experimental.pallas import tpu as pltpu
from jax.sharding import Mesh
from jax.sharding import PartitionSpec as P

MESH_ID = pl.DeviceIdType.MESH


def rs_kernel(
    nsect, ny, col_ref, logits_ref, slab_ref, wg_hbm, wu_hbm, wd_hbm, mix_ref,
    out_ref, wg, wu, wd, hid, stage, stage_f1, stage2_d, stage2_f, fin, s1, total1, s2, wsem, send1, recv1, send2, recv2, local_sem, ret_send, ret_recv,
    rows_ref, g_local, g_in_send, g_in_recv, g_send1, g_recv1, g_send2, g_recv2,
):
    nx, nz, rows, width = rows_ref.shape
    hidden_width = wd.shape[0]
    quarter = width // 4
    groups = nsect * ny
    slots = rows // groups
    c = lax.axis_index("sect")
    y = lax.axis_index("ey")
    mx = lax.axis_index("ex")
    mz = lax.axis_index("tp")

    weight_copies = [
        pltpu.make_async_copy(src, dst, wsem.at[i])
        for i, (src, dst) in enumerate(((wg_hbm, wg), (wu_hbm, wu), (wd_hbm, wd)))
    ]
    for cp in weight_copies:
        cp.start()

    def dev(axis, d):
        if axis == "z":
            return (c, y, mx, lax.rem(mz + d + nz, nz))
        return (c, y, lax.rem(mx + d + nx, nx), mz)

    me_group = c * ny + y

    def peer(o):
        g = lax.rem(me_group + o, groups)
        return (g // ny, lax.rem(g, ny), mx, mz)

    barrier = pltpu.get_barrier_semaphore()
    for axis in ("x", "z"):
        for d in (1, -1):
            pl.semaphore_signal(barrier, inc=1, device_id=dev(axis, d), device_id_type=MESH_ID)
    for o in range(1, groups):
        pl.semaphore_signal(barrier, inc=1, device_id=peer(o), device_id_type=MESH_ID)
    pl.semaphore_wait(barrier, 4 + groups - 1)

    gather_body(
        nsect, ny, slab_ref, rows_ref, g_local, g_in_send, g_in_recv, g_send1, g_recv1, g_send2, g_recv2
    )
    weight_copies[0].wait()
    weight_copies[1].wait()

    def hidden_group(i, carry):
        block = rows_ref[i].reshape(nz * rows, width)
        gate = jnp.dot(block, wg[...], preferred_element_type=jnp.float32)
        up = jnp.dot(block, wu[...], preferred_element_type=jnp.float32)
        act = (jax.nn.silu(gate) * up).astype(hid.dtype)
        hid[i] = act.reshape(nz, rows, hidden_width)
        return carry

    lax.fori_loop(0, nx, hidden_group, 0)
    weight_copies[2].wait()

    rings = [("z", 1), ("z", -1), ("x", 1), ("x", -1)]

    def me_on(axis):
        return mz if axis == "z" else mx

    def size_on(axis):
        return nz if axis == "z" else nx

    def cols(r):
        return pl.ds(r * quarter, quarter)

    def chunk(r, j):
        if rings[r][0] == "z":
            h = hid[:, j]
        else:
            h = hid[j]
        lead = h.shape[0]
        part = jnp.dot(
            h.reshape(lead * rows, hidden_width), wd[:, cols(r)], preferred_element_type=jnp.float32
        )
        return part.reshape(lead, rows, quarter)

    def other(axis):
        return "x" if axis == "z" else "z"

    def both_sides(axis_of, own, stage_d, stage_f, recv_d, recv_f, recv_s, send, recv, finish):
        copies = []
        pending = {}
        for r in range(4):
            axis, d = axis_of(r), rings[r][1]
            n = size_on(axis)
            me = me_on(axis)
            stage_d[r] = own(r, lax.rem(me + n + d, n)).astype(stage_d.dtype)
            direct = pltpu.make_async_remote_copy(
                src_ref=stage_d.at[r], dst_ref=recv_d.at[r], send_sem=send.at[r, 0],
                recv_sem=recv.at[r, 0], device_id=dev(axis, d), device_id_type=MESH_ID,
            )
            direct.start()
            stage_f[r] = own(r, lax.rem(me + 2 * n - 2 * d, n)).astype(stage_f.dtype)
            forward = pltpu.make_async_remote_copy(
                src_ref=stage_f.at[r], dst_ref=recv_f.at[r], send_sem=send.at[r, 1],
                recv_sem=recv.at[r, 1], device_id=dev(axis, -d), device_id_type=MESH_ID,
            )
            forward.start()
            pending[r] = (direct, forward)
            copies += [direct, forward]
        for r in range(4):
            axis, d = axis_of(r), rings[r][1]
            n = size_on(axis)
            me = me_on(axis)
            term = own(r, lax.rem(me + n - d, n))
            pending[r][1].wait_recv()
            recv_f[r] = (recv_f[r].astype(jnp.float32) + term).astype(recv_f.dtype)
            second = pltpu.make_async_remote_copy(
                src_ref=recv_f.at[r], dst_ref=recv_s.at[r], send_sem=send.at[r, 2],
                recv_sem=recv.at[r, 2], device_id=dev(axis, -d), device_id_type=MESH_ID,
            )
            second.start()
            pending[r] = (pending[r][0], second)
            copies.append(second)
        for r in range(4):
            axis = axis_of(r)
            term = own(r, me_on(axis))
            pending[r][0].wait_recv()
            pending[r][1].wait_recv()
            finish(r, term + recv_d[r].astype(jnp.float32) + recv_s[r].astype(jnp.float32))
        return copies

    def keep_total1(r, value):
        total1[r] = value

    copies1 = both_sides(
        lambda r: rings[r][0], chunk, stage, stage_f1, s1.at[:, 0], s1.at[:, 1], s1.at[:, 2],
        send1, recv1, keep_total1,
    )

    def other_axis(r):
        return other(rings[r][0])

    mine = pl.ds(pl.multiple_of(me_group * slots, slots), slots)
    returns = []
    locals_ = []

    def keep_fin(r, value):
        fin[:, cols(r)] = value
        local = pltpu.make_async_copy(fin.at[mine, cols(r)], out_ref.at[mine, cols(r)], local_sem.at[r])
        local.start()
        locals_.append(local)
        for o in range(1, groups):
            g = lax.rem(me_group + o, groups)
            cp = pltpu.make_async_remote_copy(
                src_ref=fin.at[pl.ds(pl.multiple_of(g * slots, slots), slots), cols(r)],
                dst_ref=out_ref.at[mine, cols(r)],
                send_sem=ret_send.at[o, r],
                recv_sem=ret_recv.at[o, r],
                device_id=peer(o),
                device_id_type=MESH_ID,
            )
            cp.start()
            returns.append(cp)

    copies2 = both_sides(
        other_axis, lambda r, j: total1[r, j], stage2_d, stage2_f, s2.at[:, 0], s2.at[:, 1], s2.at[:, 2],
        send2, recv2, keep_fin,
    )

    for local in locals_:
        local.wait()
    for cp in returns:
        cp.wait_recv()
    logits = logits_ref[...]
    gap = logits[:, 1:2] - logits[:, 0:1]
    w_first = 1.0 / (1.0 + jnp.exp(gap))
    w_second = 1.0 / (1.0 + jnp.exp(-gap))
    for t in range(mix_ref.shape[0]):
        first = out_ref[pl.ds(col_ref[2 * t], 1), :]
        second = out_ref[pl.ds(col_ref[2 * t + 1], 1), :]
        mix = w_first[t : t + 1] * first + w_second[t : t + 1] * second
        mix_ref[pl.ds(t, 1), :] = mix.astype(mix_ref.dtype)
    for cp in copies1 + copies2 + returns:
        cp.wait_send()


def expert_reduce_scatter(columns, logits, slab, w_gate, w_up, w_down, nsect, ny, nx, nz):
    rows, width = slab.shape
    groups = nsect * ny
    hidden_width = w_down.shape[0]
    quarter = width // 4
    return pl.pallas_call(
        functools.partial(rs_kernel, nsect, ny),
        out_shape=jax.ShapeDtypeStruct((columns.shape[0] // 2, width), jnp.bfloat16),
        in_specs=[
            pl.BlockSpec(memory_space=pltpu.SMEM),
            pl.BlockSpec(memory_space=pltpu.VMEM),
            pl.BlockSpec(memory_space=pltpu.VMEM),
            pl.BlockSpec(memory_space=pl.ANY),
            pl.BlockSpec(memory_space=pl.ANY),
            pl.BlockSpec(memory_space=pl.ANY),
        ],
        out_specs=pl.BlockSpec(memory_space=pltpu.VMEM),
        scratch_shapes=[
            pltpu.VMEM((rows, width), jnp.float32),
            pltpu.VMEM(w_gate.shape, w_gate.dtype),
            pltpu.VMEM(w_up.shape, w_up.dtype),
            pltpu.VMEM(w_down.shape, w_down.dtype),
            pltpu.VMEM((nx, nz, rows, hidden_width), jnp.bfloat16),
            pltpu.VMEM((4, nx, rows, quarter), jnp.bfloat16),
            pltpu.VMEM((4, nx, rows, quarter), jnp.bfloat16),
            pltpu.VMEM((4, rows, quarter), jnp.float32),
            pltpu.VMEM((4, rows, quarter), jnp.float32),
            pltpu.VMEM((rows, width), jnp.float32),
            pltpu.VMEM((4, 3, nx, rows, quarter), jnp.bfloat16),
            pltpu.VMEM((4, nx, rows, quarter), jnp.float32),
            pltpu.VMEM((4, 3, rows, quarter), jnp.float32),
            pltpu.SemaphoreType.DMA((3,)),
            pltpu.SemaphoreType.DMA((4, 3)),
            pltpu.SemaphoreType.DMA((4, 3)),
            pltpu.SemaphoreType.DMA((4, 3)),
            pltpu.SemaphoreType.DMA((4, 3)),
            pltpu.SemaphoreType.DMA((4,)),
            pltpu.SemaphoreType.DMA((groups, 4)),
            pltpu.SemaphoreType.DMA((groups, 4)),
            pltpu.VMEM((nx, nz, rows, width), slab.dtype),
            pltpu.SemaphoreType.DMA(()),
            pltpu.SemaphoreType.DMA((groups,)),
            pltpu.SemaphoreType.DMA((groups,)),
            pltpu.SemaphoreType.DMA((4, 3)),
            pltpu.SemaphoreType.DMA((4, 3)),
            pltpu.SemaphoreType.DMA((4, 3)),
            pltpu.SemaphoreType.DMA((4, 3)),
        ],
        compiler_params=pltpu.CompilerParams(
            collective_id=0, has_side_effects=True, vmem_limit_bytes=64 * 1024 * 1024
        ),
    )(columns, logits, slab, w_gate, w_up, w_down)


def gather_body(nsect, ny, in_ref, out_ref, local_sem, in_send, in_recv, send1, recv1, send2, recv2):
    nx, nz, rows, width = out_ref.shape
    groups = nsect * ny
    slots = rows // groups
    quarter = width // 4
    c = lax.axis_index("sect")
    y = lax.axis_index("ey")
    mx = lax.axis_index("ex")
    mz = lax.axis_index("tp")

    def dev(axis, d):
        if axis == "z":
            return (c, y, mx, lax.rem(mz + d + nz, nz))
        return (c, y, lax.rem(mx + d + nx, nx), mz)

    me_group = c * ny + y

    def peer(o):
        g = lax.rem(me_group + o, groups)
        return (g // ny, lax.rem(g, ny), mx, mz)

    mine = pl.ds(pl.multiple_of(me_group * slots, slots), slots)
    local = pltpu.make_async_copy(in_ref.at[mine], out_ref.at[mx, mz, mine], local_sem)
    local.start()
    dispatch = []
    for o in range(1, groups):
        cp = pltpu.make_async_remote_copy(
            src_ref=in_ref.at[pl.ds(pl.multiple_of(lax.rem(me_group + o, groups) * slots, slots), slots)],
            dst_ref=out_ref.at[mx, mz, mine],
            send_sem=in_send.at[o],
            recv_sem=in_recv.at[o],
            device_id=peer(o),
            device_id_type=MESH_ID,
        )
        cp.start()
        dispatch.append(cp)
    local.wait()
    for cp in dispatch:
        cp.wait_recv()

    rings = [("z", 1), ("z", -1), ("x", 1), ("x", -1)]

    def cols(r):
        return pl.ds(r * quarter, quarter)

    def block(axis, r, k):
        if axis == "z":
            return out_ref.at[mx, k, :, cols(r)]
        return out_ref.at[k, mz, :, cols(r)]

    def plane_block(axis, r, k):
        if axis == "x":
            return out_ref.at[k, :, :, cols(r)]
        return out_ref.at[:, k, :, cols(r)]

    def me_on(axis):
        return mz if axis == "z" else mx

    def both_sides(axis_of, view, send, recv):
        copies = []
        first = {}
        for r in range(4):
            axis, d = axis_of(r), rings[r][1]
            me = me_on(axis)
            src = view(axis, r, me)
            for side, sign in ((0, d), (1, -d)):
                cp = pltpu.make_async_remote_copy(
                    src_ref=src, dst_ref=src, send_sem=send.at[r, side], recv_sem=recv.at[r, side],
                    device_id=dev(axis, sign), device_id_type=MESH_ID,
                )
                cp.start()
                first[(r, side)] = cp
                copies.append(cp)
        later = {}
        for r in range(4):
            axis, d = axis_of(r), rings[r][1]
            n = nz if axis == "z" else nx
            first[(r, 1)].wait_recv()
            passing = view(axis, r, lax.rem(me_on(axis) + n + d, n))
            cp = pltpu.make_async_remote_copy(
                src_ref=passing, dst_ref=passing, send_sem=send.at[r, 2], recv_sem=recv.at[r, 2],
                device_id=dev(axis, -d), device_id_type=MESH_ID,
            )
            cp.start()
            later[r] = cp
            copies.append(cp)
        for r in range(4):
            first[(r, 0)].wait_recv()
            later[r].wait_recv()
        return copies

    copies1 = both_sides(lambda r: rings[r][0], block, send1, recv1)

    def second(r):
        return "x" if rings[r][0] == "z" else "z"

    copies2 = both_sides(second, plane_block, send2, recv2)
    for cp in copies1 + copies2 + dispatch:
        cp.wait_send()


ALL = ("sect", "ey", "ex", "tp")
EXPERT_AXES = ("sect", "ey")
PLANE_AXES = ("ex", "tp")


def place_slots(ids_block, experts):
    flat_ids = ids_block.reshape(-1)
    hits_mask = (flat_ids[:, None] == jnp.arange(experts, dtype=jnp.int32)[None, :]).astype(
        jnp.int32
    )
    earlier = jnp.cumsum(hits_mask, axis=0) - hits_mask
    slot_rank = jnp.sum(earlier * hits_mask, axis=1)
    return (flat_ids, slot_rank)


def per_device(tokens, router_logits, expert_ids, w_gate, w_up, w_down):
    experts_all = lax.axis_size(EXPERT_AXES)
    plane_count = lax.axis_size(PLANE_AXES)
    token_count = tokens.shape[0]
    capacity = min(token_count, 4 * token_count // experts_all)
    model_width = tokens.shape[1]
    flat_ids, slot_rank = place_slots(expert_ids, experts_all)
    columns = flat_ids * capacity + slot_rank
    positions = jnp.arange(experts_all * capacity, dtype=jnp.int32)
    picker = (positions[:, None] == columns[None, :]).astype(jnp.bfloat16)
    repeated = jnp.repeat(tokens, 2, axis=0)
    slab = jnp.dot(picker, repeated, preferred_element_type=jnp.float32).astype(jnp.bfloat16)
    nx = lax.axis_size("ex")
    return expert_reduce_scatter(
        columns.astype(jnp.int32),
        router_logits,
        slab,
        w_gate[0],
        w_up[0],
        w_down[0],
        lax.axis_size("sect"),
        lax.axis_size("ey"),
        nx,
        plane_count // nx,
    )


def x_extent(devices):
    coords = [getattr(d, "coords", None) for d in devices.flat]
    if all(c is not None for c in coords):
        return len({c[0] for c in coords})
    return int(round(np.sqrt(devices.shape[1])))


def solution(mesh):
    devices = mesh.devices
    sect, exp, tp = devices.shape
    ex = x_extent(devices)
    fine = Mesh(devices.reshape(sect, exp // ex, ex, tp), ALL)
    in_specs = (
        P(ALL, None),
        P(ALL, None),
        P(ALL, None),
        P(EXPERT_AXES + PLANE_AXES[:1], None, "tp"),
        P(EXPERT_AXES + PLANE_AXES[:1], None, "tp"),
        P(EXPERT_AXES + PLANE_AXES[:1], "tp", None),
    )
    out_specs = P(ALL, None)
    return jax.shard_map(
        per_device, mesh=fine, in_specs=in_specs, out_specs=out_specs, check_vma=False
    )
```

```python
import functools

import jax
import jax.numpy as jnp
import numpy as np
from jax import lax
from jax.experimental import pallas as pl
from jax.experimental.pallas import tpu as pltpu
from jax.sharding import Mesh
from jax.sharding import PartitionSpec as P

MESH_ID = pl.DeviceIdType.MESH


def rs_kernel(
    nsect, ny, col_ref, logits_ref, slab_ref, wg_hbm, wu_hbm, wd_hbm, mix_ref,
    out_ref, wg, wu, wd, hid, stage, stage_f1, stage2_d, stage2_f, fin, s1, total1, s2, wsem, send1, recv1, send2, recv2, local_sem, ret_send, ret_recv,
    rows_ref, g_local, g_in_send, g_in_recv, g_send1, g_recv1, g_send2, g_recv2,
):
    nx, nz, rows, width = rows_ref.shape
    hidden_width = wd.shape[0]
    quarter = width // 4
    groups = nsect * ny
    slots = rows // groups
    c = lax.axis_index("sect")
    y = lax.axis_index("ey")
    mx = lax.axis_index("ex")
    mz = lax.axis_index("tp")

    weight_copies = [
        pltpu.make_async_copy(src, dst, wsem.at[i])
        for i, (src, dst) in enumerate(((wg_hbm, wg), (wu_hbm, wu), (wd_hbm, wd)))
    ]
    for cp in weight_copies:
        cp.start()

    def dev(axis, d):
        if axis == "z":
            return (c, y, mx, lax.rem(mz + d + nz, nz))
        return (c, y, lax.rem(mx + d + nx, nx), mz)

    me_group = c * ny + y

    def peer(o):
        g = lax.rem(me_group + o, groups)
        return (g // ny, lax.rem(g, ny), mx, mz)

    barrier = pltpu.get_barrier_semaphore()
    for axis in ("x", "z"):
        for d in (1, -1):
            pl.semaphore_signal(barrier, inc=1, device_id=dev(axis, d), device_id_type=MESH_ID)
    for o in range(1, groups):
        pl.semaphore_signal(barrier, inc=1, device_id=peer(o), device_id_type=MESH_ID)
    pl.semaphore_wait(barrier, 4 + groups - 1)

    gather_body(
        nsect, ny, slab_ref, rows_ref, g_local, g_in_send, g_in_recv, g_send1, g_recv1, g_send2, g_recv2
    )
    weight_copies[0].wait()
    weight_copies[1].wait()

    pair = 2 if nx % 2 == 0 else 1

    def hidden_group(i, carry):
        lead = pl.ds(pl.multiple_of(i * pair, pair), pair)
        block = rows_ref[lead].reshape(pair * nz * rows, width)
        gate = jnp.dot(block, wg[...], preferred_element_type=jnp.float32)
        up = jnp.dot(block, wu[...], preferred_element_type=jnp.float32)
        act = (jax.nn.silu(gate) * up).astype(hid.dtype)
        hid[lead] = act.reshape(pair, nz, rows, hidden_width)
        return carry

    lax.fori_loop(0, nx // pair, hidden_group, 0)
    weight_copies[2].wait()

    rings = [("z", 1), ("z", -1), ("x", 1), ("x", -1)]

    def me_on(axis):
        return mz if axis == "z" else mx

    def size_on(axis):
        return nz if axis == "z" else nx

    def cols(r):
        return pl.ds(r * quarter, quarter)

    def chunk(r, j):
        if rings[r][0] == "z":
            h = hid[:, j]
        else:
            h = hid[j]
        lead = h.shape[0]
        part = jnp.dot(
            h.reshape(lead * rows, hidden_width), wd[:, cols(r)], preferred_element_type=jnp.float32
        )
        return part.reshape(lead, rows, quarter)

    def other(axis):
        return "x" if axis == "z" else "z"

    def both_sides(axis_of, own, stage_d, stage_f, recv_d, recv_f, recv_s, send, recv, finish):
        copies = []
        pending = {}
        for r in range(4):
            axis, d = axis_of(r), rings[r][1]
            n = size_on(axis)
            me = me_on(axis)
            stage_d[r] = own(r, lax.rem(me + n + d, n)).astype(stage_d.dtype)
            direct = pltpu.make_async_remote_copy(
                src_ref=stage_d.at[r], dst_ref=recv_d.at[r], send_sem=send.at[r, 0],
                recv_sem=recv.at[r, 0], device_id=dev(axis, d), device_id_type=MESH_ID,
            )
            direct.start()
            stage_f[r] = own(r, lax.rem(me + 2 * n - 2 * d, n)).astype(stage_f.dtype)
            forward = pltpu.make_async_remote_copy(
                src_ref=stage_f.at[r], dst_ref=recv_f.at[r], send_sem=send.at[r, 1],
                recv_sem=recv.at[r, 1], device_id=dev(axis, -d), device_id_type=MESH_ID,
            )
            forward.start()
            pending[r] = (direct, forward)
            copies += [direct, forward]
        for r in range(4):
            axis, d = axis_of(r), rings[r][1]
            n = size_on(axis)
            me = me_on(axis)
            term = own(r, lax.rem(me + n - d, n))
            pending[r][1].wait_recv()
            recv_f[r] = (recv_f[r].astype(jnp.float32) + term).astype(recv_f.dtype)
            second = pltpu.make_async_remote_copy(
                src_ref=recv_f.at[r], dst_ref=recv_s.at[r], send_sem=send.at[r, 2],
                recv_sem=recv.at[r, 2], device_id=dev(axis, -d), device_id_type=MESH_ID,
            )
            second.start()
            pending[r] = (pending[r][0], second)
            copies.append(second)
        for r in range(4):
            axis = axis_of(r)
            term = own(r, me_on(axis))
            pending[r][0].wait_recv()
            pending[r][1].wait_recv()
            finish(r, term + recv_d[r].astype(jnp.float32) + recv_s[r].astype(jnp.float32))
        return copies

    def keep_total1(r, value):
        total1[r] = value

    copies1 = both_sides(
        lambda r: rings[r][0], chunk, stage, stage_f1, s1.at[:, 0], s1.at[:, 1], s1.at[:, 2],
        send1, recv1, keep_total1,
    )

    def other_axis(r):
        return other(rings[r][0])

    mine = pl.ds(pl.multiple_of(me_group * slots, slots), slots)
    returns = []
    locals_ = []

    def keep_fin(r, value):
        fin[:, cols(r)] = value
        local = pltpu.make_async_copy(fin.at[mine, cols(r)], out_ref.at[mine, cols(r)], local_sem.at[r])
        local.start()
        locals_.append(local)
        for o in range(1, groups):
            g = lax.rem(me_group + o, groups)
            cp = pltpu.make_async_remote_copy(
                src_ref=fin.at[pl.ds(pl.multiple_of(g * slots, slots), slots), cols(r)],
                dst_ref=out_ref.at[mine, cols(r)],
                send_sem=ret_send.at[o, r],
                recv_sem=ret_recv.at[o, r],
                device_id=peer(o),
                device_id_type=MESH_ID,
            )
            cp.start()
            returns.append(cp)

    copies2 = both_sides(
        other_axis, lambda r, j: total1[r, j], stage2_d, stage2_f, s2.at[:, 0], s2.at[:, 1], s2.at[:, 2],
        send2, recv2, keep_fin,
    )

    for local in locals_:
        local.wait()
    for cp in returns:
        cp.wait_recv()
    logits = logits_ref[...]
    gap = logits[:, 1:2] - logits[:, 0:1]
    w_first = 1.0 / (1.0 + jnp.exp(gap))
    w_second = 1.0 / (1.0 + jnp.exp(-gap))
    for t in range(mix_ref.shape[0]):
        first = out_ref[pl.ds(col_ref[2 * t], 1), :]
        second = out_ref[pl.ds(col_ref[2 * t + 1], 1), :]
        mix = w_first[t : t + 1] * first + w_second[t : t + 1] * second
        mix_ref[pl.ds(t, 1), :] = mix.astype(mix_ref.dtype)
    for cp in copies1 + copies2 + returns:
        cp.wait_send()


def expert_reduce_scatter(columns, logits, slab, w_gate, w_up, w_down, nsect, ny, nx, nz):
    rows, width = slab.shape
    groups = nsect * ny
    hidden_width = w_down.shape[0]
    quarter = width // 4
    return pl.pallas_call(
        functools.partial(rs_kernel, nsect, ny),
        out_shape=jax.ShapeDtypeStruct((columns.shape[0] // 2, width), jnp.bfloat16),
        in_specs=[
            pl.BlockSpec(memory_space=pltpu.SMEM),
            pl.BlockSpec(memory_space=pltpu.VMEM),
            pl.BlockSpec(memory_space=pltpu.VMEM),
            pl.BlockSpec(memory_space=pl.ANY),
            pl.BlockSpec(memory_space=pl.ANY),
            pl.BlockSpec(memory_space=pl.ANY),
        ],
        out_specs=pl.BlockSpec(memory_space=pltpu.VMEM),
        scratch_shapes=[
            pltpu.VMEM((rows, width), jnp.float32),
            pltpu.VMEM(w_gate.shape, w_gate.dtype),
            pltpu.VMEM(w_up.shape, w_up.dtype),
            pltpu.VMEM(w_down.shape, w_down.dtype),
            pltpu.VMEM((nx, nz, rows, hidden_width), jnp.bfloat16),
            pltpu.VMEM((4, nx, rows, quarter), jnp.bfloat16),
            pltpu.VMEM((4, nx, rows, quarter), jnp.bfloat16),
            pltpu.VMEM((4, rows, quarter), jnp.float32),
            pltpu.VMEM((4, rows, quarter), jnp.float32),
            pltpu.VMEM((rows, width), jnp.float32),
            pltpu.VMEM((4, 3, nx, rows, quarter), jnp.bfloat16),
            pltpu.VMEM((4, nx, rows, quarter), jnp.float32),
            pltpu.VMEM((4, 3, rows, quarter), jnp.float32),
            pltpu.SemaphoreType.DMA((3,)),
            pltpu.SemaphoreType.DMA((4, 3)),
            pltpu.SemaphoreType.DMA((4, 3)),
            pltpu.SemaphoreType.DMA((4, 3)),
            pltpu.SemaphoreType.DMA((4, 3)),
            pltpu.SemaphoreType.DMA((4,)),
            pltpu.SemaphoreType.DMA((groups, 4)),
            pltpu.SemaphoreType.DMA((groups, 4)),
            pltpu.VMEM((nx, nz, rows, width), slab.dtype),
            pltpu.SemaphoreType.DMA(()),
            pltpu.SemaphoreType.DMA((groups,)),
            pltpu.SemaphoreType.DMA((groups,)),
            pltpu.SemaphoreType.DMA((4, 3)),
            pltpu.SemaphoreType.DMA((4, 3)),
            pltpu.SemaphoreType.DMA((4, 3)),
            pltpu.SemaphoreType.DMA((4, 3)),
        ],
        compiler_params=pltpu.CompilerParams(
            collective_id=0, has_side_effects=True, vmem_limit_bytes=64 * 1024 * 1024
        ),
    )(columns, logits, slab, w_gate, w_up, w_down)


def gather_body(nsect, ny, in_ref, out_ref, local_sem, in_send, in_recv, send1, recv1, send2, recv2):
    nx, nz, rows, width = out_ref.shape
    groups = nsect * ny
    slots = rows // groups
    quarter = width // 4
    c = lax.axis_index("sect")
    y = lax.axis_index("ey")
    mx = lax.axis_index("ex")
    mz = lax.axis_index("tp")

    def dev(axis, d):
        if axis == "z":
            return (c, y, mx, lax.rem(mz + d + nz, nz))
        return (c, y, lax.rem(mx + d + nx, nx), mz)

    me_group = c * ny + y

    def peer(o):
        g = lax.rem(me_group + o, groups)
        return (g // ny, lax.rem(g, ny), mx, mz)

    mine = pl.ds(pl.multiple_of(me_group * slots, slots), slots)
    local = pltpu.make_async_copy(in_ref.at[mine], out_ref.at[mx, mz, mine], local_sem)
    local.start()
    dispatch = []
    for o in range(1, groups):
        cp = pltpu.make_async_remote_copy(
            src_ref=in_ref.at[pl.ds(pl.multiple_of(lax.rem(me_group + o, groups) * slots, slots), slots)],
            dst_ref=out_ref.at[mx, mz, mine],
            send_sem=in_send.at[o],
            recv_sem=in_recv.at[o],
            device_id=peer(o),
            device_id_type=MESH_ID,
        )
        cp.start()
        dispatch.append(cp)
    local.wait()
    for cp in dispatch:
        cp.wait_recv()

    rings = [("z", 1), ("z", -1), ("x", 1), ("x", -1)]

    def cols(r):
        return pl.ds(r * quarter, quarter)

    def block(axis, r, k):
        if axis == "z":
            return out_ref.at[mx, k, :, cols(r)]
        return out_ref.at[k, mz, :, cols(r)]

    def plane_block(axis, r, k):
        if axis == "x":
            return out_ref.at[k, :, :, cols(r)]
        return out_ref.at[:, k, :, cols(r)]

    def me_on(axis):
        return mz if axis == "z" else mx

    def both_sides(axis_of, view, send, recv):
        copies = []
        first = {}
        for r in range(4):
            axis, d = axis_of(r), rings[r][1]
            me = me_on(axis)
            src = view(axis, r, me)
            for side, sign in ((0, d), (1, -d)):
                cp = pltpu.make_async_remote_copy(
                    src_ref=src, dst_ref=src, send_sem=send.at[r, side], recv_sem=recv.at[r, side],
                    device_id=dev(axis, sign), device_id_type=MESH_ID,
                )
                cp.start()
                first[(r, side)] = cp
                copies.append(cp)
        later = {}
        for r in range(4):
            axis, d = axis_of(r), rings[r][1]
            n = nz if axis == "z" else nx
            first[(r, 1)].wait_recv()
            passing = view(axis, r, lax.rem(me_on(axis) + n + d, n))
            cp = pltpu.make_async_remote_copy(
                src_ref=passing, dst_ref=passing, send_sem=send.at[r, 2], recv_sem=recv.at[r, 2],
                device_id=dev(axis, -d), device_id_type=MESH_ID,
            )
            cp.start()
            later[r] = cp
            copies.append(cp)
        for r in range(4):
            first[(r, 0)].wait_recv()
            later[r].wait_recv()
        return copies

    copies1 = both_sides(lambda r: rings[r][0], block, send1, recv1)

    def second(r):
        return "x" if rings[r][0] == "z" else "z"

    copies2 = both_sides(second, plane_block, send2, recv2)
    for cp in copies1 + copies2 + dispatch:
        cp.wait_send()


ALL = ("sect", "ey", "ex", "tp")
EXPERT_AXES = ("sect", "ey")
PLANE_AXES = ("ex", "tp")


def place_slots(ids_block, experts):
    flat_ids = ids_block.reshape(-1)
    hits_mask = (flat_ids[:, None] == jnp.arange(experts, dtype=jnp.int32)[None, :]).astype(
        jnp.int32
    )
    earlier = jnp.cumsum(hits_mask, axis=0) - hits_mask
    slot_rank = jnp.sum(earlier * hits_mask, axis=1)
    return (flat_ids, slot_rank)


def per_device(tokens, router_logits, expert_ids, w_gate, w_up, w_down):
    experts_all = lax.axis_size(EXPERT_AXES)
    plane_count = lax.axis_size(PLANE_AXES)
    token_count = tokens.shape[0]
    capacity = min(token_count, 4 * token_count // experts_all)
    model_width = tokens.shape[1]
    flat_ids, slot_rank = place_slots(expert_ids, experts_all)
    columns = flat_ids * capacity + slot_rank
    positions = jnp.arange(experts_all * capacity, dtype=jnp.int32)
    picker = (positions[:, None] == columns[None, :]).astype(jnp.bfloat16)
    repeated = jnp.repeat(tokens, 2, axis=0)
    slab = jnp.dot(picker, repeated, preferred_element_type=jnp.float32).astype(jnp.bfloat16)
    nx = lax.axis_size("ex")
    return expert_reduce_scatter(
        columns.astype(jnp.int32),
        router_logits,
        slab,
        w_gate[0],
        w_up[0],
        w_down[0],
        lax.axis_size("sect"),
        lax.axis_size("ey"),
        nx,
        plane_count // nx,
    )


def x_extent(devices):
    coords = [getattr(d, "coords", None) for d in devices.flat]
    if all(c is not None for c in coords):
        return len({c[0] for c in coords})
    return int(round(np.sqrt(devices.shape[1])))


def solution(mesh):
    devices = mesh.devices
    sect, exp, tp = devices.shape
    ex = x_extent(devices)
    fine = Mesh(devices.reshape(sect, exp // ex, ex, tp), ALL)
    in_specs = (
        P(ALL, None),
        P(ALL, None),
        P(ALL, None),
        P(EXPERT_AXES + PLANE_AXES[:1], None, "tp"),
        P(EXPERT_AXES + PLANE_AXES[:1], None, "tp"),
        P(EXPERT_AXES + PLANE_AXES[:1], "tp", None),
    )
    out_specs = P(ALL, None)
    return jax.shard_map(
        per_device, mesh=fine, in_specs=in_specs, out_specs=out_specs, check_vma=False
    )
```

```python
import functools

import jax
import jax.numpy as jnp
import numpy as np
from jax import lax
from jax.experimental import pallas as pl
from jax.experimental.pallas import tpu as pltpu
from jax.sharding import Mesh
from jax.sharding import PartitionSpec as P

MESH_ID = pl.DeviceIdType.MESH


def rs_kernel(
    nsect, ny, col_ref, logits_ref, slab_ref, wg_hbm, wu_hbm, wd_hbm, mix_ref,
    out_ref, wg, wu, wd, hid, stage, stage_f1, stage2_d, stage2_f, fin, s1, total1, s2, wsem, send1, recv1, send2, recv2, local_sem, ret_send, ret_recv,
    rows_ref, g_local, g_in_send, g_in_recv, g_send1, g_recv1, g_send2, g_recv2,
):
    nx, nz, rows, width = rows_ref.shape
    hidden_width = wd.shape[0]
    quarter = width // 4
    groups = nsect * ny
    slots = rows // groups
    c = lax.axis_index("sect")
    y = lax.axis_index("ey")
    mx = lax.axis_index("ex")
    mz = lax.axis_index("tp")

    weight_copies = [
        pltpu.make_async_copy(src, dst, wsem.at[i])
        for i, (src, dst) in enumerate(((wg_hbm, wg), (wu_hbm, wu), (wd_hbm, wd)))
    ]
    for cp in weight_copies:
        cp.start()

    def dev(axis, d):
        if axis == "z":
            return (c, y, mx, lax.rem(mz + d + nz, nz))
        return (c, y, lax.rem(mx + d + nx, nx), mz)

    me_group = c * ny + y

    def peer(o):
        g = lax.rem(me_group + o, groups)
        return (g // ny, lax.rem(g, ny), mx, mz)

    barrier = pltpu.get_barrier_semaphore()
    for axis in ("x", "z"):
        for d in (1, -1):
            pl.semaphore_signal(barrier, inc=1, device_id=dev(axis, d), device_id_type=MESH_ID)
    for o in range(1, groups):
        pl.semaphore_signal(barrier, inc=1, device_id=peer(o), device_id_type=MESH_ID)
    pl.semaphore_wait(barrier, 4 + groups - 1)

    gather_body(
        nsect, ny, slab_ref, rows_ref, g_local, g_in_send, g_in_recv, g_send1, g_recv1, g_send2, g_recv2
    )
    weight_copies[0].wait()
    weight_copies[1].wait()

    pair = 2 if nx % 2 == 0 else 1

    def hidden_group(i, carry):
        lead = pl.ds(pl.multiple_of(i * pair, pair), pair)
        block = rows_ref[lead].reshape(pair * nz * rows, width)
        gate = jnp.dot(block, wg[...], preferred_element_type=jnp.float32)
        up = jnp.dot(block, wu[...], preferred_element_type=jnp.float32)
        act = (jax.nn.silu(gate) * up).astype(hid.dtype)
        hid[lead] = act.reshape(pair, nz, rows, hidden_width)
        return carry

    lax.fori_loop(0, nx // pair, hidden_group, 0)
    weight_copies[2].wait()

    rings = [("z", 1), ("z", -1), ("x", 1), ("x", -1)]

    def me_on(axis):
        return mz if axis == "z" else mx

    def size_on(axis):
        return nz if axis == "z" else nx

    def cols(r):
        return pl.ds(r * quarter, quarter)

    def chunk(r, j):
        if rings[r][0] == "z":
            h = hid[:, j]
        else:
            h = hid[j]
        lead = h.shape[0]
        part = jnp.dot(
            h.reshape(lead * rows, hidden_width), wd[:, cols(r)], preferred_element_type=jnp.float32
        )
        return part.reshape(lead, rows, quarter)

    def other(axis):
        return "x" if axis == "z" else "z"

    def both_sides(axis_of, own, stage_d, stage_f, recv_d, recv_f, recv_s, send, recv, finish):
        copies = []
        pending = {}
        for r in range(4):
            axis, d = axis_of(r), rings[r][1]
            n = size_on(axis)
            me = me_on(axis)
            stage_d[r] = own(r, lax.rem(me + n + d, n)).astype(stage_d.dtype)
            direct = pltpu.make_async_remote_copy(
                src_ref=stage_d.at[r], dst_ref=recv_d.at[r], send_sem=send.at[r, 0],
                recv_sem=recv.at[r, 0], device_id=dev(axis, d), device_id_type=MESH_ID,
            )
            direct.start()
            stage_f[r] = own(r, lax.rem(me + 2 * n - 2 * d, n)).astype(stage_f.dtype)
            forward = pltpu.make_async_remote_copy(
                src_ref=stage_f.at[r], dst_ref=recv_f.at[r], send_sem=send.at[r, 1],
                recv_sem=recv.at[r, 1], device_id=dev(axis, -d), device_id_type=MESH_ID,
            )
            forward.start()
            pending[r] = (direct, forward)
            copies += [direct, forward]
        for r in range(4):
            axis, d = axis_of(r), rings[r][1]
            n = size_on(axis)
            me = me_on(axis)
            term = own(r, lax.rem(me + n - d, n))
            pending[r][1].wait_recv()
            recv_f[r] = (recv_f[r].astype(jnp.float32) + term).astype(recv_f.dtype)
            second = pltpu.make_async_remote_copy(
                src_ref=recv_f.at[r], dst_ref=recv_s.at[r], send_sem=send.at[r, 2],
                recv_sem=recv.at[r, 2], device_id=dev(axis, -d), device_id_type=MESH_ID,
            )
            second.start()
            pending[r] = (pending[r][0], second)
            copies.append(second)
        for r in range(4):
            axis = axis_of(r)
            term = own(r, me_on(axis))
            pending[r][0].wait_recv()
            pending[r][1].wait_recv()
            finish(r, term + recv_d[r].astype(jnp.float32) + recv_s[r].astype(jnp.float32))
        return copies

    def keep_total1(r, value):
        total1[r] = value

    copies1 = both_sides(
        lambda r: rings[r][0], chunk, stage, stage_f1, s1.at[:, 0], s1.at[:, 1], s1.at[:, 2],
        send1, recv1, keep_total1,
    )

    def other_axis(r):
        return other(rings[r][0])

    mine = pl.ds(pl.multiple_of(me_group * slots, slots), slots)
    returns = []
    locals_ = []

    def keep_fin(r, value):
        fin[:, cols(r)] = value
        local = pltpu.make_async_copy(fin.at[mine, cols(r)], out_ref.at[mine, cols(r)], local_sem.at[r])
        local.start()
        locals_.append(local)
        for o in range(1, groups):
            g = lax.rem(me_group + o, groups)
            cp = pltpu.make_async_remote_copy(
                src_ref=fin.at[pl.ds(pl.multiple_of(g * slots, slots), slots), cols(r)],
                dst_ref=out_ref.at[mine, cols(r)],
                send_sem=ret_send.at[o, r],
                recv_sem=ret_recv.at[o, r],
                device_id=peer(o),
                device_id_type=MESH_ID,
            )
            cp.start()
            returns.append(cp)

    copies2 = both_sides(
        other_axis, lambda r, j: total1[r, j], stage2_d, stage2_f, s2.at[:, 0], s2.at[:, 1], s2.at[:, 2],
        send2, recv2, keep_fin,
    )

    for local in locals_:
        local.wait()
    for cp in returns:
        cp.wait_recv()
    for t in range(mix_ref.shape[0]):
        gap = jnp.full((1, width), logits_ref[2 * t + 1] - logits_ref[2 * t], jnp.float32)
        first = out_ref[pl.ds(col_ref[2 * t], 1), :]
        second = out_ref[pl.ds(col_ref[2 * t + 1], 1), :]
        mix = first / (1.0 + jnp.exp(gap)) + second / (1.0 + jnp.exp(-gap))
        mix_ref[pl.ds(t, 1), :] = mix.astype(mix_ref.dtype)
    for cp in copies1 + copies2 + returns:
        cp.wait_send()


def expert_reduce_scatter(columns, logits, slab, w_gate, w_up, w_down, nsect, ny, nx, nz):
    rows, width = slab.shape
    groups = nsect * ny
    hidden_width = w_down.shape[0]
    quarter = width // 4
    return pl.pallas_call(
        functools.partial(rs_kernel, nsect, ny),
        out_shape=jax.ShapeDtypeStruct((columns.shape[0] // 2, width), jnp.bfloat16),
        in_specs=[
            pl.BlockSpec(memory_space=pltpu.SMEM),
            pl.BlockSpec(memory_space=pltpu.SMEM),
            pl.BlockSpec(memory_space=pltpu.VMEM),
            pl.BlockSpec(memory_space=pl.ANY),
            pl.BlockSpec(memory_space=pl.ANY),
            pl.BlockSpec(memory_space=pl.ANY),
        ],
        out_specs=pl.BlockSpec(memory_space=pltpu.VMEM),
        scratch_shapes=[
            pltpu.VMEM((rows, width), jnp.float32),
            pltpu.VMEM(w_gate.shape, w_gate.dtype),
            pltpu.VMEM(w_up.shape, w_up.dtype),
            pltpu.VMEM(w_down.shape, w_down.dtype),
            pltpu.VMEM((nx, nz, rows, hidden_width), jnp.bfloat16),
            pltpu.VMEM((4, nx, rows, quarter), jnp.bfloat16),
            pltpu.VMEM((4, nx, rows, quarter), jnp.bfloat16),
            pltpu.VMEM((4, rows, quarter), jnp.float32),
            pltpu.VMEM((4, rows, quarter), jnp.float32),
            pltpu.VMEM((rows, width), jnp.float32),
            pltpu.VMEM((4, 3, nx, rows, quarter), jnp.bfloat16),
            pltpu.VMEM((4, nx, rows, quarter), jnp.float32),
            pltpu.VMEM((4, 3, rows, quarter), jnp.float32),
            pltpu.SemaphoreType.DMA((3,)),
            pltpu.SemaphoreType.DMA((4, 3)),
            pltpu.SemaphoreType.DMA((4, 3)),
            pltpu.SemaphoreType.DMA((4, 3)),
            pltpu.SemaphoreType.DMA((4, 3)),
            pltpu.SemaphoreType.DMA((4,)),
            pltpu.SemaphoreType.DMA((groups, 4)),
            pltpu.SemaphoreType.DMA((groups, 4)),
            pltpu.VMEM((nx, nz, rows, width), slab.dtype),
            pltpu.SemaphoreType.DMA(()),
            pltpu.SemaphoreType.DMA((groups,)),
            pltpu.SemaphoreType.DMA((groups,)),
            pltpu.SemaphoreType.DMA((4, 3)),
            pltpu.SemaphoreType.DMA((4, 3)),
            pltpu.SemaphoreType.DMA((4, 3)),
            pltpu.SemaphoreType.DMA((4, 3)),
        ],
        compiler_params=pltpu.CompilerParams(
            collective_id=0, has_side_effects=True, vmem_limit_bytes=64 * 1024 * 1024
        ),
    )(columns, logits, slab, w_gate, w_up, w_down)


def gather_body(nsect, ny, in_ref, out_ref, local_sem, in_send, in_recv, send1, recv1, send2, recv2):
    nx, nz, rows, width = out_ref.shape
    groups = nsect * ny
    slots = rows // groups
    quarter = width // 4
    c = lax.axis_index("sect")
    y = lax.axis_index("ey")
    mx = lax.axis_index("ex")
    mz = lax.axis_index("tp")

    def dev(axis, d):
        if axis == "z":
            return (c, y, mx, lax.rem(mz + d + nz, nz))
        return (c, y, lax.rem(mx + d + nx, nx), mz)

    me_group = c * ny + y

    def peer(o):
        g = lax.rem(me_group + o, groups)
        return (g // ny, lax.rem(g, ny), mx, mz)

    mine = pl.ds(pl.multiple_of(me_group * slots, slots), slots)
    local = pltpu.make_async_copy(in_ref.at[mine], out_ref.at[mx, mz, mine], local_sem)
    local.start()
    dispatch = []
    for o in range(1, groups):
        cp = pltpu.make_async_remote_copy(
            src_ref=in_ref.at[pl.ds(pl.multiple_of(lax.rem(me_group + o, groups) * slots, slots), slots)],
            dst_ref=out_ref.at[mx, mz, mine],
            send_sem=in_send.at[o],
            recv_sem=in_recv.at[o],
            device_id=peer(o),
            device_id_type=MESH_ID,
        )
        cp.start()
        dispatch.append(cp)
    local.wait()
    for cp in dispatch:
        cp.wait_recv()

    rings = [("z", 1), ("z", -1), ("x", 1), ("x", -1)]

    def cols(r):
        return pl.ds(r * quarter, quarter)

    def block(axis, r, k):
        if axis == "z":
            return out_ref.at[mx, k, :, cols(r)]
        return out_ref.at[k, mz, :, cols(r)]

    def plane_block(axis, r, k):
        if axis == "x":
            return out_ref.at[k, :, :, cols(r)]
        return out_ref.at[:, k, :, cols(r)]

    def me_on(axis):
        return mz if axis == "z" else mx

    def both_sides(axis_of, view, send, recv):
        copies = []
        first = {}
        for r in range(4):
            axis, d = axis_of(r), rings[r][1]
            me = me_on(axis)
            src = view(axis, r, me)
            for side, sign in ((0, d), (1, -d)):
                cp = pltpu.make_async_remote_copy(
                    src_ref=src, dst_ref=src, send_sem=send.at[r, side], recv_sem=recv.at[r, side],
                    device_id=dev(axis, sign), device_id_type=MESH_ID,
                )
                cp.start()
                first[(r, side)] = cp
                copies.append(cp)
        later = {}
        for r in range(4):
            axis, d = axis_of(r), rings[r][1]
            n = nz if axis == "z" else nx
            first[(r, 1)].wait_recv()
            passing = view(axis, r, lax.rem(me_on(axis) + n + d, n))
            cp = pltpu.make_async_remote_copy(
                src_ref=passing, dst_ref=passing, send_sem=send.at[r, 2], recv_sem=recv.at[r, 2],
                device_id=dev(axis, -d), device_id_type=MESH_ID,
            )
            cp.start()
            later[r] = cp
            copies.append(cp)
        for r in range(4):
            first[(r, 0)].wait_recv()
            later[r].wait_recv()
        return copies

    copies1 = both_sides(lambda r: rings[r][0], block, send1, recv1)

    def second(r):
        return "x" if rings[r][0] == "z" else "z"

    copies2 = both_sides(second, plane_block, send2, recv2)
    for cp in copies1 + copies2 + dispatch:
        cp.wait_send()


ALL = ("sect", "ey", "ex", "tp")
EXPERT_AXES = ("sect", "ey")
PLANE_AXES = ("ex", "tp")


def place_slots(ids_block, experts):
    flat_ids = ids_block.reshape(-1)
    hits_mask = (flat_ids[:, None] == jnp.arange(experts, dtype=jnp.int32)[None, :]).astype(
        jnp.int32
    )
    earlier = jnp.cumsum(hits_mask, axis=0) - hits_mask
    slot_rank = jnp.sum(earlier * hits_mask, axis=1)
    return (flat_ids, slot_rank)


def per_device(tokens, router_logits, expert_ids, w_gate, w_up, w_down):
    experts_all = lax.axis_size(EXPERT_AXES)
    plane_count = lax.axis_size(PLANE_AXES)
    token_count = tokens.shape[0]
    capacity = min(token_count, 4 * token_count // experts_all)
    model_width = tokens.shape[1]
    flat_ids, slot_rank = place_slots(expert_ids, experts_all)
    columns = flat_ids * capacity + slot_rank
    positions = jnp.arange(experts_all * capacity, dtype=jnp.int32)
    source = columns.reshape(token_count, 2)
    picker = (positions[:, None, None] == source[None, :, :]).any(axis=2).astype(jnp.bfloat16)
    slab = jnp.dot(picker, tokens, preferred_element_type=jnp.float32).astype(jnp.bfloat16)
    nx = lax.axis_size("ex")
    return expert_reduce_scatter(
        columns.astype(jnp.int32),
        router_logits.reshape(-1),
        slab,
        w_gate[0],
        w_up[0],
        w_down[0],
        lax.axis_size("sect"),
        lax.axis_size("ey"),
        nx,
        plane_count // nx,
    )


def x_extent(devices):
    coords = [getattr(d, "coords", None) for d in devices.flat]
    if all(c is not None for c in coords):
        return len({c[0] for c in coords})
    return int(round(np.sqrt(devices.shape[1])))


def solution(mesh):
    devices = mesh.devices
    sect, exp, tp = devices.shape
    ex = x_extent(devices)
    fine = Mesh(devices.reshape(sect, exp // ex, ex, tp), ALL)
    in_specs = (
        P(ALL, None),
        P(ALL, None),
        P(ALL, None),
        P(EXPERT_AXES + PLANE_AXES[:1], None, "tp"),
        P(EXPERT_AXES + PLANE_AXES[:1], None, "tp"),
        P(EXPERT_AXES + PLANE_AXES[:1], "tp", None),
    )
    out_specs = P(ALL, None)
    return jax.shard_map(
        per_device, mesh=fine, in_specs=in_specs, out_specs=out_specs, check_vma=False
    )
```

```python
import functools

import jax
import jax.numpy as jnp
import numpy as np
from jax import lax
from jax.experimental import pallas as pl
from jax.experimental.pallas import tpu as pltpu
from jax.sharding import Mesh
from jax.sharding import PartitionSpec as P

MESH_ID = pl.DeviceIdType.MESH


def rs_kernel(
    nsect, ny, col_ref, logits_ref, slab_ref, wg_hbm, wu_hbm, wd_hbm, mix_ref,
    out_ref, wg, wu, wd, hid, stage, stage_f1, stage2_d, stage2_f, fin, s1, total1, s2, wsem, send1, recv1, send2, recv2, local_sem, ret_send, ret_recv,
    rows_ref, g_local, g_in_send, g_in_recv, g_send1, g_recv1, g_send2, g_recv2,
):
    nx, nz, rows, width = rows_ref.shape
    hidden_width = wd.shape[0]
    quarter = width // 4
    groups = nsect * ny
    slots = rows // groups
    c = lax.axis_index("sect")
    y = lax.axis_index("ey")
    mx = lax.axis_index("ex")
    mz = lax.axis_index("tp")

    weight_copies = [
        pltpu.make_async_copy(src, dst, wsem.at[i])
        for i, (src, dst) in enumerate(((wg_hbm, wg), (wu_hbm, wu), (wd_hbm, wd)))
    ]
    for cp in weight_copies:
        cp.start()

    def dev(axis, d):
        if axis == "z":
            return (c, y, mx, lax.rem(mz + d + nz, nz))
        return (c, y, lax.rem(mx + d + nx, nx), mz)

    me_group = c * ny + y

    def peer(o):
        g = lax.rem(me_group + o, groups)
        return (g // ny, lax.rem(g, ny), mx, mz)

    barrier = pltpu.get_barrier_semaphore()
    for axis in ("x", "z"):
        for d in (1, -1):
            pl.semaphore_signal(barrier, inc=1, device_id=dev(axis, d), device_id_type=MESH_ID)
    for o in range(1, groups):
        pl.semaphore_signal(barrier, inc=1, device_id=peer(o), device_id_type=MESH_ID)
    pl.semaphore_wait(barrier, 4 + groups - 1)

    gather_body(
        nsect, ny, slab_ref, rows_ref, g_local, g_in_send, g_in_recv, g_send1, g_recv1, g_send2, g_recv2
    )
    weight_copies[0].wait()
    weight_copies[1].wait()

    pair = 2 if nx % 2 == 0 else 1

    def hidden_group(i, carry):
        lead = pl.ds(pl.multiple_of(i * pair, pair), pair)
        block = rows_ref[lead].reshape(pair * nz * rows, width)
        gate = jnp.dot(block, wg[...], preferred_element_type=jnp.float32)
        up = jnp.dot(block, wu[...], preferred_element_type=jnp.float32)
        act = (jax.nn.silu(gate) * up).astype(hid.dtype)
        hid[lead] = act.reshape(pair, nz, rows, hidden_width)
        return carry

    lax.fori_loop(0, nx // pair, hidden_group, 0)
    weight_copies[2].wait()

    rings = [("z", 1), ("z", -1), ("x", 1), ("x", -1)]

    def me_on(axis):
        return mz if axis == "z" else mx

    def size_on(axis):
        return nz if axis == "z" else nx

    def cols(r):
        return pl.ds(r * quarter, quarter)

    def chunk(r, j):
        if rings[r][0] == "z":
            h = hid[:, j]
        else:
            h = hid[j]
        lead = h.shape[0]
        part = jnp.dot(
            h.reshape(lead * rows, hidden_width), wd[:, cols(r)], preferred_element_type=jnp.float32
        )
        return part.reshape(lead, rows, quarter)

    def other(axis):
        return "x" if axis == "z" else "z"

    class Exchange:
        def __init__(self, axis_of, own, stage_d, stage_f, recv_d, recv_f, recv_s, send, recv, finish):
            self.axis_of, self.own = axis_of, own
            self.stage_d, self.stage_f = stage_d, stage_f
            self.recv_d, self.recv_f, self.recv_s = recv_d, recv_f, recv_s
            self.send, self.recv, self.finish = send, recv, finish
            self.copies, self.pending = [], {}

        def begin(self, r):
            axis, d = self.axis_of(r), rings[r][1]
            n = size_on(axis)
            me = me_on(axis)
            self.stage_d[r] = self.own(r, lax.rem(me + n + d, n)).astype(self.stage_d.dtype)
            direct = pltpu.make_async_remote_copy(
                src_ref=self.stage_d.at[r], dst_ref=self.recv_d.at[r], send_sem=self.send.at[r, 0],
                recv_sem=self.recv.at[r, 0], device_id=dev(axis, d), device_id_type=MESH_ID,
            )
            direct.start()
            self.stage_f[r] = self.own(r, lax.rem(me + 2 * n - 2 * d, n)).astype(self.stage_f.dtype)
            forward = pltpu.make_async_remote_copy(
                src_ref=self.stage_f.at[r], dst_ref=self.recv_f.at[r], send_sem=self.send.at[r, 1],
                recv_sem=self.recv.at[r, 1], device_id=dev(axis, -d), device_id_type=MESH_ID,
            )
            forward.start()
            self.pending[r] = (direct, forward)
            self.copies += [direct, forward]

        def middle(self, r):
            axis, d = self.axis_of(r), rings[r][1]
            n = size_on(axis)
            me = me_on(axis)
            term = self.own(r, lax.rem(me + n - d, n))
            self.pending[r][1].wait_recv()
            self.recv_f[r] = (self.recv_f[r].astype(jnp.float32) + term).astype(self.recv_f.dtype)
            second = pltpu.make_async_remote_copy(
                src_ref=self.recv_f.at[r], dst_ref=self.recv_s.at[r], send_sem=self.send.at[r, 2],
                recv_sem=self.recv.at[r, 2], device_id=dev(axis, -d), device_id_type=MESH_ID,
            )
            second.start()
            self.pending[r] = (self.pending[r][0], second)
            self.copies.append(second)

        def end(self, r):
            term = self.own(r, me_on(self.axis_of(r)))
            self.pending[r][0].wait_recv()
            self.pending[r][1].wait_recv()
            self.finish(
                r, term + self.recv_d[r].astype(jnp.float32) + self.recv_s[r].astype(jnp.float32)
            )

    def keep_total1(r, value):
        total1[r] = value

    def other_axis(r):
        return other(rings[r][0])

    mine = pl.ds(pl.multiple_of(me_group * slots, slots), slots)
    returns = []
    locals_ = []

    def keep_fin(r, value):
        fin[:, cols(r)] = value
        local = pltpu.make_async_copy(fin.at[mine, cols(r)], out_ref.at[mine, cols(r)], local_sem.at[r])
        local.start()
        locals_.append(local)
        for o in range(1, groups):
            g = lax.rem(me_group + o, groups)
            cp = pltpu.make_async_remote_copy(
                src_ref=fin.at[pl.ds(pl.multiple_of(g * slots, slots), slots), cols(r)],
                dst_ref=out_ref.at[mine, cols(r)],
                send_sem=ret_send.at[o, r],
                recv_sem=ret_recv.at[o, r],
                device_id=peer(o),
                device_id_type=MESH_ID,
            )
            cp.start()
            returns.append(cp)

    first_phase = Exchange(
        lambda r: rings[r][0], chunk, stage, stage_f1, s1.at[:, 0], s1.at[:, 1], s1.at[:, 2],
        send1, recv1, keep_total1,
    )
    second_phase = Exchange(
        other_axis, lambda r, j: total1[r, j], stage2_d, stage2_f, s2.at[:, 0], s2.at[:, 1], s2.at[:, 2],
        send2, recv2, keep_fin,
    )
    for r in range(4):
        first_phase.begin(r)
    for r in range(4):
        first_phase.middle(r)
    for r in range(4):
        first_phase.end(r)
        second_phase.begin(r)
    for r in range(4):
        second_phase.middle(r)
    for r in range(4):
        second_phase.end(r)
    copies1, copies2 = first_phase.copies, second_phase.copies

    for local in locals_:
        local.wait()
    for cp in returns:
        cp.wait_recv()
    for t in range(mix_ref.shape[0]):
        gap = jnp.full((1, width), logits_ref[2 * t + 1] - logits_ref[2 * t], jnp.float32)
        first = out_ref[pl.ds(col_ref[2 * t], 1), :]
        second = out_ref[pl.ds(col_ref[2 * t + 1], 1), :]
        mix = first / (1.0 + jnp.exp(gap)) + second / (1.0 + jnp.exp(-gap))
        mix_ref[pl.ds(t, 1), :] = mix.astype(mix_ref.dtype)
    for cp in copies1 + copies2 + returns:
        cp.wait_send()


def expert_reduce_scatter(columns, logits, slab, w_gate, w_up, w_down, nsect, ny, nx, nz):
    rows, width = slab.shape
    groups = nsect * ny
    hidden_width = w_down.shape[0]
    quarter = width // 4
    return pl.pallas_call(
        functools.partial(rs_kernel, nsect, ny),
        out_shape=jax.ShapeDtypeStruct((columns.shape[0] // 2, width), jnp.bfloat16),
        in_specs=[
            pl.BlockSpec(memory_space=pltpu.SMEM),
            pl.BlockSpec(memory_space=pltpu.SMEM),
            pl.BlockSpec(memory_space=pltpu.VMEM),
            pl.BlockSpec(memory_space=pl.ANY),
            pl.BlockSpec(memory_space=pl.ANY),
            pl.BlockSpec(memory_space=pl.ANY),
        ],
        out_specs=pl.BlockSpec(memory_space=pltpu.VMEM),
        scratch_shapes=[
            pltpu.VMEM((rows, width), jnp.float32),
            pltpu.VMEM(w_gate.shape, w_gate.dtype),
            pltpu.VMEM(w_up.shape, w_up.dtype),
            pltpu.VMEM(w_down.shape, w_down.dtype),
            pltpu.VMEM((nx, nz, rows, hidden_width), jnp.bfloat16),
            pltpu.VMEM((4, nx, rows, quarter), jnp.bfloat16),
            pltpu.VMEM((4, nx, rows, quarter), jnp.bfloat16),
            pltpu.VMEM((4, rows, quarter), jnp.float32),
            pltpu.VMEM((4, rows, quarter), jnp.float32),
            pltpu.VMEM((rows, width), jnp.float32),
            pltpu.VMEM((4, 3, nx, rows, quarter), jnp.bfloat16),
            pltpu.VMEM((4, nx, rows, quarter), jnp.float32),
            pltpu.VMEM((4, 3, rows, quarter), jnp.float32),
            pltpu.SemaphoreType.DMA((3,)),
            pltpu.SemaphoreType.DMA((4, 3)),
            pltpu.SemaphoreType.DMA((4, 3)),
            pltpu.SemaphoreType.DMA((4, 3)),
            pltpu.SemaphoreType.DMA((4, 3)),
            pltpu.SemaphoreType.DMA((4,)),
            pltpu.SemaphoreType.DMA((groups, 4)),
            pltpu.SemaphoreType.DMA((groups, 4)),
            pltpu.VMEM((nx, nz, rows, width), slab.dtype),
            pltpu.SemaphoreType.DMA(()),
            pltpu.SemaphoreType.DMA((groups,)),
            pltpu.SemaphoreType.DMA((groups,)),
            pltpu.SemaphoreType.DMA((4, 3)),
            pltpu.SemaphoreType.DMA((4, 3)),
            pltpu.SemaphoreType.DMA((4, 3)),
            pltpu.SemaphoreType.DMA((4, 3)),
        ],
        compiler_params=pltpu.CompilerParams(
            collective_id=0, has_side_effects=True, vmem_limit_bytes=64 * 1024 * 1024
        ),
    )(columns, logits, slab, w_gate, w_up, w_down)


def gather_body(nsect, ny, in_ref, out_ref, local_sem, in_send, in_recv, send1, recv1, send2, recv2):
    nx, nz, rows, width = out_ref.shape
    groups = nsect * ny
    slots = rows // groups
    quarter = width // 4
    c = lax.axis_index("sect")
    y = lax.axis_index("ey")
    mx = lax.axis_index("ex")
    mz = lax.axis_index("tp")

    def dev(axis, d):
        if axis == "z":
            return (c, y, mx, lax.rem(mz + d + nz, nz))
        return (c, y, lax.rem(mx + d + nx, nx), mz)

    me_group = c * ny + y

    def peer(o):
        g = lax.rem(me_group + o, groups)
        return (g // ny, lax.rem(g, ny), mx, mz)

    mine = pl.ds(pl.multiple_of(me_group * slots, slots), slots)
    local = pltpu.make_async_copy(in_ref.at[mine], out_ref.at[mx, mz, mine], local_sem)
    local.start()
    dispatch = []
    for o in range(1, groups):
        cp = pltpu.make_async_remote_copy(
            src_ref=in_ref.at[pl.ds(pl.multiple_of(lax.rem(me_group + o, groups) * slots, slots), slots)],
            dst_ref=out_ref.at[mx, mz, mine],
            send_sem=in_send.at[o],
            recv_sem=in_recv.at[o],
            device_id=peer(o),
            device_id_type=MESH_ID,
        )
        cp.start()
        dispatch.append(cp)
    local.wait()
    for cp in dispatch:
        cp.wait_recv()

    rings = [("z", 1), ("z", -1), ("x", 1), ("x", -1)]

    def cols(r):
        return pl.ds(r * quarter, quarter)

    def block(axis, r, k):
        if axis == "z":
            return out_ref.at[mx, k, :, cols(r)]
        return out_ref.at[k, mz, :, cols(r)]

    def plane_block(axis, r, k):
        if axis == "x":
            return out_ref.at[k, :, :, cols(r)]
        return out_ref.at[:, k, :, cols(r)]

    def me_on(axis):
        return mz if axis == "z" else mx

    def both_sides(axis_of, view, send, recv):
        copies = []
        first = {}
        for r in range(4):
            axis, d = axis_of(r), rings[r][1]
            me = me_on(axis)
            src = view(axis, r, me)
            for side, sign in ((0, d), (1, -d)):
                cp = pltpu.make_async_remote_copy(
                    src_ref=src, dst_ref=src, send_sem=send.at[r, side], recv_sem=recv.at[r, side],
                    device_id=dev(axis, sign), device_id_type=MESH_ID,
                )
                cp.start()
                first[(r, side)] = cp
                copies.append(cp)
        later = {}
        for r in range(4):
            axis, d = axis_of(r), rings[r][1]
            n = nz if axis == "z" else nx
            first[(r, 1)].wait_recv()
            passing = view(axis, r, lax.rem(me_on(axis) + n + d, n))
            cp = pltpu.make_async_remote_copy(
                src_ref=passing, dst_ref=passing, send_sem=send.at[r, 2], recv_sem=recv.at[r, 2],
                device_id=dev(axis, -d), device_id_type=MESH_ID,
            )
            cp.start()
            later[r] = cp
            copies.append(cp)
        for r in range(4):
            first[(r, 0)].wait_recv()
            later[r].wait_recv()
        return copies

    copies1 = both_sides(lambda r: rings[r][0], block, send1, recv1)

    def second(r):
        return "x" if rings[r][0] == "z" else "z"

    copies2 = both_sides(second, plane_block, send2, recv2)
    for cp in copies1 + copies2 + dispatch:
        cp.wait_send()


ALL = ("sect", "ey", "ex", "tp")
EXPERT_AXES = ("sect", "ey")
PLANE_AXES = ("ex", "tp")


def place_slots(ids_block, experts):
    flat_ids = ids_block.reshape(-1)
    hits_mask = (flat_ids[:, None] == jnp.arange(experts, dtype=jnp.int32)[None, :]).astype(
        jnp.int32
    )
    earlier = jnp.cumsum(hits_mask, axis=0) - hits_mask
    slot_rank = jnp.sum(earlier * hits_mask, axis=1)
    return (flat_ids, slot_rank)


def per_device(tokens, router_logits, expert_ids, w_gate, w_up, w_down):
    experts_all = lax.axis_size(EXPERT_AXES)
    plane_count = lax.axis_size(PLANE_AXES)
    token_count = tokens.shape[0]
    capacity = min(token_count, 4 * token_count // experts_all)
    model_width = tokens.shape[1]
    flat_ids, slot_rank = place_slots(expert_ids, experts_all)
    columns = flat_ids * capacity + slot_rank
    positions = jnp.arange(experts_all * capacity, dtype=jnp.int32)
    source = columns.reshape(token_count, 2)
    picker = (positions[:, None, None] == source[None, :, :]).any(axis=2).astype(jnp.bfloat16)
    slab = jnp.dot(picker, tokens, preferred_element_type=jnp.float32).astype(jnp.bfloat16)
    nx = lax.axis_size("ex")
    return expert_reduce_scatter(
        columns.astype(jnp.int32),
        router_logits.reshape(-1),
        slab,
        w_gate[0],
        w_up[0],
        w_down[0],
        lax.axis_size("sect"),
        lax.axis_size("ey"),
        nx,
        plane_count // nx,
    )


def x_extent(devices):
    coords = [getattr(d, "coords", None) for d in devices.flat]
    if all(c is not None for c in coords):
        return len({c[0] for c in coords})
    return int(round(np.sqrt(devices.shape[1])))


def solution(mesh):
    devices = mesh.devices
    sect, exp, tp = devices.shape
    ex = x_extent(devices)
    fine = Mesh(devices.reshape(sect, exp // ex, ex, tp), ALL)
    in_specs = (
        P(ALL, None),
        P(ALL, None),
        P(ALL, None),
        P(EXPERT_AXES + PLANE_AXES[:1], None, "tp"),
        P(EXPERT_AXES + PLANE_AXES[:1], None, "tp"),
        P(EXPERT_AXES + PLANE_AXES[:1], "tp", None),
    )
    out_specs = P(ALL, None)
    return jax.shard_map(
        per_device, mesh=fine, in_specs=in_specs, out_specs=out_specs, check_vma=False
    )
```

```python
import functools

import jax
import jax.numpy as jnp
import numpy as np
from jax import lax
from jax.experimental import pallas as pl
from jax.experimental.pallas import tpu as pltpu
from jax.sharding import Mesh
from jax.sharding import PartitionSpec as P

MESH_ID = pl.DeviceIdType.MESH


def rs_kernel(
    nsect, ny, col_ref, logits_ref, slab_ref, wg_hbm, wu_hbm, wd_hbm, mix_ref,
    out_ref, wg, wu, wd, hid, stage, stage_f1, stage2_d, stage2_f, fin, s1, total1, s2, wsem, send1, recv1, send2, recv2, local_sem, ret_send, ret_recv,
    rows_ref, g_local, g_in_send, g_in_recv, g_send1, g_recv1, g_send2, g_recv2,
):
    nx, nz, rows, width = rows_ref.shape
    hidden_width = wd.shape[0]
    quarter = width // 4
    groups = nsect * ny
    slots = rows // groups
    c = lax.axis_index("sect")
    y = lax.axis_index("ey")
    mx = lax.axis_index("ex")
    mz = lax.axis_index("tp")

    weight_copies = [
        pltpu.make_async_copy(src, dst, wsem.at[i])
        for i, (src, dst) in enumerate(((wg_hbm, wg), (wu_hbm, wu), (wd_hbm, wd)))
    ]
    for cp in weight_copies:
        cp.start()

    def dev(axis, d):
        if axis == "z":
            return (c, y, mx, lax.rem(mz + d + nz, nz))
        return (c, y, lax.rem(mx + d + nx, nx), mz)

    me_group = c * ny + y

    def peer(o):
        g = lax.rem(me_group + o, groups)
        return (g // ny, lax.rem(g, ny), mx, mz)

    barrier = pltpu.get_barrier_semaphore()
    for axis in ("x", "z"):
        for d in (1, -1):
            pl.semaphore_signal(barrier, inc=1, device_id=dev(axis, d), device_id_type=MESH_ID)
    for o in range(1, groups):
        pl.semaphore_signal(barrier, inc=1, device_id=peer(o), device_id_type=MESH_ID)
    pl.semaphore_wait(barrier, 4 + groups - 1)

    gather_body(
        nsect, ny, slab_ref, rows_ref, g_local, g_in_send, g_in_recv, g_send1, g_recv1, g_send2, g_recv2
    )
    weight_copies[0].wait()
    weight_copies[1].wait()

    pair = 2 if nx % 2 == 0 else 1

    def hidden_group(i, carry):
        lead = pl.ds(pl.multiple_of(i * pair, pair), pair)
        block = rows_ref[lead].reshape(pair * nz * rows, width)
        gate = jnp.dot(block, wg[...], preferred_element_type=jnp.float32)
        up = jnp.dot(block, wu[...], preferred_element_type=jnp.float32)
        act = (jax.nn.silu(gate) * up).astype(hid.dtype)
        hid[lead] = act.reshape(pair, nz, rows, hidden_width)
        return carry

    lax.fori_loop(0, nx // pair, hidden_group, 0)
    weight_copies[2].wait()

    rings = [("z", 1), ("z", -1), ("x", 1), ("x", -1)]

    def me_on(axis):
        return mz if axis == "z" else mx

    def size_on(axis):
        return nz if axis == "z" else nx

    def cols(r):
        return pl.ds(r * quarter, quarter)

    def chunk(r, j):
        if rings[r][0] == "z":
            h = hid[:, j]
        else:
            h = hid[j]
        lead = h.shape[0]
        part = jnp.dot(
            h.reshape(lead * rows, hidden_width), wd[:, cols(r)], preferred_element_type=jnp.float32
        )
        return part.reshape(lead, rows, quarter)

    def other(axis):
        return "x" if axis == "z" else "z"

    class Exchange:
        def __init__(self, axis_of, own, stage_d, stage_f, recv_d, recv_f, recv_s, send, recv, finish):
            self.axis_of, self.own = axis_of, own
            self.stage_d, self.stage_f = stage_d, stage_f
            self.recv_d, self.recv_f, self.recv_s = recv_d, recv_f, recv_s
            self.send, self.recv, self.finish = send, recv, finish
            self.copies, self.pending = [], {}

        def begin(self, r):
            axis, d = self.axis_of(r), rings[r][1]
            n = size_on(axis)
            me = me_on(axis)
            self.stage_d[r] = self.own(r, lax.rem(me + n + d, n)).astype(self.stage_d.dtype)
            direct = pltpu.make_async_remote_copy(
                src_ref=self.stage_d.at[r], dst_ref=self.recv_d.at[r], send_sem=self.send.at[r, 0],
                recv_sem=self.recv.at[r, 0], device_id=dev(axis, d), device_id_type=MESH_ID,
            )
            direct.start()
            self.stage_f[r] = self.own(r, lax.rem(me + 2 * n - 2 * d, n)).astype(self.stage_f.dtype)
            forward = pltpu.make_async_remote_copy(
                src_ref=self.stage_f.at[r], dst_ref=self.recv_f.at[r], send_sem=self.send.at[r, 1],
                recv_sem=self.recv.at[r, 1], device_id=dev(axis, -d), device_id_type=MESH_ID,
            )
            forward.start()
            self.pending[r] = (direct, forward)
            self.copies += [direct, forward]

        def middle(self, r):
            axis, d = self.axis_of(r), rings[r][1]
            n = size_on(axis)
            me = me_on(axis)
            term = self.own(r, lax.rem(me + n - d, n))
            self.pending[r][1].wait_recv()
            self.recv_f[r] = (self.recv_f[r].astype(jnp.float32) + term).astype(self.recv_f.dtype)
            second = pltpu.make_async_remote_copy(
                src_ref=self.recv_f.at[r], dst_ref=self.recv_s.at[r], send_sem=self.send.at[r, 2],
                recv_sem=self.recv.at[r, 2], device_id=dev(axis, -d), device_id_type=MESH_ID,
            )
            second.start()
            self.pending[r] = (self.pending[r][0], second)
            self.copies.append(second)

        def end(self, r):
            term = self.own(r, me_on(self.axis_of(r)))
            self.pending[r][0].wait_recv()
            self.pending[r][1].wait_recv()
            self.finish(
                r, term + self.recv_d[r].astype(jnp.float32) + self.recv_s[r].astype(jnp.float32)
            )

    def keep_total1(r, value):
        total1[r] = value

    def other_axis(r):
        return other(rings[r][0])

    mine = pl.ds(pl.multiple_of(me_group * slots, slots), slots)
    returns = []
    locals_ = []

    def keep_fin(r, value):
        fin[:, cols(r)] = value
        local = pltpu.make_async_copy(fin.at[mine, cols(r)], out_ref.at[mine, cols(r)], local_sem.at[r])
        local.start()
        locals_.append(local)
        for o in range(1, groups):
            g = lax.rem(me_group + o, groups)
            cp = pltpu.make_async_remote_copy(
                src_ref=fin.at[pl.ds(pl.multiple_of(g * slots, slots), slots), cols(r)],
                dst_ref=out_ref.at[mine, cols(r)],
                send_sem=ret_send.at[o, r],
                recv_sem=ret_recv.at[o, r],
                device_id=peer(o),
                device_id_type=MESH_ID,
            )
            cp.start()
            returns.append(cp)

    first_phase = Exchange(
        lambda r: rings[r][0], chunk, stage, stage_f1, s1.at[:, 0], s1.at[:, 1], s1.at[:, 2],
        send1, recv1, keep_total1,
    )
    second_phase = Exchange(
        other_axis, lambda r, j: total1[r, j], stage2_d, stage2_f, s2.at[:, 0], s2.at[:, 1], s2.at[:, 2],
        send2, recv2, keep_fin,
    )
    for r in range(4):
        first_phase.begin(r)
    for r in range(4):
        first_phase.middle(r)
    for r in range(4):
        first_phase.end(r)
        second_phase.begin(r)
    for r in range(4):
        second_phase.middle(r)
    for r in range(4):
        second_phase.end(r)
    copies1, copies2 = first_phase.copies, second_phase.copies

    for local in locals_:
        local.wait()
    for cp in returns:
        cp.wait_recv()
    for t in range(mix_ref.shape[0]):
        gap = jnp.full((1, width), logits_ref[2 * t + 1] - logits_ref[2 * t], jnp.float32)
        first = out_ref[pl.ds(col_ref[2 * t], 1), :]
        second = out_ref[pl.ds(col_ref[2 * t + 1], 1), :]
        mix = first / (1.0 + jnp.exp(gap)) + second / (1.0 + jnp.exp(-gap))
        mix_ref[pl.ds(t, 1), :] = mix.astype(mix_ref.dtype)
    for cp in copies1 + copies2 + returns:
        cp.wait_send()


def expert_reduce_scatter(columns, logits, slab, w_gate, w_up, w_down, nsect, ny, nx, nz):
    rows, width = slab.shape
    groups = nsect * ny
    hidden_width = w_down.shape[0]
    quarter = width // 4
    return pl.pallas_call(
        functools.partial(rs_kernel, nsect, ny),
        out_shape=jax.ShapeDtypeStruct((columns.shape[0] // 2, width), jnp.bfloat16),
        in_specs=[
            pl.BlockSpec(memory_space=pltpu.SMEM),
            pl.BlockSpec(memory_space=pltpu.SMEM),
            pl.BlockSpec(memory_space=pltpu.VMEM),
            pl.BlockSpec(memory_space=pl.ANY),
            pl.BlockSpec(memory_space=pl.ANY),
            pl.BlockSpec(memory_space=pl.ANY),
        ],
        out_specs=pl.BlockSpec(memory_space=pltpu.VMEM),
        scratch_shapes=[
            pltpu.VMEM((rows, width), jnp.float32),
            pltpu.VMEM(w_gate.shape, w_gate.dtype),
            pltpu.VMEM(w_up.shape, w_up.dtype),
            pltpu.VMEM(w_down.shape, w_down.dtype),
            pltpu.VMEM((nx, nz, rows, hidden_width), jnp.bfloat16),
            pltpu.VMEM((4, nx, rows, quarter), jnp.bfloat16),
            pltpu.VMEM((4, nx, rows, quarter), jnp.bfloat16),
            pltpu.VMEM((4, rows, quarter), jnp.float32),
            pltpu.VMEM((4, rows, quarter), jnp.float32),
            pltpu.VMEM((rows, width), jnp.float32),
            pltpu.VMEM((4, 3, nx, rows, quarter), jnp.bfloat16),
            pltpu.VMEM((4, nx, rows, quarter), jnp.float32),
            pltpu.VMEM((4, 3, rows, quarter), jnp.float32),
            pltpu.SemaphoreType.DMA((3,)),
            pltpu.SemaphoreType.DMA((4, 3)),
            pltpu.SemaphoreType.DMA((4, 3)),
            pltpu.SemaphoreType.DMA((4, 3)),
            pltpu.SemaphoreType.DMA((4, 3)),
            pltpu.SemaphoreType.DMA((4,)),
            pltpu.SemaphoreType.DMA((groups, 4)),
            pltpu.SemaphoreType.DMA((groups, 4)),
            pltpu.VMEM((nx, nz, rows, width), slab.dtype),
            pltpu.SemaphoreType.DMA(()),
            pltpu.SemaphoreType.DMA((groups,)),
            pltpu.SemaphoreType.DMA((groups,)),
            pltpu.SemaphoreType.DMA((4, 3)),
            pltpu.SemaphoreType.DMA((4, 3)),
            pltpu.SemaphoreType.DMA((4, 3)),
            pltpu.SemaphoreType.DMA((4, 3)),
        ],
        compiler_params=pltpu.CompilerParams(
            collective_id=0, has_side_effects=True, vmem_limit_bytes=64 * 1024 * 1024
        ),
    )(columns, logits, slab, w_gate, w_up, w_down)


def gather_body(nsect, ny, in_ref, out_ref, local_sem, in_send, in_recv, send1, recv1, send2, recv2):
    nx, nz, rows, width = out_ref.shape
    groups = nsect * ny
    slots = rows // groups
    quarter = width // 4
    c = lax.axis_index("sect")
    y = lax.axis_index("ey")
    mx = lax.axis_index("ex")
    mz = lax.axis_index("tp")

    def dev(axis, d):
        if axis == "z":
            return (c, y, mx, lax.rem(mz + d + nz, nz))
        return (c, y, lax.rem(mx + d + nx, nx), mz)

    me_group = c * ny + y

    def peer(o):
        g = lax.rem(me_group + o, groups)
        return (g // ny, lax.rem(g, ny), mx, mz)

    mine = pl.ds(pl.multiple_of(me_group * slots, slots), slots)
    local = pltpu.make_async_copy(in_ref.at[mine], out_ref.at[mx, mz, mine], local_sem)
    local.start()
    dispatch = []
    for o in range(1, groups):
        cp = pltpu.make_async_remote_copy(
            src_ref=in_ref.at[pl.ds(pl.multiple_of(lax.rem(me_group + o, groups) * slots, slots), slots)],
            dst_ref=out_ref.at[mx, mz, mine],
            send_sem=in_send.at[o],
            recv_sem=in_recv.at[o],
            device_id=peer(o),
            device_id_type=MESH_ID,
        )
        cp.start()
        dispatch.append(cp)
    local.wait()
    for cp in dispatch:
        cp.wait_recv()

    rings = [("z", 1), ("z", -1), ("x", 1), ("x", -1)]

    def cols(r):
        return pl.ds(r * quarter, quarter)

    def block(axis, r, k):
        if axis == "z":
            return out_ref.at[mx, k, :, cols(r)]
        return out_ref.at[k, mz, :, cols(r)]

    def plane_block(axis, r, k):
        if axis == "x":
            return out_ref.at[k, :, :, cols(r)]
        return out_ref.at[:, k, :, cols(r)]

    def me_on(axis):
        return mz if axis == "z" else mx

    class Broadcast:
        def __init__(self, axis_of, view, send, recv):
            self.axis_of, self.view, self.send, self.recv = axis_of, view, send, recv
            self.copies, self.first, self.later = [], {}, {}

        def begin(self, r):
            axis, d = self.axis_of(r), rings[r][1]
            src = self.view(axis, r, me_on(axis))
            for side, sign in ((0, d), (1, -d)):
                cp = pltpu.make_async_remote_copy(
                    src_ref=src, dst_ref=src, send_sem=self.send.at[r, side],
                    recv_sem=self.recv.at[r, side], device_id=dev(axis, sign), device_id_type=MESH_ID,
                )
                cp.start()
                self.first[(r, side)] = cp
                self.copies.append(cp)

        def middle(self, r):
            axis, d = self.axis_of(r), rings[r][1]
            n = nz if axis == "z" else nx
            self.first[(r, 1)].wait_recv()
            passing = self.view(axis, r, lax.rem(me_on(axis) + n + d, n))
            cp = pltpu.make_async_remote_copy(
                src_ref=passing, dst_ref=passing, send_sem=self.send.at[r, 2],
                recv_sem=self.recv.at[r, 2], device_id=dev(axis, -d), device_id_type=MESH_ID,
            )
            cp.start()
            self.later[r] = cp
            self.copies.append(cp)

        def end(self, r):
            self.first[(r, 0)].wait_recv()
            self.later[r].wait_recv()

    def second(r):
        return "x" if rings[r][0] == "z" else "z"

    first_phase = Broadcast(lambda r: rings[r][0], block, send1, recv1)
    second_phase = Broadcast(second, plane_block, send2, recv2)
    for r in range(4):
        first_phase.begin(r)
    for r in range(4):
        first_phase.middle(r)
    for r in range(4):
        first_phase.end(r)
        second_phase.begin(r)
    for r in range(4):
        second_phase.middle(r)
    for r in range(4):
        second_phase.end(r)
    copies1, copies2 = first_phase.copies, second_phase.copies
    for cp in copies1 + copies2 + dispatch:
        cp.wait_send()


ALL = ("sect", "ey", "ex", "tp")
EXPERT_AXES = ("sect", "ey")
PLANE_AXES = ("ex", "tp")


def place_slots(ids_block, experts):
    flat_ids = ids_block.reshape(-1)
    hits_mask = (flat_ids[:, None] == jnp.arange(experts, dtype=jnp.int32)[None, :]).astype(
        jnp.int32
    )
    earlier = jnp.cumsum(hits_mask, axis=0) - hits_mask
    slot_rank = jnp.sum(earlier * hits_mask, axis=1)
    return (flat_ids, slot_rank)


def per_device(tokens, router_logits, expert_ids, w_gate, w_up, w_down):
    experts_all = lax.axis_size(EXPERT_AXES)
    plane_count = lax.axis_size(PLANE_AXES)
    token_count = tokens.shape[0]
    capacity = min(token_count, 4 * token_count // experts_all)
    model_width = tokens.shape[1]
    flat_ids, slot_rank = place_slots(expert_ids, experts_all)
    columns = flat_ids * capacity + slot_rank
    positions = jnp.arange(experts_all * capacity, dtype=jnp.int32)
    source = columns.reshape(token_count, 2)
    picker = (positions[:, None, None] == source[None, :, :]).any(axis=2).astype(jnp.bfloat16)
    slab = jnp.dot(picker, tokens, preferred_element_type=jnp.float32).astype(jnp.bfloat16)
    nx = lax.axis_size("ex")
    return expert_reduce_scatter(
        columns.astype(jnp.int32),
        router_logits.reshape(-1),
        slab,
        w_gate[0],
        w_up[0],
        w_down[0],
        lax.axis_size("sect"),
        lax.axis_size("ey"),
        nx,
        plane_count // nx,
    )


def x_extent(devices):
    coords = [getattr(d, "coords", None) for d in devices.flat]
    if all(c is not None for c in coords):
        return len({c[0] for c in coords})
    return int(round(np.sqrt(devices.shape[1])))


def solution(mesh):
    devices = mesh.devices
    sect, exp, tp = devices.shape
    ex = x_extent(devices)
    fine = Mesh(devices.reshape(sect, exp // ex, ex, tp), ALL)
    in_specs = (
        P(ALL, None),
        P(ALL, None),
        P(ALL, None),
        P(EXPERT_AXES + PLANE_AXES[:1], None, "tp"),
        P(EXPERT_AXES + PLANE_AXES[:1], None, "tp"),
        P(EXPERT_AXES + PLANE_AXES[:1], "tp", None),
    )
    out_specs = P(ALL, None)
    return jax.shard_map(
        per_device, mesh=fine, in_specs=in_specs, out_specs=out_specs, check_vma=False
    )
```

```python
import functools

import jax
import jax.numpy as jnp
import numpy as np
from jax import lax
from jax.experimental import pallas as pl
from jax.experimental.pallas import tpu as pltpu
from jax.sharding import Mesh
from jax.sharding import PartitionSpec as P

MESH_ID = pl.DeviceIdType.MESH


def rs_kernel(
    nsect, ny, col_ref, logits_ref, slab_ref, wg_hbm, wu_hbm, wd_hbm, mix_ref,
    out_ref, wg, wu, wd, hid, stage, stage_f1, stage2_d, stage2_f, fin, s1, total1, s2, wsem, send1, recv1, send2, recv2, local_sem, ret_send, ret_recv,
    rows_ref, g_local, g_in_send, g_in_recv, g_send1, g_recv1, g_send2, g_recv2,
):
    nx, nz, rows, width = rows_ref.shape
    hidden_width = wd.shape[0]
    quarter = width // 4
    groups = nsect * ny
    slots = rows // groups
    c = lax.axis_index("sect")
    y = lax.axis_index("ey")
    mx = lax.axis_index("ex")
    mz = lax.axis_index("tp")

    weight_copies = [
        pltpu.make_async_copy(src, dst, wsem.at[i])
        for i, (src, dst) in enumerate(((wg_hbm, wg), (wu_hbm, wu), (wd_hbm, wd)))
    ]
    for cp in weight_copies:
        cp.start()

    def dev(axis, d):
        if axis == "z":
            return (c, y, mx, lax.rem(mz + d + nz, nz))
        return (c, y, lax.rem(mx + d + nx, nx), mz)

    me_group = c * ny + y

    def peer(o):
        g = lax.rem(me_group + o, groups)
        return (g // ny, lax.rem(g, ny), mx, mz)

    barrier = pltpu.get_barrier_semaphore()
    for axis in ("x", "z"):
        for d in (1, -1):
            pl.semaphore_signal(barrier, inc=1, device_id=dev(axis, d), device_id_type=MESH_ID)
    for o in range(1, groups):
        pl.semaphore_signal(barrier, inc=1, device_id=peer(o), device_id_type=MESH_ID)
    pl.semaphore_wait(barrier, 4 + groups - 1)

    gather_body(
        nsect, ny, slab_ref, rows_ref, g_local, g_in_send, g_in_recv, g_send1, g_recv1, g_send2, g_recv2
    )
    weight_copies[0].wait()
    weight_copies[1].wait()

    pair = nx

    def hidden_group(i, carry):
        lead = pl.ds(pl.multiple_of(i * pair, pair), pair)
        block = rows_ref[lead].reshape(pair * nz * rows, width)
        gate = jnp.dot(block, wg[...], preferred_element_type=jnp.float32)
        up = jnp.dot(block, wu[...], preferred_element_type=jnp.float32)
        act = (jax.nn.silu(gate) * up).astype(hid.dtype)
        hid[lead] = act.reshape(pair, nz, rows, hidden_width)
        return carry

    lax.fori_loop(0, nx // pair, hidden_group, 0)
    weight_copies[2].wait()

    rings = [("z", 1), ("z", -1), ("x", 1), ("x", -1)]

    def me_on(axis):
        return mz if axis == "z" else mx

    def size_on(axis):
        return nz if axis == "z" else nx

    def cols(r):
        return pl.ds(r * quarter, quarter)

    def chunk(r, j):
        if rings[r][0] == "z":
            h = hid[:, j]
        else:
            h = hid[j]
        lead = h.shape[0]
        part = jnp.dot(
            h.reshape(lead * rows, hidden_width), wd[:, cols(r)], preferred_element_type=jnp.float32
        )
        return part.reshape(lead, rows, quarter)

    def other(axis):
        return "x" if axis == "z" else "z"

    class Exchange:
        def __init__(self, axis_of, own, stage_d, stage_f, recv_d, recv_f, recv_s, send, recv, finish):
            self.axis_of, self.own = axis_of, own
            self.stage_d, self.stage_f = stage_d, stage_f
            self.recv_d, self.recv_f, self.recv_s = recv_d, recv_f, recv_s
            self.send, self.recv, self.finish = send, recv, finish
            self.copies, self.pending = [], {}

        def begin(self, r):
            axis, d = self.axis_of(r), rings[r][1]
            n = size_on(axis)
            me = me_on(axis)
            self.stage_d[r] = self.own(r, lax.rem(me + n + d, n)).astype(self.stage_d.dtype)
            direct = pltpu.make_async_remote_copy(
                src_ref=self.stage_d.at[r], dst_ref=self.recv_d.at[r], send_sem=self.send.at[r, 0],
                recv_sem=self.recv.at[r, 0], device_id=dev(axis, d), device_id_type=MESH_ID,
            )
            direct.start()
            self.stage_f[r] = self.own(r, lax.rem(me + 2 * n - 2 * d, n)).astype(self.stage_f.dtype)
            forward = pltpu.make_async_remote_copy(
                src_ref=self.stage_f.at[r], dst_ref=self.recv_f.at[r], send_sem=self.send.at[r, 1],
                recv_sem=self.recv.at[r, 1], device_id=dev(axis, -d), device_id_type=MESH_ID,
            )
            forward.start()
            self.pending[r] = (direct, forward)
            self.copies += [direct, forward]

        def middle(self, r):
            axis, d = self.axis_of(r), rings[r][1]
            n = size_on(axis)
            me = me_on(axis)
            term = self.own(r, lax.rem(me + n - d, n))
            self.pending[r][1].wait_recv()
            self.recv_f[r] = (self.recv_f[r].astype(jnp.float32) + term).astype(self.recv_f.dtype)
            second = pltpu.make_async_remote_copy(
                src_ref=self.recv_f.at[r], dst_ref=self.recv_s.at[r], send_sem=self.send.at[r, 2],
                recv_sem=self.recv.at[r, 2], device_id=dev(axis, -d), device_id_type=MESH_ID,
            )
            second.start()
            self.pending[r] = (self.pending[r][0], second)
            self.copies.append(second)

        def end(self, r):
            term = self.own(r, me_on(self.axis_of(r)))
            self.pending[r][0].wait_recv()
            self.pending[r][1].wait_recv()
            self.finish(
                r, term + self.recv_d[r].astype(jnp.float32) + self.recv_s[r].astype(jnp.float32)
            )

    def keep_total1(r, value):
        total1[r] = value

    def other_axis(r):
        return other(rings[r][0])

    mine = pl.ds(pl.multiple_of(me_group * slots, slots), slots)
    returns = []
    locals_ = []

    def keep_fin(r, value):
        fin[:, cols(r)] = value
        local = pltpu.make_async_copy(fin.at[mine, cols(r)], out_ref.at[mine, cols(r)], local_sem.at[r])
        local.start()
        locals_.append(local)
        for o in range(1, groups):
            g = lax.rem(me_group + o, groups)
            cp = pltpu.make_async_remote_copy(
                src_ref=fin.at[pl.ds(pl.multiple_of(g * slots, slots), slots), cols(r)],
                dst_ref=out_ref.at[mine, cols(r)],
                send_sem=ret_send.at[o, r],
                recv_sem=ret_recv.at[o, r],
                device_id=peer(o),
                device_id_type=MESH_ID,
            )
            cp.start()
            returns.append(cp)

    first_phase = Exchange(
        lambda r: rings[r][0], chunk, stage, stage_f1, s1.at[:, 0], s1.at[:, 1], s1.at[:, 2],
        send1, recv1, keep_total1,
    )
    second_phase = Exchange(
        other_axis, lambda r, j: total1[r, j], stage2_d, stage2_f, s2.at[:, 0], s2.at[:, 1], s2.at[:, 2],
        send2, recv2, keep_fin,
    )
    for r in range(4):
        first_phase.begin(r)
    for r in range(4):
        first_phase.middle(r)
    for r in range(4):
        first_phase.end(r)
        second_phase.begin(r)
    for r in range(4):
        second_phase.middle(r)
    for r in range(4):
        second_phase.end(r)
    copies1, copies2 = first_phase.copies, second_phase.copies

    for local in locals_:
        local.wait()
    for cp in returns:
        cp.wait_recv()
    for t in range(mix_ref.shape[0]):
        gap = jnp.full((1, width), logits_ref[2 * t + 1] - logits_ref[2 * t], jnp.float32)
        first = out_ref[pl.ds(col_ref[2 * t], 1), :]
        second = out_ref[pl.ds(col_ref[2 * t + 1], 1), :]
        mix = first / (1.0 + jnp.exp(gap)) + second / (1.0 + jnp.exp(-gap))
        mix_ref[pl.ds(t, 1), :] = mix.astype(mix_ref.dtype)
    for cp in copies1 + copies2 + returns:
        cp.wait_send()


def expert_reduce_scatter(columns, logits, slab, w_gate, w_up, w_down, nsect, ny, nx, nz):
    rows, width = slab.shape
    groups = nsect * ny
    hidden_width = w_down.shape[0]
    quarter = width // 4
    return pl.pallas_call(
        functools.partial(rs_kernel, nsect, ny),
        out_shape=jax.ShapeDtypeStruct((columns.shape[0] // 2, width), jnp.bfloat16),
        in_specs=[
            pl.BlockSpec(memory_space=pltpu.SMEM),
            pl.BlockSpec(memory_space=pltpu.SMEM),
            pl.BlockSpec(memory_space=pltpu.VMEM),
            pl.BlockSpec(memory_space=pl.ANY),
            pl.BlockSpec(memory_space=pl.ANY),
            pl.BlockSpec(memory_space=pl.ANY),
        ],
        out_specs=pl.BlockSpec(memory_space=pltpu.VMEM),
        scratch_shapes=[
            pltpu.VMEM((rows, width), jnp.float32),
            pltpu.VMEM(w_gate.shape, w_gate.dtype),
            pltpu.VMEM(w_up.shape, w_up.dtype),
            pltpu.VMEM(w_down.shape, w_down.dtype),
            pltpu.VMEM((nx, nz, rows, hidden_width), jnp.bfloat16),
            pltpu.VMEM((4, nx, rows, quarter), jnp.bfloat16),
            pltpu.VMEM((4, nx, rows, quarter), jnp.bfloat16),
            pltpu.VMEM((4, rows, quarter), jnp.float32),
            pltpu.VMEM((4, rows, quarter), jnp.float32),
            pltpu.VMEM((rows, width), jnp.float32),
            pltpu.VMEM((4, 3, nx, rows, quarter), jnp.bfloat16),
            pltpu.VMEM((4, nx, rows, quarter), jnp.float32),
            pltpu.VMEM((4, 3, rows, quarter), jnp.float32),
            pltpu.SemaphoreType.DMA((3,)),
            pltpu.SemaphoreType.DMA((4, 3)),
            pltpu.SemaphoreType.DMA((4, 3)),
            pltpu.SemaphoreType.DMA((4, 3)),
            pltpu.SemaphoreType.DMA((4, 3)),
            pltpu.SemaphoreType.DMA((4,)),
            pltpu.SemaphoreType.DMA((groups, 4)),
            pltpu.SemaphoreType.DMA((groups, 4)),
            pltpu.VMEM((nx, nz, rows, width), slab.dtype),
            pltpu.SemaphoreType.DMA(()),
            pltpu.SemaphoreType.DMA((groups,)),
            pltpu.SemaphoreType.DMA((groups,)),
            pltpu.SemaphoreType.DMA((4, 3)),
            pltpu.SemaphoreType.DMA((4, 3)),
            pltpu.SemaphoreType.DMA((4, 3)),
            pltpu.SemaphoreType.DMA((4, 3)),
        ],
        compiler_params=pltpu.CompilerParams(
            collective_id=0, has_side_effects=True, vmem_limit_bytes=64 * 1024 * 1024
        ),
    )(columns, logits, slab, w_gate, w_up, w_down)


def gather_body(nsect, ny, in_ref, out_ref, local_sem, in_send, in_recv, send1, recv1, send2, recv2):
    nx, nz, rows, width = out_ref.shape
    groups = nsect * ny
    slots = rows // groups
    quarter = width // 4
    c = lax.axis_index("sect")
    y = lax.axis_index("ey")
    mx = lax.axis_index("ex")
    mz = lax.axis_index("tp")

    def dev(axis, d):
        if axis == "z":
            return (c, y, mx, lax.rem(mz + d + nz, nz))
        return (c, y, lax.rem(mx + d + nx, nx), mz)

    me_group = c * ny + y

    def peer(o):
        g = lax.rem(me_group + o, groups)
        return (g // ny, lax.rem(g, ny), mx, mz)

    mine = pl.ds(pl.multiple_of(me_group * slots, slots), slots)
    local = pltpu.make_async_copy(in_ref.at[mine], out_ref.at[mx, mz, mine], local_sem)
    local.start()
    dispatch = []
    for o in range(1, groups):
        cp = pltpu.make_async_remote_copy(
            src_ref=in_ref.at[pl.ds(pl.multiple_of(lax.rem(me_group + o, groups) * slots, slots), slots)],
            dst_ref=out_ref.at[mx, mz, mine],
            send_sem=in_send.at[o],
            recv_sem=in_recv.at[o],
            device_id=peer(o),
            device_id_type=MESH_ID,
        )
        cp.start()
        dispatch.append(cp)
    local.wait()
    for cp in dispatch:
        cp.wait_recv()

    rings = [("z", 1), ("z", -1), ("x", 1), ("x", -1)]

    def cols(r):
        return pl.ds(r * quarter, quarter)

    def block(axis, r, k):
        if axis == "z":
            return out_ref.at[mx, k, :, cols(r)]
        return out_ref.at[k, mz, :, cols(r)]

    def plane_block(axis, r, k):
        if axis == "x":
            return out_ref.at[k, :, :, cols(r)]
        return out_ref.at[:, k, :, cols(r)]

    def me_on(axis):
        return mz if axis == "z" else mx

    def both_sides(axis_of, view, send, recv):
        copies = []
        first = {}
        for r in range(4):
            axis, d = axis_of(r), rings[r][1]
            me = me_on(axis)
            src = view(axis, r, me)
            for side, sign in ((0, d), (1, -d)):
                cp = pltpu.make_async_remote_copy(
                    src_ref=src, dst_ref=src, send_sem=send.at[r, side], recv_sem=recv.at[r, side],
                    device_id=dev(axis, sign), device_id_type=MESH_ID,
                )
                cp.start()
                first[(r, side)] = cp
                copies.append(cp)
        later = {}
        for r in range(4):
            axis, d = axis_of(r), rings[r][1]
            n = nz if axis == "z" else nx
            first[(r, 1)].wait_recv()
            passing = view(axis, r, lax.rem(me_on(axis) + n + d, n))
            cp = pltpu.make_async_remote_copy(
                src_ref=passing, dst_ref=passing, send_sem=send.at[r, 2], recv_sem=recv.at[r, 2],
                device_id=dev(axis, -d), device_id_type=MESH_ID,
            )
            cp.start()
            later[r] = cp
            copies.append(cp)
        for r in range(4):
            first[(r, 0)].wait_recv()
            later[r].wait_recv()
        return copies

    copies1 = both_sides(lambda r: rings[r][0], block, send1, recv1)

    def second(r):
        return "x" if rings[r][0] == "z" else "z"

    copies2 = both_sides(second, plane_block, send2, recv2)
    for cp in copies1 + copies2 + dispatch:
        cp.wait_send()


ALL = ("sect", "ey", "ex", "tp")
EXPERT_AXES = ("sect", "ey")
PLANE_AXES = ("ex", "tp")


def place_slots(ids_block, experts):
    flat_ids = ids_block.reshape(-1)
    hits_mask = (flat_ids[:, None] == jnp.arange(experts, dtype=jnp.int32)[None, :]).astype(
        jnp.int32
    )
    earlier = jnp.cumsum(hits_mask, axis=0) - hits_mask
    slot_rank = jnp.sum(earlier * hits_mask, axis=1)
    return (flat_ids, slot_rank)


def per_device(tokens, router_logits, expert_ids, w_gate, w_up, w_down):
    experts_all = lax.axis_size(EXPERT_AXES)
    plane_count = lax.axis_size(PLANE_AXES)
    token_count = tokens.shape[0]
    capacity = min(token_count, 4 * token_count // experts_all)
    model_width = tokens.shape[1]
    flat_ids, slot_rank = place_slots(expert_ids, experts_all)
    columns = flat_ids * capacity + slot_rank
    positions = jnp.arange(experts_all * capacity, dtype=jnp.int32)
    source = columns.reshape(token_count, 2)
    picker = (positions[:, None, None] == source[None, :, :]).any(axis=2).astype(jnp.bfloat16)
    slab = jnp.dot(picker, tokens, preferred_element_type=jnp.float32).astype(jnp.bfloat16)
    nx = lax.axis_size("ex")
    return expert_reduce_scatter(
        columns.astype(jnp.int32),
        router_logits.reshape(-1),
        slab,
        w_gate[0],
        w_up[0],
        w_down[0],
        lax.axis_size("sect"),
        lax.axis_size("ey"),
        nx,
        plane_count // nx,
    )


def x_extent(devices):
    coords = [getattr(d, "coords", None) for d in devices.flat]
    if all(c is not None for c in coords):
        return len({c[0] for c in coords})
    return int(round(np.sqrt(devices.shape[1])))


def solution(mesh):
    devices = mesh.devices
    sect, exp, tp = devices.shape
    ex = x_extent(devices)
    fine = Mesh(devices.reshape(sect, exp // ex, ex, tp), ALL)
    in_specs = (
        P(ALL, None),
        P(ALL, None),
        P(ALL, None),
        P(EXPERT_AXES + PLANE_AXES[:1], None, "tp"),
        P(EXPERT_AXES + PLANE_AXES[:1], None, "tp"),
        P(EXPERT_AXES + PLANE_AXES[:1], "tp", None),
    )
    out_specs = P(ALL, None)
    return jax.shard_map(
        per_device, mesh=fine, in_specs=in_specs, out_specs=out_specs, check_vma=False
    )
```

```python
import functools

import jax
import jax.numpy as jnp
import numpy as np
from jax import lax
from jax.experimental import pallas as pl
from jax.experimental.pallas import tpu as pltpu
from jax.sharding import Mesh
from jax.sharding import PartitionSpec as P

MESH_ID = pl.DeviceIdType.MESH


def rs_kernel(
    nsect, ny, col_ref, logits_ref, slab_ref, wg_hbm, wu_hbm, wd_hbm, mix_ref,
    out_ref, wg, wu, wd, hid, stage, stage_f1, stage2_d, stage2_f, fin, s1, total1, s2, wsem, send1, recv1, send2, recv2, local_sem, ret_send, ret_recv,
    rows_ref, g_local, g_in_send, g_in_recv, g_send1, g_recv1, g_send2, g_recv2,
):
    nx, nz, rows, width = rows_ref.shape
    hidden_width = wd.shape[0]
    quarter = width // 4
    groups = nsect * ny
    slots = rows // groups
    c = lax.axis_index("sect")
    y = lax.axis_index("ey")
    mx = lax.axis_index("ex")
    mz = lax.axis_index("tp")

    weight_copies = [
        pltpu.make_async_copy(src, dst, wsem.at[i])
        for i, (src, dst) in enumerate(((wg_hbm, wg), (wu_hbm, wu), (wd_hbm, wd)))
    ]
    for cp in weight_copies:
        cp.start()

    def dev(axis, d):
        if axis == "z":
            return (c, y, mx, lax.rem(mz + d + nz, nz))
        return (c, y, lax.rem(mx + d + nx, nx), mz)

    me_group = c * ny + y

    def peer(o):
        g = lax.rem(me_group + o, groups)
        return (g // ny, lax.rem(g, ny), mx, mz)

    barrier = pltpu.get_barrier_semaphore()
    for axis in ("x", "z"):
        for d in (1, -1):
            pl.semaphore_signal(barrier, inc=1, device_id=dev(axis, d), device_id_type=MESH_ID)
    for o in range(1, groups):
        pl.semaphore_signal(barrier, inc=1, device_id=peer(o), device_id_type=MESH_ID)
    pl.semaphore_wait(barrier, 4 + groups - 1)

    gather_body(
        nsect, ny, slab_ref, rows_ref, g_local, g_in_send, g_in_recv, g_send1, g_recv1, g_send2, g_recv2
    )
    weight_copies[0].wait()
    weight_copies[1].wait()

    pair = 2 if nx % 2 == 0 else 1

    def hidden_group(i, carry):
        lead = pl.ds(pl.multiple_of(i * pair, pair), pair)
        block = rows_ref[lead].reshape(pair * nz * rows, width)
        gate = jnp.dot(block, wg[...], preferred_element_type=jnp.float32)
        up = jnp.dot(block, wu[...], preferred_element_type=jnp.float32)
        act = (jax.nn.silu(gate) * up).astype(hid.dtype)
        hid[lead] = act.reshape(pair, nz, rows, hidden_width)
        return carry

    lax.fori_loop(0, nx // pair, hidden_group, 0)
    weight_copies[2].wait()

    rings = [("z", 1), ("z", -1), ("x", 1), ("x", -1)]

    def me_on(axis):
        return mz if axis == "z" else mx

    def size_on(axis):
        return nz if axis == "z" else nx

    def cols(r):
        return pl.ds(r * quarter, quarter)

    def chunk(r, j):
        if rings[r][0] == "z":
            h = hid[:, j]
        else:
            h = hid[j]
        lead = h.shape[0]
        part = jnp.dot(
            h.reshape(lead * rows, hidden_width), wd[:, cols(r)], preferred_element_type=jnp.float32
        )
        return part.reshape(lead, rows, quarter)

    def other(axis):
        return "x" if axis == "z" else "z"

    class Exchange:
        def __init__(self, axis_of, own, stage_d, stage_f, recv_d, recv_f, recv_s, send, recv, finish):
            self.axis_of, self.own = axis_of, own
            self.stage_d, self.stage_f = stage_d, stage_f
            self.recv_d, self.recv_f, self.recv_s = recv_d, recv_f, recv_s
            self.send, self.recv, self.finish = send, recv, finish
            self.copies, self.pending = [], {}

        def begin(self, r):
            axis, d = self.axis_of(r), rings[r][1]
            n = size_on(axis)
            me = me_on(axis)
            self.stage_f[r] = self.own(r, lax.rem(me + 2 * n - 2 * d, n)).astype(self.stage_f.dtype)
            forward = pltpu.make_async_remote_copy(
                src_ref=self.stage_f.at[r], dst_ref=self.recv_f.at[r], send_sem=self.send.at[r, 1],
                recv_sem=self.recv.at[r, 1], device_id=dev(axis, -d), device_id_type=MESH_ID,
            )
            forward.start()
            self.stage_d[r] = self.own(r, lax.rem(me + n + d, n)).astype(self.stage_d.dtype)
            direct = pltpu.make_async_remote_copy(
                src_ref=self.stage_d.at[r], dst_ref=self.recv_d.at[r], send_sem=self.send.at[r, 0],
                recv_sem=self.recv.at[r, 0], device_id=dev(axis, d), device_id_type=MESH_ID,
            )
            direct.start()
            self.pending[r] = (direct, forward)
            self.copies += [direct, forward]

        def middle(self, r):
            axis, d = self.axis_of(r), rings[r][1]
            n = size_on(axis)
            me = me_on(axis)
            term = self.own(r, lax.rem(me + n - d, n))
            self.pending[r][1].wait_recv()
            self.recv_f[r] = (self.recv_f[r].astype(jnp.float32) + term).astype(self.recv_f.dtype)
            second = pltpu.make_async_remote_copy(
                src_ref=self.recv_f.at[r], dst_ref=self.recv_s.at[r], send_sem=self.send.at[r, 2],
                recv_sem=self.recv.at[r, 2], device_id=dev(axis, -d), device_id_type=MESH_ID,
            )
            second.start()
            self.pending[r] = (self.pending[r][0], second)
            self.copies.append(second)

        def end(self, r):
            term = self.own(r, me_on(self.axis_of(r)))
            self.pending[r][0].wait_recv()
            self.pending[r][1].wait_recv()
            self.finish(
                r, term + self.recv_d[r].astype(jnp.float32) + self.recv_s[r].astype(jnp.float32)
            )

    def keep_total1(r, value):
        total1[r] = value

    def other_axis(r):
        return other(rings[r][0])

    mine = pl.ds(pl.multiple_of(me_group * slots, slots), slots)
    returns = []
    locals_ = []

    def keep_fin(r, value):
        fin[:, cols(r)] = value
        local = pltpu.make_async_copy(fin.at[mine, cols(r)], out_ref.at[mine, cols(r)], local_sem.at[r])
        local.start()
        locals_.append(local)
        for o in range(1, groups):
            g = lax.rem(me_group + o, groups)
            cp = pltpu.make_async_remote_copy(
                src_ref=fin.at[pl.ds(pl.multiple_of(g * slots, slots), slots), cols(r)],
                dst_ref=out_ref.at[mine, cols(r)],
                send_sem=ret_send.at[o, r],
                recv_sem=ret_recv.at[o, r],
                device_id=peer(o),
                device_id_type=MESH_ID,
            )
            cp.start()
            returns.append(cp)

    first_phase = Exchange(
        lambda r: rings[r][0], chunk, stage, stage_f1, s1.at[:, 0], s1.at[:, 1], s1.at[:, 2],
        send1, recv1, keep_total1,
    )
    second_phase = Exchange(
        other_axis, lambda r, j: total1[r, j], stage2_d, stage2_f, s2.at[:, 0], s2.at[:, 1], s2.at[:, 2],
        send2, recv2, keep_fin,
    )
    for r in range(4):
        first_phase.begin(r)
    for r in range(4):
        first_phase.middle(r)
    for r in range(4):
        first_phase.end(r)
        second_phase.begin(r)
    for r in range(4):
        second_phase.middle(r)
    for r in range(4):
        second_phase.end(r)
    copies1, copies2 = first_phase.copies, second_phase.copies

    for local in locals_:
        local.wait()
    for cp in returns:
        cp.wait_recv()
    for t in range(mix_ref.shape[0]):
        gap = jnp.full((1, width), logits_ref[2 * t + 1] - logits_ref[2 * t], jnp.float32)
        first = out_ref[pl.ds(col_ref[2 * t], 1), :]
        second = out_ref[pl.ds(col_ref[2 * t + 1], 1), :]
        mix = first / (1.0 + jnp.exp(gap)) + second / (1.0 + jnp.exp(-gap))
        mix_ref[pl.ds(t, 1), :] = mix.astype(mix_ref.dtype)
    for cp in copies1 + copies2 + returns:
        cp.wait_send()


def expert_reduce_scatter(columns, logits, slab, w_gate, w_up, w_down, nsect, ny, nx, nz):
    rows, width = slab.shape
    groups = nsect * ny
    hidden_width = w_down.shape[0]
    quarter = width // 4
    return pl.pallas_call(
        functools.partial(rs_kernel, nsect, ny),
        out_shape=jax.ShapeDtypeStruct((columns.shape[0] // 2, width), jnp.bfloat16),
        in_specs=[
            pl.BlockSpec(memory_space=pltpu.SMEM),
            pl.BlockSpec(memory_space=pltpu.SMEM),
            pl.BlockSpec(memory_space=pltpu.VMEM),
            pl.BlockSpec(memory_space=pl.ANY),
            pl.BlockSpec(memory_space=pl.ANY),
            pl.BlockSpec(memory_space=pl.ANY),
        ],
        out_specs=pl.BlockSpec(memory_space=pltpu.VMEM),
        scratch_shapes=[
            pltpu.VMEM((rows, width), jnp.float32),
            pltpu.VMEM(w_gate.shape, w_gate.dtype),
            pltpu.VMEM(w_up.shape, w_up.dtype),
            pltpu.VMEM(w_down.shape, w_down.dtype),
            pltpu.VMEM((nx, nz, rows, hidden_width), jnp.bfloat16),
            pltpu.VMEM((4, nx, rows, quarter), jnp.bfloat16),
            pltpu.VMEM((4, nx, rows, quarter), jnp.bfloat16),
            pltpu.VMEM((4, rows, quarter), jnp.float32),
            pltpu.VMEM((4, rows, quarter), jnp.float32),
            pltpu.VMEM((rows, width), jnp.float32),
            pltpu.VMEM((4, 3, nx, rows, quarter), jnp.bfloat16),
            pltpu.VMEM((4, nx, rows, quarter), jnp.float32),
            pltpu.VMEM((4, 3, rows, quarter), jnp.float32),
            pltpu.SemaphoreType.DMA((3,)),
            pltpu.SemaphoreType.DMA((4, 3)),
            pltpu.SemaphoreType.DMA((4, 3)),
            pltpu.SemaphoreType.DMA((4, 3)),
            pltpu.SemaphoreType.DMA((4, 3)),
            pltpu.SemaphoreType.DMA((4,)),
            pltpu.SemaphoreType.DMA((groups, 4)),
            pltpu.SemaphoreType.DMA((groups, 4)),
            pltpu.VMEM((nx, nz, rows, width), slab.dtype),
            pltpu.SemaphoreType.DMA(()),
            pltpu.SemaphoreType.DMA((groups,)),
            pltpu.SemaphoreType.DMA((groups,)),
            pltpu.SemaphoreType.DMA((4, 3)),
            pltpu.SemaphoreType.DMA((4, 3)),
            pltpu.SemaphoreType.DMA((4, 3)),
            pltpu.SemaphoreType.DMA((4, 3)),
        ],
        compiler_params=pltpu.CompilerParams(
            collective_id=0, has_side_effects=True, vmem_limit_bytes=64 * 1024 * 1024
        ),
    )(columns, logits, slab, w_gate, w_up, w_down)


def gather_body(nsect, ny, in_ref, out_ref, local_sem, in_send, in_recv, send1, recv1, send2, recv2):
    nx, nz, rows, width = out_ref.shape
    groups = nsect * ny
    slots = rows // groups
    quarter = width // 4
    c = lax.axis_index("sect")
    y = lax.axis_index("ey")
    mx = lax.axis_index("ex")
    mz = lax.axis_index("tp")

    def dev(axis, d):
        if axis == "z":
            return (c, y, mx, lax.rem(mz + d + nz, nz))
        return (c, y, lax.rem(mx + d + nx, nx), mz)

    me_group = c * ny + y

    def peer(o):
        g = lax.rem(me_group + o, groups)
        return (g // ny, lax.rem(g, ny), mx, mz)

    mine = pl.ds(pl.multiple_of(me_group * slots, slots), slots)
    local = pltpu.make_async_copy(in_ref.at[mine], out_ref.at[mx, mz, mine], local_sem)
    local.start()
    dispatch = []
    for o in range(1, groups):
        cp = pltpu.make_async_remote_copy(
            src_ref=in_ref.at[pl.ds(pl.multiple_of(lax.rem(me_group + o, groups) * slots, slots), slots)],
            dst_ref=out_ref.at[mx, mz, mine],
            send_sem=in_send.at[o],
            recv_sem=in_recv.at[o],
            device_id=peer(o),
            device_id_type=MESH_ID,
        )
        cp.start()
        dispatch.append(cp)
    local.wait()
    for cp in dispatch:
        cp.wait_recv()

    rings = [("z", 1), ("z", -1), ("x", 1), ("x", -1)]

    def cols(r):
        return pl.ds(r * quarter, quarter)

    def block(axis, r, k):
        if axis == "z":
            return out_ref.at[mx, k, :, cols(r)]
        return out_ref.at[k, mz, :, cols(r)]

    def plane_block(axis, r, k):
        if axis == "x":
            return out_ref.at[k, :, :, cols(r)]
        return out_ref.at[:, k, :, cols(r)]

    def me_on(axis):
        return mz if axis == "z" else mx

    def both_sides(axis_of, view, send, recv):
        copies = []
        first = {}
        for r in range(4):
            axis, d = axis_of(r), rings[r][1]
            me = me_on(axis)
            src = view(axis, r, me)
            for side, sign in ((1, -d), (0, d)):
                cp = pltpu.make_async_remote_copy(
                    src_ref=src, dst_ref=src, send_sem=send.at[r, side], recv_sem=recv.at[r, side],
                    device_id=dev(axis, sign), device_id_type=MESH_ID,
                )
                cp.start()
                first[(r, side)] = cp
                copies.append(cp)
        later = {}
        for r in range(4):
            axis, d = axis_of(r), rings[r][1]
            n = nz if axis == "z" else nx
            first[(r, 1)].wait_recv()
            passing = view(axis, r, lax.rem(me_on(axis) + n + d, n))
            cp = pltpu.make_async_remote_copy(
                src_ref=passing, dst_ref=passing, send_sem=send.at[r, 2], recv_sem=recv.at[r, 2],
                device_id=dev(axis, -d), device_id_type=MESH_ID,
            )
            cp.start()
            later[r] = cp
            copies.append(cp)
        for r in range(4):
            first[(r, 0)].wait_recv()
            later[r].wait_recv()
        return copies

    copies1 = both_sides(lambda r: rings[r][0], block, send1, recv1)

    def second(r):
        return "x" if rings[r][0] == "z" else "z"

    copies2 = both_sides(second, plane_block, send2, recv2)
    for cp in copies1 + copies2 + dispatch:
        cp.wait_send()


ALL = ("sect", "ey", "ex", "tp")
EXPERT_AXES = ("sect", "ey")
PLANE_AXES = ("ex", "tp")


def place_slots(ids_block, experts):
    flat_ids = ids_block.reshape(-1)
    hits_mask = (flat_ids[:, None] == jnp.arange(experts, dtype=jnp.int32)[None, :]).astype(
        jnp.int32
    )
    earlier = jnp.cumsum(hits_mask, axis=0) - hits_mask
    slot_rank = jnp.sum(earlier * hits_mask, axis=1)
    return (flat_ids, slot_rank)


def per_device(tokens, router_logits, expert_ids, w_gate, w_up, w_down):
    experts_all = lax.axis_size(EXPERT_AXES)
    plane_count = lax.axis_size(PLANE_AXES)
    token_count = tokens.shape[0]
    capacity = min(token_count, 4 * token_count // experts_all)
    model_width = tokens.shape[1]
    flat_ids, slot_rank = place_slots(expert_ids, experts_all)
    columns = flat_ids * capacity + slot_rank
    positions = jnp.arange(experts_all * capacity, dtype=jnp.int32)
    source = columns.reshape(token_count, 2)
    picker = (positions[:, None, None] == source[None, :, :]).any(axis=2).astype(jnp.bfloat16)
    slab = jnp.dot(picker, tokens, preferred_element_type=jnp.float32).astype(jnp.bfloat16)
    nx = lax.axis_size("ex")
    return expert_reduce_scatter(
        columns.astype(jnp.int32),
        router_logits.reshape(-1),
        slab,
        w_gate[0],
        w_up[0],
        w_down[0],
        lax.axis_size("sect"),
        lax.axis_size("ey"),
        nx,
        plane_count // nx,
    )


def x_extent(devices):
    coords = [getattr(d, "coords", None) for d in devices.flat]
    if all(c is not None for c in coords):
        return len({c[0] for c in coords})
    return int(round(np.sqrt(devices.shape[1])))


def solution(mesh):
    devices = mesh.devices
    sect, exp, tp = devices.shape
    ex = x_extent(devices)
    fine = Mesh(devices.reshape(sect, exp // ex, ex, tp), ALL)
    in_specs = (
        P(ALL, None),
        P(ALL, None),
        P(ALL, None),
        P(EXPERT_AXES + PLANE_AXES[:1], None, "tp"),
        P(EXPERT_AXES + PLANE_AXES[:1], None, "tp"),
        P(EXPERT_AXES + PLANE_AXES[:1], "tp", None),
    )
    out_specs = P(ALL, None)
    return jax.shard_map(
        per_device, mesh=fine, in_specs=in_specs, out_specs=out_specs, check_vma=False
    )
```
